32 devices in a mesh: groups: 2 (over x), tm: 8 (over z, y), mp: 2 (over core).
Axes of the slice: x: 2, y: 2, z: 4, core: 2. Of those that a mesh axis runs over, the one named last changes fastest.
Arguments:
- branch_x: bfloat16 [8192, 4096], P(('groups', 'tm'), 'mp'), parts along dimension 0, may hold values from -6 to 6
- branch_y: bfloat16 [8192, 4096], P(('groups', 'tm'), 'mp'), parts along dimension 0, may hold values from -6 to 6
- queries: bfloat16 [8192, 4096], P(('groups', 'tm'), 'mp'), parts along dimension 0, may hold values from -1500 to 1500
- conv_weight: float32 [4, 4096], P(None, 'mp'), may hold values from -3 to 3
- conv_bias: float32 [4096], P('mp'), may hold values from -3 to 3
- gate_panel: bfloat16 [16, 256, 512], P('mp'), may hold values from -0.375 to 0.375
- gate_scale: float32 [16, 2, 512], P('mp'), may hold values from 0.5 to 2
- gate_bias: float32 [2, 4096], P(None, 'mp'), may hold values from -4 to 4
- decay_rate: float32 [4096], P('mp'), may hold values from 2.4414063e-05 to 0.05
- kv_panel: bfloat16 [4096, 512], P('mp'), may hold values from -0.09375 to 0.09375
- kv_scale: float32 [32, 512], P('mp'), may hold values from 0.5 to 2
- segment_ids: int32 [8192], P('groups'), parts along dimension 0, may hold values from 0 to 3, never falling along the last dimension, each value on 1 to 2048 neighbouring positions
Outputs:
- mixed: bfloat16 [8192, 4096], P(('groups', 'tm'), 'mp'), parts along dimension 0
- attended: bfloat16 [8192, 4096], P(('groups', 'tm'), 'mp'), parts along dimension 0
The draws below stay inside these ranges and needn't reach their ends.
There are 2 independent parts, one for each index of `groups`. The reference program is written for one: setup_inputs(seed, part) draws one part's arguments, and reference() takes and returns one part's arrays. A program takes and returns all parts, laid end to end along the dimension named above; an argument that names none is the same for every part. Nothing has to cross between parts.
Inputs may be any that keep to these rules, and one draw needn't show every extreme that they name: `segment_ids`: never falls along the sequence; each of the 4 documents holds 1 to 2048 positions, one of them exactly 2048.
All inputs are finite; a program needn't handle non-finite values.
Results may differ from the reference program's by a relative error of at most 0.03.
Values may be sent and summed in bfloat16 or wider, within the bound.
No kernel may reach another device: no remote copies, remote signals or barrier semaphores. Data moves between devices by JAX's collectives and lax.ppermute only.
A program may use at most 128 MiB of HBM per device.

```python
import math
import jax
import jax.numpy as jnp
import numpy as np
from jax import lax

D = 4096
HEADS = 16
HD = 256
BLOCKS = 16
CONV = 4
WINDOW = 2048
SCALE_ROWS = 128
DOCS = 4
TOK_DEV = 512
SEQ = 4096
BW = 256


def draw_queries(key, part):
    normal_part = jnp.clip(jax.random.normal(key, (SEQ, HEADS * HD), jnp.float32), -6.0, 6.0)
    return normal_part.astype(jnp.bfloat16)


def draw_decay_rate(key, part):
    uniform_part = jax.random.uniform(key, (D,), jnp.float32)
    lowest = jnp.log(0.25 / SEQ)
    return jnp.exp(lowest + uniform_part * (jnp.log(0.05) - lowest))


def block_scale(key, shape, shards, least, largest):
    level, own = 1.0, jax.random.fold_in(key, 6)
    for axis_at, shards_of in shards:
        heights = jnp.exp(jax.random.uniform(jax.random.fold_in(own, axis_at), (shards_of,), jnp.float32, least / len(shards), largest / len(shards)))
        level = level * jnp.repeat(heights, shape[axis_at] // shards_of).reshape([-1 if axis == axis_at else 1 for axis in range(len(shape))])
    return level


def split_up(number_of, total, limit, lean):
    weights = [(1 << 20) // math.isqrt(rank ** lean) + 1 for rank in range(2, number_of + 1)]
    rest, given = total - limit - (number_of - 1), [1] * (number_of - 1)
    while rest > 0:
        movable = [i for i in range(number_of - 1) if given[i] < limit]
        mass, remaining = sum([weights[i] for i in movable]), rest
        for i in movable:
            more = min(limit - given[i], max(1, remaining * weights[i] // mass), rest)
            given[i] = given[i] + more
            rest = rest - more
    return np.array([limit] + given)


def ragged(stream_key, number_of, total, limit, lean):
    if number_of == 2:
        one = jax.random.randint(stream_key, (), max(1, total - limit), min(limit, total - 1) + 1)
        return jnp.stack([one, total - one])
    sizes = jnp.asarray(split_up(number_of, total, limit, lean), jnp.int32)
    twos = (number_of - 1) // 2
    donor, receiver = sizes[1:1 + 2 * twos:2], sizes[2:2 + 2 * twos:2]
    margin = jnp.minimum(donor - 1, limit - receiver)
    passed = jax.random.randint(jax.random.fold_in(stream_key, 1), (twos,), 0, 1 << 20) % (margin + 1)
    sizes = sizes.at[1:1 + 2 * twos:2].set(donor - passed).at[2:2 + 2 * twos:2].set(receiver + passed)
    return sizes[jax.random.permutation(jax.random.fold_in(stream_key, 2), number_of)]


def gaussian(stream_key, dims, scale, limit, cuts=(), kind=jnp.bfloat16):
    values = jax.random.normal(stream_key, dims, jnp.float32) * scale
    if len(cuts) > 0:
        values = block_scale(stream_key, dims, cuts, -0.22, 0.18) * values
    return jnp.clip(values, min=-limit, max=limit).astype(kind)


def setup_inputs(seed: int = 0, part: int = 0) -> dict:
    key_of = jax.random.split(jax.random.key(seed), 13)
    own_keys = jax.random.split(jax.random.fold_in(key_of[12], part), 13)
    branch_x = gaussian(own_keys[0], (SEQ, D), 1.0, 6.0, ((0, 8), (1, 2)))
    branch_y = gaussian(own_keys[1], (SEQ, D), 1.0, 6.0, ((0, 8), (1, 2)))
    queries = draw_queries(jax.random.fold_in(jax.random.fold_in(key_of[12], part), 71), part)
    conv_weight = gaussian(key_of[3], (CONV, D), 0.5, 3.0, ((1, 2),), jnp.float32)
    conv_bias = gaussian(key_of[4], (D,), 0.5, 3.0, ((0, 2),), jnp.float32)
    gate_panel = gaussian(key_of[5], (BLOCKS, BW, 2 * BW), BW ** -0.5, 0.375, ((0, 2),))
    gate_scale = jnp.clip(jnp.exp(math.log(2.0) - 1.3862944 * jax.random.uniform(key_of[6], (BLOCKS, BW // SCALE_ROWS, 2 * BW), jnp.float32) ** block_scale(key_of[6], (BLOCKS, BW // SCALE_ROWS, 2 * BW), ((0, 2),), -0.2, 0.2)), 0.5, 2.0)
    gate_bias = gaussian(key_of[7], (2, D), 1.0, 4.0, ((1, 2),), jnp.float32)
    decay_rate = draw_decay_rate(jax.random.fold_in(key_of[12], 71), part)
    kv_panel = gaussian(key_of[9], (D, 2 * HD), D ** -0.5, 0.09375, ((0, 2),))
    kv_scale = jnp.clip(jnp.exp(math.log(2.0) - 1.3862944 * jax.random.uniform(key_of[10], (D // SCALE_ROWS, 2 * HD), jnp.float32) ** block_scale(key_of[10], (D // SCALE_ROWS, 2 * HD), ((0, 2),), -0.2, 0.2)), 0.5, 2.0)
    segment_ids = jnp.searchsorted(jnp.cumsum(ragged(own_keys[11], DOCS, SEQ, SEQ // 2, 2)), jnp.arange(SEQ), side="right").astype(jnp.int32)
    return dict(branch_x=branch_x, branch_y=branch_y, queries=queries, conv_weight=conv_weight, conv_bias=conv_bias, gate_panel=gate_panel, gate_scale=gate_scale, gate_bias=gate_bias, decay_rate=decay_rate, kv_panel=kv_panel, kv_scale=kv_scale, segment_ids=segment_ids)


def dequantize(weight_panel, scales):
    row_count = weight_panel.shape[-2]
    shaped = weight_panel.astype(jnp.float32).reshape(weight_panel.shape[:-2] + (row_count // SCALE_ROWS, SCALE_ROWS, weight_panel.shape[-1]))
    return (shaped * jnp.expand_dims(scales, -2)).reshape(weight_panel.shape).astype(jnp.bfloat16)

def recur_step(state, inputs):
    nxt = inputs[0] * state + inputs[1]
    return (nxt, nxt)

def reference(branch_x, branch_y, queries, conv_weight, conv_bias, gate_panel, gate_scale, gate_bias, decay_rate, kv_panel, kv_scale, segment_ids):
    length = branch_x.shape[0]
    padded_ids = jnp.concatenate([-jnp.ones((WINDOW,), jnp.int32), segment_ids.astype(jnp.int32)])
    own_ids = segment_ids.astype(jnp.int32)
    resets = padded_ids[WINDOW:] != padded_ids[WINDOW - 1:WINDOW - 1 + length]
    padded_x = jnp.concatenate([jnp.zeros((CONV - 1, D), jnp.bfloat16), branch_x], 0)
    conv_sum = jnp.zeros((length, D), jnp.float32)
    for lag_index in range(CONV):
        same_doc = (padded_ids[WINDOW - lag_index:WINDOW - lag_index + length] == own_ids).astype(jnp.float32)
        offset = CONV - 1 - lag_index
        conv_sum = conv_sum + conv_weight[lag_index] * padded_x[offset:offset + length].astype(jnp.float32) * same_doc[:, None]
    conv_out = (conv_sum + conv_bias).astype(jnp.bfloat16)
    gate_weight = dequantize(gate_panel, gate_scale)
    gate_pre = jnp.einsum('tbi,bio->tbo', conv_out.reshape(length, BLOCKS, BW).astype(jnp.float32), gate_weight.astype(jnp.float32), precision=lax.Precision.HIGHEST)
    recur_gate = jax.nn.sigmoid(gate_pre[..., :BW].reshape(length, D) + gate_bias[0])
    input_gate = jax.nn.sigmoid(gate_pre[..., BW:].reshape(length, D) + gate_bias[1])
    log_decay = -8.0 * recur_gate * decay_rate
    decay = jnp.where(resets[:, None], jnp.float32(0.0), jnp.exp(log_decay))
    normalizer = jnp.where(resets[:, None], jnp.float32(1.0), jnp.sqrt(-jnp.expm1(2.0 * log_decay)))
    scaled_input = input_gate * conv_out.astype(jnp.float32) * normalizer
    final_state, state = lax.scan(recur_step, jnp.zeros((D,), jnp.float32), (decay, scaled_input))
    mixed = (state * jax.nn.gelu(branch_y.astype(jnp.float32), approximate=True)).astype(jnp.bfloat16)
    keys_values = jnp.dot(mixed, dequantize(kv_panel, kv_scale), preferred_element_type=jnp.float32).astype(jnp.bfloat16)
    padded_keys = jnp.concatenate([jnp.zeros((WINDOW, HD), jnp.bfloat16), keys_values[:, :HD]], 0)
    padded_values = jnp.concatenate([jnp.zeros((WINDOW, HD), jnp.bfloat16), keys_values[:, HD:]], 0)
    query_heads = queries.reshape(length, HEADS, HD)

    def one_block(block_index):
        first_row = block_index * TOK_DEV
        query_block = lax.dynamic_slice_in_dim(query_heads, first_row, TOK_DEV, 0)
        key_block = lax.dynamic_slice_in_dim(padded_keys, first_row, WINDOW + TOK_DEV, 0)
        value_block = lax.dynamic_slice_in_dim(padded_values, first_row, WINDOW + TOK_DEV, 0)
        key_ids = lax.dynamic_slice_in_dim(padded_ids, first_row, WINDOW + TOK_DEV)
        query_ids = lax.dynamic_slice_in_dim(own_ids, first_row, TOK_DEV)
        query_pos = first_row + jnp.arange(TOK_DEV, dtype=jnp.int32)
        key_pos = first_row - WINDOW + jnp.arange(WINDOW + TOK_DEV, dtype=jnp.int32)
        allowed = (key_pos[None, :] <= query_pos[:, None]) & (query_pos[:, None] - key_pos[None, :] < WINDOW) & (key_ids[None, :] == query_ids[:, None])
        scores = jnp.einsum('thd,sd->hts', query_block.astype(jnp.float32), key_block.astype(jnp.float32), precision=lax.Precision.HIGHEST) * HD ** (-0.5)
        scores = jnp.where(allowed[None], scores, jnp.float32(-1e+30))
        highest = lax.optimization_barrier(jnp.max(scores, axis=-1, keepdims=True))
        weights_raw = jnp.exp(scores - highest) * allowed[None].astype(jnp.float32)
        totals = lax.optimization_barrier(jnp.sum(weights_raw, axis=-1, keepdims=True))
        weights = (weights_raw / totals).astype(jnp.bfloat16)
        result = jnp.einsum('hts,sd->thd', weights.astype(jnp.float32), value_block.astype(jnp.float32), precision=lax.Precision.HIGHEST)
        return result.astype(jnp.bfloat16).reshape(TOK_DEV, HEADS * HD)
    blocks_out = lax.map(one_block, jnp.arange(length // TOK_DEV, dtype=jnp.int32))
    attended = blocks_out.reshape(length, HEADS * HD)
    return (mixed, attended)
```

```python
import functools

import jax
import jax.numpy as jnp
from jax import lax
from jax.experimental import pallas as pl
from jax.experimental.pallas import tpu as pltpu
from jax.sharding import PartitionSpec as P

HD = 256
CONV = 4
WINDOW = 2048
SCALE_ROWS = 128
DOCS = 4
SEGS = 8
PAD = 8
LOG2E = 1.4426950408889634
LN2 = 0.6931471805599453
F32 = jnp.float32
BF16 = jnp.bfloat16


def ring(x, lag):
    n = lax.axis_size("tm")
    return lax.ppermute(x, "tm", [(i, (i + lag) % n) for i in range(n)])


def swap(x):
    n = lax.axis_size("tm")
    return lax.ppermute(x, "tm", [(i, i ^ 1) for i in range(n)])


def partner(x):
    return lax.ppermute(x, "mp", [(0, 1), (1, 0)])


def dequantized(panel, scale):
    rows = panel.shape[0]
    parts = []
    for g in range(rows // SCALE_ROWS):
        part = panel[g * SCALE_ROWS : (g + 1) * SCALE_ROWS, :].astype(F32)
        parts.append((part * scale[g : g + 1, :]).astype(BF16))
    return jnp.concatenate(parts, 0)


def recur_kernel(
    starts_ref,
    x_ref,
    halo_ref,
    cw_ref,
    cb_ref,
    panel_ref,
    scale_ref,
    gb_ref,
    rate_ref,
    h_ref,
    p_ref,
    ends_ref,
    tot_ref,
    keep,
    xs,
    co,
    gate,
):
    rows, width = x_ref.shape
    seg_len = rows // SEGS
    base = lax.axis_index("tm") * rows

    @pl.when(pl.program_id(0) == 0)
    def _():
        def fill(i, carry):
            pos = base + i - 2 + seg_len * lax.broadcasted_iota(jnp.int32, (SEGS, 128), 0)
            hit = pos == starts_ref[0]
            for d in range(1, DOCS):
                hit = hit | (pos == starts_ref[d])
            keep[pl.ds(pl.multiple_of(i * SEGS, SEGS), SEGS), :] = jnp.where(hit, 0.0, 1.0)
            return carry

        lax.fori_loop(0, seg_len + 2, fill, 0)

    for c in range(width // 128):
        lanes = slice(c * 128, (c + 1) * 128)
        xs[c, PAD:, :] = x_ref[:, lanes].astype(F32)
        xs[c, PAD - CONV + 1 : PAD, :] = halo_ref[:, lanes].astype(F32)

    def mask(i):
        m = keep[pl.ds(pl.multiple_of((i + 2) * SEGS, SEGS), SEGS), :]
        return jnp.concatenate([m] * (width // 128), 1)

    def row(i):
        return jnp.concatenate(
            [xs[c, pl.ds(PAD + i, SEGS, stride=seg_len), :] for c in range(width // 128)], 1
        )

    w = [jnp.broadcast_to(cw_ref[j : j + 1, :], (SEGS, width)) for j in range(CONV)]
    bias = jnp.broadcast_to(cb_ref[...], (SEGS, width))

    def conv_step(i, carry):
        a, b, c = carry
        x = row(i)
        m = mask(i)
        d = w[0] * x + m * c + bias
        c = w[1] * x + m * b
        b = w[2] * x + m * a
        a = w[3] * x
        return (a, b, c), d

    x3, x2, x1 = row(-3), row(-2), row(-1)
    a1 = w[3] * x1
    b1 = w[2] * x1 + mask(-1) * (w[3] * x2)
    c1 = w[1] * x1 + mask(-1) * (w[2] * x2 + mask(-2) * (w[3] * x3))

    def conv_pair(k, carry):
        carry, d0 = conv_step(2 * k, carry)
        carry, d1 = conv_step(2 * k + 1, carry)
        co[pl.ds(pl.multiple_of(k * 2 * SEGS, 2 * SEGS), 2 * SEGS), :] = jnp.concatenate([d0, d1], 0).astype(BF16)
        return carry

    lax.fori_loop(0, seg_len // 2, conv_pair, (a1, b1, c1), unroll=4)

    weight = dequantized(panel_ref[0], scale_ref[0]) * BF16(0.5)
    gate[...] = jnp.dot(co[...], weight, preferred_element_type=F32)

    bias_r = jnp.broadcast_to(gb_ref[0:1, :] * 0.5, (SEGS, width))
    bias_i = jnp.broadcast_to(gb_ref[1:2, :] * 0.5, (SEGS, width))
    rate4 = jnp.broadcast_to(rate_ref[...] * 4.0, (SEGS, width))

    def scan_step(i, conv, carry):
        h, p = carry
        at = pl.ds(pl.multiple_of(i * SEGS, SEGS), SEGS)
        m = mask(i)
        v = rate4 * (1.0 + jnp.tanh(gate[at, :width] + bias_r))
        ti = 1.0 + jnp.tanh(gate[at, width:] + bias_i)
        decay = jnp.exp2(v * (-LOG2E))
        s = v * v
        series = ((s * (0.5 / 5040.0) + (0.5 / 120.0)) * s + (0.5 / 6.0)) * s + 0.5
        quarter = decay * (v * series)
        half = quarter * lax.rsqrt(jnp.maximum(quarter, 1e-37))
        half = jnp.where(m > 0.0, half, 0.5)
        decay = decay * m
        h = decay * h + ti * (conv * half)
        p = p * decay
        h_ref[at, :] = h
        p_ref[at, :] = p
        return h, p

    def scan_pair(k, carry):
        conv = co[pl.ds(pl.multiple_of(k * 2 * SEGS, 2 * SEGS), 2 * SEGS), :].astype(F32)
        carry = scan_step(2 * k, conv[:SEGS], carry)
        return scan_step(2 * k + 1, conv[SEGS:], carry)

    h, p = lax.fori_loop(
        0,
        seg_len // 2,
        scan_pair,
        (jnp.zeros((SEGS, width), F32), jnp.ones((SEGS, width), F32)),
        unroll=4,
    )
    ends_ref[0] = p
    ends_ref[1] = h
    tp, th = p[0:1], h[0:1]
    for s in range(1, SEGS):
        th = p[s : s + 1] * th + h[s : s + 1]
        tp = tp * p[s : s + 1]
    tot_ref[0:1, :] = tp
    tot_ref[1:2, :] = th


def mix_kernel(h_ref, p_ref, ends_ref, in_ref, y_ref, panel_ref, scale_ref, mixed_ref, kv_ref, carry, state):
    rows, width = y_ref.shape
    seg_len = rows // SEGS
    c = in_ref[...]
    carry[0:1, :] = c
    for s in range(SEGS - 1):
        c = ends_ref[0, s : s + 1, :] * c + ends_ref[1, s : s + 1, :]
        carry[s + 1 : s + 2, :] = c
    enter = carry[...]

    def fix(i, z):
        at = pl.ds(pl.multiple_of(i * SEGS, SEGS), SEGS)
        st = h_ref[at, :] + p_ref[at, :] * enter
        for g in range(width // 128):
            state[g, pl.ds(i, SEGS, stride=seg_len), :] = st[:, g * 128 : (g + 1) * 128]
        return z

    lax.fori_loop(0, seg_len, fix, 0, unroll=8)
    y = y_ref[...].astype(F32)
    inner = y * (0.7978845608028654 + (0.7978845608028654 * 0.044715) * (y * y))
    gelu = (0.5 * y) * (1.0 + jnp.tanh(inner))
    mixed = (jnp.concatenate([state[g] for g in range(width // 128)], 1) * gelu).astype(BF16)
    mixed_ref[...] = mixed
    part = jnp.dot(mixed, dequantized(panel_ref[...], scale_ref[0]), preferred_element_type=F32)

    @pl.when(pl.program_id(0) == 0)
    def _():
        kv_ref[...] = part

    @pl.when(pl.program_id(0) > 0)
    def _():
        kv_ref[...] += part


def sum_kernel(a_ref, b_ref, full_ref, half_ref):
    rows = half_ref.shape[0]
    full_ref[...] = (a_ref[...] + b_ref[...]).astype(BF16)
    at = pl.ds(pl.multiple_of(lax.axis_index("mp") * rows, rows), rows)
    half_ref[...] = (a_ref[at, :] + b_ref[at, :]).astype(BF16)


def attend_kernel(lags, starts_ref, q_ref, own_ref, *refs):
    n_half = len(lags)
    halves, (o_ref, low, qs, m_ref, l_ref, acc) = refs[:n_half], refs[n_half:]
    rows = q_ref.shape[0]
    me = lax.axis_index("tm")
    first = me * rows
    core = lax.axis_index("mp")
    turn = 2 * (me % 2) - 1
    scale = LOG2E / 16.0

    def lowest(t):
        d0 = jnp.maximum(t - (WINDOW - 1), 0)
        for d in range(DOCS):
            d0 = jnp.maximum(d0, jnp.where(starts_ref[d] <= t, starts_ref[d], 0))
        return d0

    @pl.when(pl.program_id(0) == 0)
    def _():
        low[...] = lowest(first + lax.broadcasted_iota(jnp.int32, (rows, 128), 0))

    q = q_ref[...]
    lo_first = lowest(first)

    def scores(keys):
        return lax.dot_general(q, keys, (((1,), (1,)), ((), ())), preferred_element_type=F32)

    def wide(col, n):
        return jnp.concatenate([col] * (n // 128), 1)

    n = rows
    s = scores(own_ref[:, :HD])
    kpos = first + lax.broadcasted_iota(jnp.int32, (rows, n), 1)
    qpos = first + lax.broadcasted_iota(jnp.int32, (rows, n), 0)
    s = jnp.where((kpos <= qpos) & (kpos >= wide(low[...], n)), s * scale, -1e30)
    m = jnp.max(s, axis=1, keepdims=True)
    p = jnp.exp2(s - m)
    l_ref[...] = jnp.broadcast_to(jnp.sum(p, axis=1, keepdims=True), (rows, 128))
    m_ref[...] = jnp.broadcast_to(m, (rows, 128))
    acc[...] = jnp.dot(p.astype(BF16), own_ref[:, HD:], preferred_element_type=F32)

    for k in range(n_half):
        lag = lags[k][0] + lags[k][1] * turn
        side = core if k % 2 == 0 else 1 - core
        n = halves[k].shape[0]
        start = first - lag * rows + side * n

        @pl.when((start >= 0) & (start < first) & (start + n > lo_first))
        def _(k=k, n=n, start=start):
            s = scores(halves[k][:, :HD]) * scale
            kpos = start + lax.broadcasted_iota(jnp.int32, (rows, n), 1)
            s = jnp.where(kpos >= wide(low[...], n), s, -1e30)
            m0 = m_ref[...]
            m1 = jnp.maximum(m0, jnp.max(s, axis=1, keepdims=True))
            fade = jnp.exp2(m0 - m1)
            p = jnp.exp2(s - wide(m1, n))
            l_ref[...] = l_ref[...] * fade + jnp.sum(p, axis=1, keepdims=True)
            m_ref[...] = m1
            acc[...] = acc[...] * wide(fade, HD) + jnp.dot(
                p.astype(BF16), halves[k][:, HD:], preferred_element_type=F32
            )

    o_ref[...] = (acc[...] / wide(l_ref[...], HD)).astype(BF16)


def recur_call(starts, x, halo, conv_weight, conv_bias, gate_panel, gate_scale, gate_bias, decay_rate):
    rows, channels = x.shape
    blocks, width, _ = gate_panel.shape
    col = lambda b, s: (0, b)
    return pl.pallas_call(
        recur_kernel,
        grid_spec=pltpu.PrefetchScalarGridSpec(
            num_scalar_prefetch=1,
            grid=(blocks,),
            in_specs=[
                pl.BlockSpec((rows, width), col),
                pl.BlockSpec((CONV - 1, width), col),
                pl.BlockSpec((CONV, width), col),
                pl.BlockSpec((1, width), col),
                pl.BlockSpec((1, width, 2 * width), lambda b, s: (b, 0, 0)),
                pl.BlockSpec((1, width // SCALE_ROWS, 2 * width), lambda b, s: (b, 0, 0)),
                pl.BlockSpec((2, width), col),
                pl.BlockSpec((1, width), col),
            ],
            out_specs=[
                pl.BlockSpec((rows, width), col),
                pl.BlockSpec((rows, width), col),
                pl.BlockSpec((2, SEGS, width), lambda b, s: (0, 0, b)),
                pl.BlockSpec((2, width), col),
            ],
            scratch_shapes=[
                pltpu.VMEM((rows + 2 * SEGS, 128), F32),
                pltpu.VMEM((width // 128, PAD + rows, 128), F32),
                pltpu.VMEM((rows, width), BF16),
                pltpu.VMEM((rows, 2 * width), F32),
            ],
        ),
        out_shape=[
            jax.ShapeDtypeStruct((rows, channels), F32),
            jax.ShapeDtypeStruct((rows, channels), F32),
            jax.ShapeDtypeStruct((2, SEGS, channels), F32),
            jax.ShapeDtypeStruct((2, channels), F32),
        ],
        compiler_params=pltpu.CompilerParams(vmem_limit_bytes=32 << 20),
        name="recur",
    )(starts, x, halo, conv_weight, conv_bias, gate_panel, gate_scale, gate_bias, decay_rate)


def mix_call(h, p, ends, incoming, y, kv_panel, kv_scale):
    rows, channels = y.shape
    width = 2 * SCALE_ROWS
    col = lambda b: (0, b)
    out = kv_panel.shape[1]
    return pl.pallas_call(
        mix_kernel,
        grid=(channels // width,),
        in_specs=[
            pl.BlockSpec((rows, width), col),
            pl.BlockSpec((rows, width), col),
            pl.BlockSpec((2, SEGS, width), lambda b: (0, 0, b)),
            pl.BlockSpec((1, width), col),
            pl.BlockSpec((rows, width), col),
            pl.BlockSpec((width, out), lambda b: (b, 0)),
            pl.BlockSpec((1, 2, out), lambda b: (b, 0, 0)),
        ],
        out_specs=[pl.BlockSpec((rows, width), col), pl.BlockSpec((rows, out), lambda b: (0, 0))],
        out_shape=[jax.ShapeDtypeStruct((rows, channels), BF16), jax.ShapeDtypeStruct((rows, out), F32)],
        scratch_shapes=[pltpu.VMEM((SEGS, width), F32), pltpu.VMEM((width // 128, rows, 128), F32)],
        compiler_params=pltpu.CompilerParams(vmem_limit_bytes=32 << 20),
        name="mix",
    )(h, p, ends, incoming, y, kv_panel, kv_scale.reshape(-1, 2, out))


def sum_call(a, b):
    rows, out = a.shape
    return pl.pallas_call(
        sum_kernel,
        out_shape=[jax.ShapeDtypeStruct((rows, out), BF16), jax.ShapeDtypeStruct((rows // 2, out), BF16)],
        compiler_params=pltpu.CompilerParams(vmem_limit_bytes=16 << 20),
        name="kvsum",
    )(a, b)


def attend_call(starts, q, own, halves, lags):
    rows, width = q.shape
    heads = width // HD
    whole = lambda a: pl.BlockSpec(a.shape, lambda h, s: (0, 0))
    return pl.pallas_call(
        functools.partial(attend_kernel, lags),
        grid_spec=pltpu.PrefetchScalarGridSpec(
            num_scalar_prefetch=1,
            grid=(heads,),
            in_specs=[pl.BlockSpec((rows, HD), lambda h, s: (0, h)), whole(own)] + [whole(a) for a in halves],
            out_specs=pl.BlockSpec((rows, HD), lambda h, s: (0, h)),
            scratch_shapes=[
                pltpu.VMEM((rows, 128), jnp.int32),
                pltpu.VMEM((rows, HD), BF16),
                pltpu.VMEM((rows, 128), F32),
                pltpu.VMEM((rows, 128), F32),
                pltpu.VMEM((rows, HD), F32),
            ],
        ),
        out_shape=jax.ShapeDtypeStruct((rows, width), BF16),
        compiler_params=pltpu.CompilerParams(vmem_limit_bytes=32 << 20),
        name="attend",
    )(starts, q, own, *halves)


def local(
    branch_x,
    branch_y,
    queries,
    conv_weight,
    conv_bias,
    gate_panel,
    gate_scale,
    gate_bias,
    decay_rate,
    kv_panel,
    kv_scale,
    segment_ids,
):
    rows = branch_x.shape[0]
    seq = segment_ids.shape[0]
    me = lax.axis_index("tm")
    halo = ring(branch_x[rows - CONV + 1 :], 1)
    starts = jnp.sum(
        (segment_ids[None, :] < jnp.arange(DOCS, dtype=jnp.int32)[:, None]).astype(jnp.int32), axis=1
    )
    h, p, ends, tot = recur_call(
        starts,
        branch_x,
        halo,
        conv_weight,
        conv_bias[None],
        gate_panel,
        gate_scale,
        gate_bias,
        decay_rate[None],
    )
    odd = (me % 2) == 1
    near = swap(tot)
    lower = jnp.where(odd, near, tot)
    upper = jnp.where(odd, tot, near)
    level = jnp.stack([lower[0] * upper[0], upper[0] * lower[1] + upper[1]])
    levels = -(-(seq // 2) // (2 * rows))
    past = [ring(level, 2 * k) for k in range(1, levels + 1)]
    incoming = jnp.zeros_like(tot[1])
    for k in range(levels, 0, -1):
        got = past[k - 1]
        incoming = jnp.where(me >= 2 * k, got[0] * incoming + got[1], 0.0)
    incoming = jnp.where(odd, near[0] * incoming + near[1], incoming)
    mixed, partial_kv = mix_call(h, p, ends, incoming[None], branch_y, kv_panel, kv_scale)
    own, half = sum_call(partial_kv, partner(partial_kv))

    window_blocks = WINDOW // rows
    pair_levels = window_blocks // 2
    straight = [half]
    for k in range(pair_levels):
        straight.append(ring(straight[-1], 2))
    crossed = [swap(a) for a in straight]
    tiles = [(a, 2 * k, 0) for k, a in enumerate(straight) if k > 0]
    tiles += [(a, 2 * k, 1) for k, a in enumerate(crossed)]
    halves, lags = [], []
    for a, even_part, odd_part in tiles:
        halves += [a, partner(a)]
        lags += [(even_part, odd_part)] * 2
    attended = attend_call(starts, queries, own, halves, lags)
    return mixed, attended


def solution(mesh):
    in_specs = (
        P(("groups", "tm"), "mp"),
        P(("groups", "tm"), "mp"),
        P(("groups", "tm"), "mp"),
        P(None, "mp"),
        P("mp"),
        P("mp", None, None),
        P("mp", None, None),
        P(None, "mp"),
        P("mp"),
        P("mp", None),
        P("mp", None),
        P("groups"),
    )
    out_specs = (P(("groups", "tm"), "mp"), P(("groups", "tm"), "mp"))
    return jax.shard_map(local, mesh=mesh, in_specs=in_specs, out_specs=out_specs, check_vma=False)
```

```python
import functools
import math

import jax
import jax.numpy as jnp
from jax import lax
from jax.experimental import pallas as pl
from jax.experimental.pallas import tpu as pltpu
from jax.sharding import PartitionSpec as P

HD = 256
CONV = 4
WINDOW = 2048
SCALE_ROWS = 128
DOCS = 4
SEGS = 8
MIX_GROUPS = 4
HIST = 4
LOG2E = 1.4426950408889634
LN2 = 0.6931471805599453
SINH = [-0.5 * LN2 ** (2 * k + 1) / math.factorial(2 * k + 1) for k in range(4)]
F32 = jnp.float32
BF16 = jnp.bfloat16


def ring(x, lag):
    n = lax.axis_size("tm")
    return lax.ppermute(x, "tm", [(i, (i + lag) % n) for i in range(n)])


def swap(x):
    n = lax.axis_size("tm")
    return lax.ppermute(x, "tm", [(i, i ^ 1) for i in range(n)])


def partner(x):
    return lax.ppermute(x, "mp", [(0, 1), (1, 0)])


def dequantized(panel, scale):
    rows = panel.shape[0]
    parts = []
    for g in range(rows // SCALE_ROWS):
        part = panel[g * SCALE_ROWS : (g + 1) * SCALE_ROWS, :].astype(F32)
        parts.append((part * scale[g : g + 1, :]).astype(BF16))
    return jnp.concatenate(parts, 0)


def recur_kernel(
    starts_ref,
    x_ref,
    halo_ref,
    cw_ref,
    cb_ref,
    panel_ref,
    scale_ref,
    gb_ref,
    rate_ref,
    h_ref,
    p_ref,
    ends_ref,
    tot_ref,
    keep,
    xs,
    co,
    gate,
):
    rows, width = x_ref.shape
    seg_len = rows // SEGS
    base = lax.axis_index("tm") * rows

    @pl.when(pl.program_id(0) == 0)
    def _():
        def fill(i, carry):
            pos = base + i - 2 + seg_len * lax.broadcasted_iota(jnp.int32, (SEGS, 128), 0)
            hit = pos == starts_ref[0]
            for d in range(1, DOCS):
                hit = hit | (pos == starts_ref[d])
            keep[pl.ds(pl.multiple_of(i * SEGS, SEGS), SEGS), :] = jnp.where(hit, 0.0, 1.0)
            return carry

        lax.fori_loop(0, seg_len + 2, fill, 0)

    pitch = seg_len + HIST
    for c in range(width // 128):
        lanes = slice(c * 128, (c + 1) * 128)
        xs[c, HIST + 1 : 2 * HIST, :] = halo_ref[:, lanes].astype(F32)
        for s in range(1, SEGS):
            past = x_ref[s * seg_len - 2 * HIST : s * seg_len, lanes].astype(F32)
            xs[c, s * pitch : s * pitch + 2 * HIST, :] = past
        for s in range(SEGS):
            rest = x_ref[s * seg_len : (s + 1) * seg_len, lanes].astype(F32)
            xs[c, s * pitch + 2 * HIST : (s + 1) * pitch + HIST, :] = rest

    def mask(i):
        m = keep[pl.ds(pl.multiple_of((i + 2) * SEGS, SEGS), SEGS), :]
        return jnp.concatenate([m] * (width // 128), 1)

    def row(i):
        return jnp.concatenate(
            [xs[c, pl.ds(2 * HIST + i, SEGS, stride=pitch), :] for c in range(width // 128)], 1
        )

    w = [jnp.broadcast_to(cw_ref[j : j + 1, :], (SEGS, width)) for j in range(CONV)]
    bias = jnp.broadcast_to(cb_ref[...], (SEGS, width))

    def conv_step(i, carry):
        a, b, c = carry
        x = row(i)
        m = mask(i)
        d = w[0] * x + m * c + bias
        c = w[1] * x + m * b
        b = w[2] * x + m * a
        a = w[3] * x
        return (a, b, c), d

    x3, x2, x1 = row(-3), row(-2), row(-1)
    a1 = w[3] * x1
    b1 = w[2] * x1 + mask(-1) * (w[3] * x2)
    c1 = w[1] * x1 + mask(-1) * (w[2] * x2 + mask(-2) * (w[3] * x3))

    def conv_pair(k, carry):
        carry, d0 = conv_step(2 * k, carry)
        carry, d1 = conv_step(2 * k + 1, carry)
        co[pl.ds(pl.multiple_of(k * 2 * SEGS, 2 * SEGS), 2 * SEGS), :] = jnp.concatenate([d0, d1], 0).astype(BF16)
        return carry

    lax.fori_loop(0, seg_len // 2, conv_pair, (a1, b1, c1), unroll=8)

    weight = dequantized(panel_ref[0], scale_ref[0]) * BF16(0.5)
    gate[...] = jnp.dot(co[...], weight, preferred_element_type=F32)

    bias_r = jnp.broadcast_to(gb_ref[0:1, :] * 0.5, (SEGS, width))
    bias_i = jnp.broadcast_to(gb_ref[1:2, :] * 0.5, (SEGS, width))
    rate4 = jnp.broadcast_to(rate_ref[...] * (-4.0 * LOG2E), (SEGS, width))

    def scan_step(i, conv, carry):
        h, p = carry
        at = pl.ds(pl.multiple_of(i * SEGS, SEGS), SEGS)
        m = mask(i)
        v = rate4 * (1.0 + jnp.tanh(gate[at, :width] + bias_r))
        ti = 1.0 + jnp.tanh(gate[at, width:] + bias_i)
        decay = jnp.exp2(v)
        s = v * v
        series = ((s * SINH[3] + SINH[2]) * s + SINH[1]) * s + SINH[0]
        quarter = decay * (v * series)
        half = quarter * lax.rsqrt(jnp.maximum(quarter, 1e-37))
        half = jnp.where(m > 0.0, half, 0.5)
        decay = decay * m
        h = decay * h + ti * (conv * half)
        p = p * decay
        for c in range(width // 128):
            h_ref[c, at, :] = h[:, c * 128 : (c + 1) * 128]
            p_ref[c, at, :] = p[:, c * 128 : (c + 1) * 128]
        return h, p

    def scan_pair(k, carry):
        conv = co[pl.ds(pl.multiple_of(k * 2 * SEGS, 2 * SEGS), 2 * SEGS), :].astype(F32)
        carry = scan_step(2 * k, conv[:SEGS], carry)
        return scan_step(2 * k + 1, conv[SEGS:], carry)

    h, p = lax.fori_loop(
        0,
        seg_len // 2,
        scan_pair,
        (jnp.zeros((SEGS, width), F32), jnp.ones((SEGS, width), F32)),
        unroll=8,
    )
    ends_ref[0] = p
    ends_ref[1] = h
    tp, th = p[0:1], h[0:1]
    for s in range(1, SEGS):
        th = p[s : s + 1] * th + h[s : s + 1]
        tp = tp * p[s : s + 1]
    tot_ref[0:1, :] = tp
    tot_ref[1:2, :] = th


def mix_kernel(h_ref, p_ref, ends_ref, in_ref, y_ref, panel_ref, scale_ref, mixed_ref, kv_ref, carry):
    rows, width = y_ref.shape
    seg_len = rows // SEGS

    @pl.when(pl.program_id(0) == 0)
    def _():
        kv_ref[...] = jnp.zeros_like(kv_ref)

    c = in_ref[...]
    for s in range(SEGS):
        carry[s : s + 1, :] = c
        c = ends_ref[0, s : s + 1, :] * c + ends_ref[1, s : s + 1, :]
    weight = dequantized(panel_ref[...], scale_ref[0])

    def natural(ref, g, s):
        return jnp.concatenate(
            [ref[g, pl.ds(s + k * 8 * SEGS, 8, stride=SEGS), :] for k in range(seg_len // 8)], 0
        )

    for s in range(SEGS):
        at = slice(s * seg_len, (s + 1) * seg_len)
        y = y_ref[at, :].astype(F32)
        inner = y * (0.7978845608028654 + (0.7978845608028654 * 0.044715) * (y * y))
        gelu = (0.5 * y) * (1.0 + jnp.tanh(inner))
        local_h = jnp.concatenate([natural(h_ref, g, s) for g in range(width // 128)], 1)
        local_p = jnp.concatenate([natural(p_ref, g, s) for g in range(width // 128)], 1)
        mixed_ref[at, :] = ((local_h + local_p * carry[s : s + 1, :]) * gelu).astype(BF16)
    kv_ref[...] += jnp.dot(mixed_ref[...], weight, preferred_element_type=F32)


def sum_kernel(a_ref, b_ref, full_ref, half_ref):
    rows = half_ref.shape[0]
    full_ref[...] = (a_ref[...] + b_ref[...]).astype(BF16)
    at = pl.ds(pl.multiple_of(lax.axis_index("mp") * rows, rows), rows)
    half_ref[...] = (a_ref[at, :] + b_ref[at, :]).astype(BF16)


def attend_kernel(own, lags, has_prev, final, starts_ref, q_ref, *refs):
    refs = list(refs)
    take = lambda n: [refs.pop(0) for _ in range(n)]
    own_ref = take(1)[0] if own else None
    pairs = [take(2) for _ in lags]
    prev = take(2) if has_prev else None
    out = take(1) if final else take(2)
    low, score, top = take(3)
    acc, ml = take(2) if final else out
    rows = q_ref.shape[0]
    half = rows // 2
    step = pl.program_id(0)
    heads = pl.num_programs(0) - 1
    slot, last = step % 2, (step + 1) % 2
    me = lax.axis_index("tm")
    first = me * rows
    core = lax.axis_index("mp")
    turn = 2 * (me % 2) - 1
    scale = LOG2E / math.sqrt(HD)

    def lowest(t):
        d0 = jnp.maximum(t - (WINDOW - 1), 0)
        for d in range(DOCS):
            d0 = jnp.maximum(d0, jnp.where(starts_ref[d] <= t, starts_ref[d], 0))
        return d0

    @pl.when(step == 0)
    def _():
        low[...] = lowest(first + lax.broadcasted_iota(jnp.int32, (rows, 128), 0))

    lo_first = lowest(first)

    def wide(col, n):
        return jnp.concatenate([col] * (n // 128), 1)

    def fold(x, op):
        parts = [x[:, c * 128 : (c + 1) * 128] for c in range(x.shape[1] // 128)]
        return functools.reduce(op, parts)

    pieces = []
    if own:
        for r in range(2):
            pieces.append((r * half, half, (r + 1) * half, None, None, 0))
    for k, (even_part, odd_part) in enumerate(lags):
        pieces.append((0, rows, rows, pairs[k], first - (even_part + odd_part * turn) * rows, k + own))

    def keys_of(piece, lanes):
        if piece[3] is None:
            return own_ref[: piece[2], lanes]
        return jnp.concatenate([piece[3][0][:, lanes], piece[3][1][:, lanes]], 0)

    def score_pass(piece):
        r0, nr, nk, pair, start, t = piece
        at = slice(r0, r0 + nr)
        s = lax.dot_general(
            q_ref[at, :], keys_of(piece, slice(0, HD)), (((1,), (1,)), ((), ())), preferred_element_type=F32
        )
        lane = lax.broadcasted_iota(jnp.int32, (nr, 128), 1)
        lowr = low[at, :]
        cols = []
        for c in range(nk // 128):
            if pair is None:
                kpos = lane + (first + c * 128)
                qpos = lax.broadcasted_iota(jnp.int32, (nr, 128), 0) + (first + r0)
                ok = (kpos >= lowr) & (kpos <= qpos)
            else:
                side = core if c * 128 < half else 1 - core
                kpos = lane + (start + side * half + (c * 128) % half)
                ok = kpos >= lowr
            cols.append(jnp.where(ok, s[:, c * 128 : (c + 1) * 128] * scale, -1e30))
        s = jnp.concatenate(cols, 1)
        score[slot, t, at, :nk] = s
        top[slot, at, :] = jnp.maximum(top[slot, at, :], fold(s, jnp.maximum))

    def value_pass(piece):
        r0, nr, nk, pair, start, t = piece
        at = slice(r0, r0 + nr)
        m = ml[at, 0:1]
        p = jnp.exp2(score[last, t, at, :nk] - m)
        ml[at, 64:65] += jnp.sum(fold(p, jnp.add), axis=1, keepdims=True)
        acc[at, :] += jnp.dot(p.astype(BF16), keys_of(piece, slice(HD, 2 * HD)), preferred_element_type=F32)

    @pl.when(step < heads)
    def _():
        top[slot] = jnp.full((rows, 128), -1e30, F32)

    @pl.when(step > 0)
    def _():
        m = jnp.max(top[last], axis=1, keepdims=True)
        if has_prev:
            m0 = prev[1][:, 0:1]
            m = jnp.maximum(m, m0)
            fade = jnp.exp2(m0 - m)
            acc[...] = prev[0][...] * fade
            ml[:, 64:128] = jnp.broadcast_to(prev[1][:, 64:65] * fade, (rows, 64))
        else:
            acc[...] = jnp.zeros((rows, HD), F32)
            ml[:, 64:128] = jnp.zeros((rows, 64), F32)
        ml[:, 0:64] = jnp.broadcast_to(m, (rows, 64))

    for group in ([p for p in pieces if p[3] is None], *[[p] for p in pieces if p[3] is not None]):
        if not group:
            continue
        start = group[0][4]
        live = True if start is None else (start >= 0) & (start < first) & (start + rows > lo_first)

        @pl.when(live & (step == 0))
        def _(group=group):
            for piece in group:
                score_pass(piece)

        @pl.when(live & (step > 0) & (step < heads))
        def _(group=group):
            for piece in group:
                score_pass(piece)
                value_pass(piece)

        @pl.when(live & (step == heads))
        def _(group=group):
            for piece in group:
                value_pass(piece)

    if final:

        @pl.when(step > 0)
        def _():
            out[0][...] = (acc[...] / ml[:, 64:65]).astype(BF16)


def recur_call(starts, x, halo, conv_weight, conv_bias, gate_panel, gate_scale, gate_bias, decay_rate):
    rows, channels = x.shape
    blocks, width, _ = gate_panel.shape
    col = lambda b, s: (0, b)
    return pl.pallas_call(
        recur_kernel,
        grid_spec=pltpu.PrefetchScalarGridSpec(
            num_scalar_prefetch=1,
            grid=(blocks,),
            in_specs=[
                pl.BlockSpec((rows, width), col),
                pl.BlockSpec((CONV - 1, width), col),
                pl.BlockSpec((CONV, width), col),
                pl.BlockSpec((1, width), col),
                pl.BlockSpec((1, width, 2 * width), lambda b, s: (b, 0, 0)),
                pl.BlockSpec((1, width // SCALE_ROWS, 2 * width), lambda b, s: (b, 0, 0)),
                pl.BlockSpec((2, width), col),
                pl.BlockSpec((1, width), col),
            ],
            out_specs=[
                pl.BlockSpec((width // 128, rows, 128), lambda b, s: (b, 0, 0)),
                pl.BlockSpec((width // 128, rows, 128), lambda b, s: (b, 0, 0)),
                pl.BlockSpec((2, SEGS, width), lambda b, s: (0, 0, b)),
                pl.BlockSpec((2, width), col),
            ],
            scratch_shapes=[
                pltpu.VMEM((rows + 2 * SEGS, 128), F32),
                pltpu.VMEM((width // 128, rows + HIST * (SEGS + 1), 128), F32),
                pltpu.VMEM((rows, width), BF16),
                pltpu.VMEM((rows, 2 * width), F32),
            ],
        ),
        out_shape=[
            jax.ShapeDtypeStruct((channels // 128, rows, 128), F32),
            jax.ShapeDtypeStruct((channels // 128, rows, 128), F32),
            jax.ShapeDtypeStruct((2, SEGS, channels), F32),
            jax.ShapeDtypeStruct((2, channels), F32),
        ],
        name="recur",
    )(starts, x, halo, conv_weight, conv_bias, gate_panel, gate_scale, gate_bias, decay_rate)


def mix_call(h, p, ends, incoming, y, kv_panel, kv_scale):
    rows, channels = y.shape
    width = MIX_GROUPS * SCALE_ROWS
    col = lambda b: (0, b)
    out = kv_panel.shape[1]
    return pl.pallas_call(
        mix_kernel,
        grid=(channels // width,),
        in_specs=[
            pl.BlockSpec((width // 128, rows, 128), lambda b: (b, 0, 0)),
            pl.BlockSpec((width // 128, rows, 128), lambda b: (b, 0, 0)),
            pl.BlockSpec((2, SEGS, width), lambda b: (0, 0, b)),
            pl.BlockSpec((1, width), col),
            pl.BlockSpec((rows, width), col),
            pl.BlockSpec((width, out), lambda b: (b, 0)),
            pl.BlockSpec((1, MIX_GROUPS, out), lambda b: (b, 0, 0)),
        ],
        out_specs=[pl.BlockSpec((rows, width), col), pl.BlockSpec((rows, out), lambda b: (0, 0))],
        out_shape=[jax.ShapeDtypeStruct((rows, channels), BF16), jax.ShapeDtypeStruct((rows, out), F32)],
        scratch_shapes=[pltpu.VMEM((SEGS, width), F32)],
        name="mix",
    )(h, p, ends, incoming, y, kv_panel, kv_scale.reshape(-1, MIX_GROUPS, out))


def sum_call(a, b):
    rows, out = a.shape
    return pl.pallas_call(
        sum_kernel,
        out_shape=[jax.ShapeDtypeStruct((rows, out), BF16), jax.ShapeDtypeStruct((rows // 2, out), BF16)],
        compiler_params=pltpu.CompilerParams(vmem_limit_bytes=16 << 20),
        name="kvsum",
    )(a, b)


def attend_call(starts, q, own, halves, lags, prev, final):
    rows, width = q.shape
    heads = width // HD
    whole = lambda a: pl.BlockSpec(a.shape, lambda h, s: (0, 0))
    now = lambda h, s: (0, jnp.minimum(h, heads - 1))
    before = lambda h, s: (0, jnp.maximum(h - 1, 0))
    held = [] if own is None else [own]
    held += halves
    carried = [pl.BlockSpec((rows, HD), before), pl.BlockSpec((rows, 128), before)]
    tiles = len(lags) + (own is not None)
    if final:
        out_specs = pl.BlockSpec((rows, HD), before)
        out_shape = jax.ShapeDtypeStruct((rows, width), BF16)
        extra = [pltpu.VMEM((rows, HD), F32), pltpu.VMEM((rows, 128), F32)]
    else:
        out_specs = carried
        out_shape = [jax.ShapeDtypeStruct((rows, width), F32), jax.ShapeDtypeStruct((rows, heads * 128), F32)]
        extra = []
    return pl.pallas_call(
        functools.partial(attend_kernel, own is not None, lags, prev is not None, final),
        grid_spec=pltpu.PrefetchScalarGridSpec(
            num_scalar_prefetch=1,
            grid=(heads + 1,),
            in_specs=[pl.BlockSpec((rows, HD), now)]
            + [whole(a) for a in held]
            + (carried if prev is not None else []),
            out_specs=out_specs,
            scratch_shapes=[
                pltpu.VMEM((rows, 128), jnp.int32),
                pltpu.VMEM((2, tiles, rows, rows), F32),
                pltpu.VMEM((2, rows, 128), F32),
            ]
            + extra,
        ),
        out_shape=out_shape,
        compiler_params=pltpu.CompilerParams(vmem_limit_bytes=28 << 20),
        name="attend_own" if own is not None else "attend_end" if final else "attend_mid",
    )(starts, q, *held, *(prev or []))


def local(
    branch_x,
    branch_y,
    queries,
    conv_weight,
    conv_bias,
    gate_panel,
    gate_scale,
    gate_bias,
    decay_rate,
    kv_panel,
    kv_scale,
    segment_ids,
):
    rows = branch_x.shape[0]
    seq = segment_ids.shape[0]
    me = lax.axis_index("tm")
    halo = ring(branch_x[rows - CONV + 1 :], 1)
    starts = jnp.sum(
        (segment_ids[None, :] < jnp.arange(DOCS, dtype=jnp.int32)[:, None]).astype(jnp.int32), axis=1
    )
    h, p, ends, tot = recur_call(
        starts,
        branch_x,
        halo,
        conv_weight,
        conv_bias[None],
        gate_panel,
        gate_scale,
        gate_bias,
        decay_rate[None],
    )
    odd = (me % 2) == 1
    near = swap(tot)
    lower = jnp.where(odd, near, tot)
    upper = jnp.where(odd, tot, near)
    level = jnp.stack([lower[0] * upper[0], upper[0] * lower[1] + upper[1]])
    levels = -(-(seq // 2) // (2 * rows))
    past = [ring(level, 2 * k) for k in range(1, levels + 1)]
    incoming = jnp.zeros_like(tot[1])
    for k in range(levels, 0, -1):
        got = past[k - 1]
        incoming = jnp.where(me >= 2 * k, got[0] * incoming + got[1], 0.0)
    incoming = jnp.where(odd, near[0] * incoming + near[1], incoming)
    mixed, partial_kv = mix_call(h, p, ends, incoming[None], branch_y, kv_panel, kv_scale)
    own, half = sum_call(partial_kv, partner(partial_kv))

    levels = -(-WINDOW // rows) // 2
    carried = attend_call(starts, queries, own, [], [], None, False)
    straight = half
    for k in range(1, levels + 1):
        beyond = ring(straight, 2)
        crossed = swap(straight)
        tiles = [crossed, partner(crossed), beyond, partner(beyond)]
        lags = [(2 * k - 2, 1), (2 * k, 0)]
        carried = attend_call(starts, queries, None, tiles, lags, carried, False)
        straight = beyond
    crossed = swap(straight)
    tiles, lags = [crossed, partner(crossed)], [(2 * levels, 1)]
    carried = attend_call(starts, queries, None, tiles, lags, carried, True)
    return mixed, carried


def solution(mesh):
    in_specs = (
        P(("groups", "tm"), "mp"),
        P(("groups", "tm"), "mp"),
        P(("groups", "tm"), "mp"),
        P(None, "mp"),
        P("mp"),
        P("mp", None, None),
        P("mp", None, None),
        P(None, "mp"),
        P("mp"),
        P("mp", None),
        P("mp", None),
        P("groups"),
    )
    out_specs = (P(("groups", "tm"), "mp"), P(("groups", "tm"), "mp"))
    return jax.shard_map(local, mesh=mesh, in_specs=in_specs, out_specs=out_specs, check_vma=False)
```

```python
import functools
import math

import jax
import jax.numpy as jnp
from jax import lax
from jax.experimental import pallas as pl
from jax.experimental.pallas import tpu as pltpu
from jax.sharding import PartitionSpec as P

HD = 256
CONV = 4
WINDOW = 2048
SCALE_ROWS = 128
DOCS = 4
SEGS = 8
MIX_GROUPS = 4
GROUP = 2
HIST = 4
LOG2E = 1.4426950408889634
LN2 = 0.6931471805599453
SINH = [-0.5 * LN2 ** (2 * k + 1) / math.factorial(2 * k + 1) for k in range(4)]
F32 = jnp.float32
BF16 = jnp.bfloat16


def ring(x, lag):
    n = lax.axis_size("tm")
    return lax.ppermute(x, "tm", [(i, (i + lag) % n) for i in range(n)])


def swap(x):
    n = lax.axis_size("tm")
    return lax.ppermute(x, "tm", [(i, i ^ 1) for i in range(n)])


def partner(x):
    return lax.ppermute(x, "mp", [(0, 1), (1, 0)])


def dequantized(panel, scale):
    rows = panel.shape[0]
    parts = []
    for g in range(rows // SCALE_ROWS):
        part = panel[g * SCALE_ROWS : (g + 1) * SCALE_ROWS, :].astype(F32)
        parts.append((part * scale[g : g + 1, :]).astype(BF16))
    return jnp.concatenate(parts, 0)


def recur_kernel(
    starts_ref,
    x_ref,
    halo_ref,
    cw_ref,
    cb_ref,
    panel_ref,
    scale_ref,
    gb_ref,
    rate_ref,
    h_ref,
    p_ref,
    ends_ref,
    tot_ref,
    keep,
    xs,
    co,
    gate,
):
    rows, width = x_ref.shape
    seg_len = rows // SEGS
    base = lax.axis_index("tm") * rows

    @pl.when(pl.program_id(0) == 0)
    def _():
        def fill(i, carry):
            pos = base + i - 2 + seg_len * lax.broadcasted_iota(jnp.int32, (SEGS, 128), 0)
            hit = pos == starts_ref[0]
            for d in range(1, DOCS):
                hit = hit | (pos == starts_ref[d])
            keep[pl.ds(pl.multiple_of(i * SEGS, SEGS), SEGS), :] = jnp.where(hit, 0.0, 1.0)
            return carry

        lax.fori_loop(0, seg_len + 2, fill, 0)

    pitch = seg_len + HIST
    for c in range(width // 128):
        lanes = slice(c * 128, (c + 1) * 128)
        xs[c, HIST + 1 : 2 * HIST, :] = halo_ref[:, lanes].astype(F32)
        for s in range(1, SEGS):
            past = x_ref[s * seg_len - 2 * HIST : s * seg_len, lanes].astype(F32)
            xs[c, s * pitch : s * pitch + 2 * HIST, :] = past
        for s in range(SEGS):
            rest = x_ref[s * seg_len : (s + 1) * seg_len, lanes].astype(F32)
            xs[c, s * pitch + 2 * HIST : (s + 1) * pitch + HIST, :] = rest

    def mask(i):
        m = keep[pl.ds(pl.multiple_of((i + 2) * SEGS, SEGS), SEGS), :]
        return jnp.concatenate([m] * (width // 128), 1)

    def row(i):
        return jnp.concatenate(
            [xs[c, pl.ds(2 * HIST + i, SEGS, stride=pitch), :] for c in range(width // 128)], 1
        )

    w = [jnp.broadcast_to(cw_ref[j : j + 1, :], (SEGS, width)) for j in range(CONV)]
    bias = jnp.broadcast_to(cb_ref[...], (SEGS, width))

    def conv_step(i, carry):
        a, b, c = carry
        x = row(i)
        m = mask(i)
        d = w[0] * x + m * c + bias
        c = w[1] * x + m * b
        b = w[2] * x + m * a
        a = w[3] * x
        return (a, b, c), d

    x3, x2, x1 = row(-3), row(-2), row(-1)
    a1 = w[3] * x1
    b1 = w[2] * x1 + mask(-1) * (w[3] * x2)
    c1 = w[1] * x1 + mask(-1) * (w[2] * x2 + mask(-2) * (w[3] * x3))

    def conv_pair(k, carry):
        carry, d0 = conv_step(2 * k, carry)
        carry, d1 = conv_step(2 * k + 1, carry)
        co[pl.ds(pl.multiple_of(k * 2 * SEGS, 2 * SEGS), 2 * SEGS), :] = jnp.concatenate([d0, d1], 0).astype(BF16)
        return carry

    lax.fori_loop(0, seg_len // 2, conv_pair, (a1, b1, c1), unroll=8)

    weight = dequantized(panel_ref[0], scale_ref[0]) * BF16(0.5)
    gate[...] = jnp.dot(co[...], weight, preferred_element_type=F32)

    bias_r = jnp.broadcast_to(gb_ref[0:1, :] * 0.5, (SEGS, width))
    bias_i = jnp.broadcast_to(gb_ref[1:2, :] * 0.5, (SEGS, width))
    rate4 = jnp.broadcast_to(rate_ref[...] * (-4.0 * LOG2E), (SEGS, width))

    def scan_step(i, conv, carry):
        h, p = carry
        at = pl.ds(pl.multiple_of(i * SEGS, SEGS), SEGS)
        m = mask(i)
        v = rate4 * (1.0 + jnp.tanh(gate[at, :width] + bias_r))
        ti = 1.0 + jnp.tanh(gate[at, width:] + bias_i)
        decay = jnp.exp2(v)
        s = v * v
        series = ((s * SINH[3] + SINH[2]) * s + SINH[1]) * s + SINH[0]
        quarter = decay * (v * series)
        half = quarter * lax.rsqrt(jnp.maximum(quarter, 1e-37))
        half = jnp.where(m > 0.0, half, 0.5)
        decay = decay * m
        h = decay * h + ti * (conv * half)
        p = p * decay
        for c in range(width // 128):
            h_ref[c, at, :] = h[:, c * 128 : (c + 1) * 128]
            p_ref[c, at, :] = p[:, c * 128 : (c + 1) * 128]
        return h, p

    def scan_pair(k, carry):
        conv = co[pl.ds(pl.multiple_of(k * 2 * SEGS, 2 * SEGS), 2 * SEGS), :].astype(F32)
        carry = scan_step(2 * k, conv[:SEGS], carry)
        return scan_step(2 * k + 1, conv[SEGS:], carry)

    h, p = lax.fori_loop(
        0,
        seg_len // 2,
        scan_pair,
        (jnp.zeros((SEGS, width), F32), jnp.ones((SEGS, width), F32)),
        unroll=8,
    )
    ends_ref[0] = p
    ends_ref[1] = h
    tp, th = p[0:1], h[0:1]
    for s in range(1, SEGS):
        th = p[s : s + 1] * th + h[s : s + 1]
        tp = tp * p[s : s + 1]
    tot_ref[0:1, :] = tp
    tot_ref[1:2, :] = th


def mix_kernel(h_ref, p_ref, ends_ref, in_ref, y_ref, panel_ref, scale_ref, mixed_ref, kv_ref, carry):
    rows, width = y_ref.shape
    seg_len = rows // SEGS

    @pl.when(pl.program_id(0) == 0)
    def _():
        kv_ref[...] = jnp.zeros_like(kv_ref)

    c = in_ref[...]
    for s in range(SEGS):
        carry[s : s + 1, :] = c
        c = ends_ref[0, s : s + 1, :] * c + ends_ref[1, s : s + 1, :]
    weight = dequantized(panel_ref[...], scale_ref[0])

    def natural(ref, g, s):
        return jnp.concatenate(
            [ref[g, pl.ds(s + k * 8 * SEGS, 8, stride=SEGS), :] for k in range(seg_len // 8)], 0
        )

    for s in range(SEGS):
        at = slice(s * seg_len, (s + 1) * seg_len)
        y = y_ref[at, :].astype(F32)
        inner = y * (0.7978845608028654 + (0.7978845608028654 * 0.044715) * (y * y))
        gelu = (0.5 * y) * (1.0 + jnp.tanh(inner))
        local_h = jnp.concatenate([natural(h_ref, g, s) for g in range(width // 128)], 1)
        local_p = jnp.concatenate([natural(p_ref, g, s) for g in range(width // 128)], 1)
        mixed_ref[at, :] = ((local_h + local_p * carry[s : s + 1, :]) * gelu).astype(BF16)
    kv_ref[...] += jnp.dot(mixed_ref[...], weight, preferred_element_type=F32)


def sum_kernel(a_ref, b_ref, own_ref, half_ref):
    rows = half_ref.shape[0]
    both = a_ref[...] + b_ref[...]
    n = both.shape[0] // 2
    core = lax.axis_index("mp")
    parts = []
    for side in range(2):
        keys = both[side * n : (side + 1) * n, :HD].T.astype(BF16)
        values = both[side * n : (side + 1) * n, HD:].astype(BF16)
        own_ref[side, :HD, :] = keys
        own_ref[side, HD:, :] = values
    half_ref[...] = own_ref[core]


def attend_kernel(own, lags, has_prev, final, starts_ref, q_ref, *refs):
    refs = list(refs)
    take = lambda n: [refs.pop(0) for _ in range(n)]
    own_ref = take(1)[0] if own else None
    pairs = [take(2) for _ in lags]
    prev_acc, prev_m, prev_l = take(3) if has_prev else (None, None, None)
    out = take(1) if final else take(3)
    low, score, top = take(3)
    acc, m_ref, l_ref = take(3) if final else out
    rows = q_ref.shape[0]
    half = rows // 2
    me = lax.axis_index("tm")
    first = me * rows
    core = lax.axis_index("mp")
    turn = 2 * (me % 2) - 1
    scale = LOG2E / math.sqrt(HD)

    def lowest(t):
        d0 = jnp.maximum(t - (WINDOW - 1), 0)
        for d in range(DOCS):
            d0 = jnp.maximum(d0, jnp.where(starts_ref[d] <= t, starts_ref[d], 0))
        return d0

    @pl.when(pl.program_id(0) == 0)
    def _():
        low[...] = lowest(first + lax.broadcasted_iota(jnp.int32, (rows, 128), 0))

    lo_first = lowest(first)
    lo_last = lowest(first + rows - 1)

    def keys_of(pair, t):
        return own_ref[t, :HD, :] if pair is None else pair[t][:HD, :]

    def values_of(pair, t):
        return own_ref[t, HD:, :] if pair is None else pair[t][HD:, :]

    def score_pass(j, pair, start, masked):
        for h in range(GROUP):
            for t in range(2):
                r0 = half * t if pair is None else 0
                at = slice(r0, rows)
                s = jnp.dot(
                    q_ref[at, h * HD : (h + 1) * HD], keys_of(pair, t), preferred_element_type=F32
                )
                peak = top[h, at, :]
                for c in range(half // 128):
                    part = s[:, c * 128 : (c + 1) * 128] * scale
                    if masked:
                        side = t if pair is None else jnp.where(core == t, 0, 1)
                        kpos = lax.broadcasted_iota(jnp.int32, part.shape, 1) + (start + side * half + c * 128)
                        ok = kpos >= low[at, :]
                        if pair is None:
                            ok = ok & (kpos <= lax.broadcasted_iota(jnp.int32, part.shape, 0) + (first + r0))
                        part = jnp.where(ok, part, -1e30)
                    score[j, h, t, at, c * 128 : (c + 1) * 128] = part
                    peak = jnp.maximum(peak, part)
                top[h, at, :] = peak

    def value_pass(j, pair):
        for h in range(GROUP):
            spans = [(0, half, 1), (half, rows, 2)] if pair is None else [(0, rows, 2)]
            for r0, r1, n in spans:
                at = slice(r0, r1)
                m = m_ref[at, h * 128 : (h + 1) * 128]
                total = l_ref[at, h * 128 : (h + 1) * 128]
                ps, vs = [], []
                for t in range(n):
                    for c in range(half // 128):
                        p = jnp.exp2(score[j, h, t, at, c * 128 : (c + 1) * 128] - m)
                        total = total + p
                        ps.append(p.astype(BF16))
                    vs.append(values_of(pair, t))
                l_ref[at, h * 128 : (h + 1) * 128] = total
                acc[at, h * HD : (h + 1) * HD] += jnp.dot(
                    jnp.concatenate(ps, 1), jnp.concatenate(vs, 0), preferred_element_type=F32
                )

    tiles = [(None, first)] if own else []
    for k, (even_part, odd_part) in enumerate(lags):
        tiles.append((pairs[k], first - (even_part + odd_part * turn) * rows))
    live = [True if pair is None else (start >= 0) & (start < first) & (start + rows > lo_first) for pair, start in tiles]

    top[...] = jnp.full(top.shape, -1e30, F32)
    for j, (pair, start) in enumerate(tiles):
        if pair is None:
            score_pass(j, pair, start, True)
            continue

        @pl.when(live[j] & (start >= lo_last))
        def _(j=j, pair=pair, start=start):
            score_pass(j, pair, start, False)

        @pl.when(live[j] & (start < lo_last))
        def _(j=j, pair=pair, start=start):
            score_pass(j, pair, start, True)

    for h in range(GROUP):
        lanes = slice(h * 128, (h + 1) * 128)
        wide = slice(h * HD, (h + 1) * HD)
        m = jnp.broadcast_to(jnp.max(top[h], axis=1, keepdims=True), (rows, 128))
        if has_prev:
            m0 = prev_m[:, lanes]
            m = jnp.maximum(m, m0)
            fade = jnp.exp2(m0 - m)
            l_ref[:, lanes] = prev_l[:, lanes] * fade
            acc[:, wide] = prev_acc[:, wide] * jnp.concatenate([fade] * (HD // 128), 1)
        else:
            l_ref[:, lanes] = jnp.zeros((rows, 128), F32)
            acc[:, wide] = jnp.zeros((rows, HD), F32)
        m_ref[:, lanes] = m
    for j, (pair, start) in enumerate(tiles):
        if pair is None:
            value_pass(j, pair)
            continue

        @pl.when(live[j])
        def _(j=j, pair=pair):
            value_pass(j, pair)

    if final:
        for h in range(GROUP):
            total = jnp.sum(l_ref[:, h * 128 : (h + 1) * 128], axis=1, keepdims=True)
            share = jnp.broadcast_to(1.0 / total, (rows, 128))
            wide = slice(h * HD, (h + 1) * HD)
            out[0][:, wide] = (acc[:, wide] * jnp.concatenate([share] * (HD // 128), 1)).astype(BF16)


def recur_call(starts, x, halo, conv_weight, conv_bias, gate_panel, gate_scale, gate_bias, decay_rate):
    rows, channels = x.shape
    blocks, width, _ = gate_panel.shape
    col = lambda b, s: (0, b)
    return pl.pallas_call(
        recur_kernel,
        grid_spec=pltpu.PrefetchScalarGridSpec(
            num_scalar_prefetch=1,
            grid=(blocks,),
            in_specs=[
                pl.BlockSpec((rows, width), col),
                pl.BlockSpec((CONV - 1, width), col),
                pl.BlockSpec((CONV, width), col),
                pl.BlockSpec((1, width), col),
                pl.BlockSpec((1, width, 2 * width), lambda b, s: (b, 0, 0)),
                pl.BlockSpec((1, width // SCALE_ROWS, 2 * width), lambda b, s: (b, 0, 0)),
                pl.BlockSpec((2, width), col),
                pl.BlockSpec((1, width), col),
            ],
            out_specs=[
                pl.BlockSpec((width // 128, rows, 128), lambda b, s: (b, 0, 0)),
                pl.BlockSpec((width // 128, rows, 128), lambda b, s: (b, 0, 0)),
                pl.BlockSpec((2, SEGS, width), lambda b, s: (0, 0, b)),
                pl.BlockSpec((2, width), col),
            ],
            scratch_shapes=[
                pltpu.VMEM((rows + 2 * SEGS, 128), F32),
                pltpu.VMEM((width // 128, rows + HIST * (SEGS + 1), 128), F32),
                pltpu.VMEM((rows, width), BF16),
                pltpu.VMEM((rows, 2 * width), F32),
            ],
        ),
        out_shape=[
            jax.ShapeDtypeStruct((channels // 128, rows, 128), F32),
            jax.ShapeDtypeStruct((channels // 128, rows, 128), F32),
            jax.ShapeDtypeStruct((2, SEGS, channels), F32),
            jax.ShapeDtypeStruct((2, channels), F32),
        ],
        name="recur",
    )(starts, x, halo, conv_weight, conv_bias, gate_panel, gate_scale, gate_bias, decay_rate)


def mix_call(h, p, ends, incoming, y, kv_panel, kv_scale):
    rows, channels = y.shape
    width = MIX_GROUPS * SCALE_ROWS
    col = lambda b: (0, b)
    out = kv_panel.shape[1]
    return pl.pallas_call(
        mix_kernel,
        grid=(channels // width,),
        in_specs=[
            pl.BlockSpec((width // 128, rows, 128), lambda b: (b, 0, 0)),
            pl.BlockSpec((width // 128, rows, 128), lambda b: (b, 0, 0)),
            pl.BlockSpec((2, SEGS, width), lambda b: (0, 0, b)),
            pl.BlockSpec((1, width), col),
            pl.BlockSpec((rows, width), col),
            pl.BlockSpec((width, out), lambda b: (b, 0)),
            pl.BlockSpec((1, MIX_GROUPS, out), lambda b: (b, 0, 0)),
        ],
        out_specs=[pl.BlockSpec((rows, width), col), pl.BlockSpec((rows, out), lambda b: (0, 0))],
        out_shape=[jax.ShapeDtypeStruct((rows, channels), BF16), jax.ShapeDtypeStruct((rows, out), F32)],
        scratch_shapes=[pltpu.VMEM((SEGS, width), F32)],
        name="mix",
    )(h, p, ends, incoming, y, kv_panel, kv_scale.reshape(-1, MIX_GROUPS, out))


def sum_call(a, b):
    rows, out = a.shape
    half = rows // 2
    return pl.pallas_call(
        sum_kernel,
        out_shape=[
            jax.ShapeDtypeStruct((2, 2 * HD, half), BF16),
            jax.ShapeDtypeStruct((2 * HD, half), BF16),
        ],
        compiler_params=pltpu.CompilerParams(vmem_limit_bytes=16 << 20),
        name="kvsum",
    )(a, b)


def attend_call(starts, q, own, halves, lags, prev, final):
    rows, width = q.shape
    heads = width // HD
    whole = lambda a: pl.BlockSpec(a.shape, lambda h, s: (0,) * a.ndim)
    per_head = lambda h, s: (0, h)
    held = [] if own is None else [own]
    held += halves
    carried = [pl.BlockSpec((rows, GROUP * n), per_head) for n in (HD, 128, 128)]
    tiles = len(lags) + (own is not None)
    if final:
        out_specs = pl.BlockSpec((rows, GROUP * HD), per_head)
        out_shape = jax.ShapeDtypeStruct((rows, width), BF16)
        extra = [pltpu.VMEM((rows, GROUP * n), F32) for n in (HD, 128, 128)]
    else:
        out_specs = carried
        out_shape = [jax.ShapeDtypeStruct((rows, heads * n), F32) for n in (HD, 128, 128)]
        extra = []
    return pl.pallas_call(
        functools.partial(attend_kernel, own is not None, lags, prev is not None, final),
        grid_spec=pltpu.PrefetchScalarGridSpec(
            num_scalar_prefetch=1,
            grid=(heads // GROUP,),
            in_specs=[pl.BlockSpec((rows, GROUP * HD), per_head)]
            + [whole(a) for a in held]
            + (carried if prev is not None else []),
            out_specs=out_specs,
            scratch_shapes=[
                pltpu.VMEM((rows, 128), jnp.int32),
                pltpu.VMEM((tiles, GROUP, 2, rows, rows // 2), F32),
                pltpu.VMEM((GROUP, rows, 128), F32),
            ]
            + extra,
        ),
        out_shape=out_shape,
        cost_estimate=pl.CostEstimate(
            flops=4 * tiles * rows * rows * width,
            bytes_accessed=4 * rows * width,
            transcendentals=tiles * rows * rows * heads,
        ),
        compiler_params=pltpu.CompilerParams(vmem_limit_bytes=32 << 20),
        name="attend_own" if own is not None else "attend_end" if final else "attend_mid",
    )(starts, q, *held, *(prev or []))


def local(
    branch_x,
    branch_y,
    queries,
    conv_weight,
    conv_bias,
    gate_panel,
    gate_scale,
    gate_bias,
    decay_rate,
    kv_panel,
    kv_scale,
    segment_ids,
):
    rows = branch_x.shape[0]
    seq = segment_ids.shape[0]
    me = lax.axis_index("tm")
    halo = ring(branch_x[rows - CONV + 1 :], 1)
    starts = jnp.sum(
        (segment_ids[None, :] < jnp.arange(DOCS, dtype=jnp.int32)[:, None]).astype(jnp.int32), axis=1
    )
    h, p, ends, tot = recur_call(
        starts,
        branch_x,
        halo,
        conv_weight,
        conv_bias[None],
        gate_panel,
        gate_scale,
        gate_bias,
        decay_rate[None],
    )
    odd = (me % 2) == 1
    near = swap(tot)
    lower = jnp.where(odd, near, tot)
    upper = jnp.where(odd, tot, near)
    level = jnp.stack([lower[0] * upper[0], upper[0] * lower[1] + upper[1]])
    levels = -(-(seq // 2) // (2 * rows))
    past = [ring(level, 2 * k) for k in range(1, levels + 1)]
    incoming = jnp.zeros_like(tot[1])
    for k in range(levels, 0, -1):
        got = past[k - 1]
        incoming = jnp.where(me >= 2 * k, got[0] * incoming + got[1], 0.0)
    incoming = jnp.where(odd, near[0] * incoming + near[1], incoming)
    mixed, partial_kv = mix_call(h, p, ends, incoming[None], branch_y, kv_panel, kv_scale)
    own, half = sum_call(partial_kv, partner(partial_kv))

    levels = -(-WINDOW // rows) // 2
    straight, tiles, lags = [half], [], []
    for k in range(1, levels + 1):
        straight.append(ring(straight[-1], 2))
        crossed = swap(straight[-2])
        tiles.append([crossed, partner(crossed), straight[-1], partner(straight[-1])])
        lags.append([(2 * k - 2, 1), (2 * k, 0)])
    crossed = swap(straight[-1])
    tiles.append([crossed, partner(crossed)])
    lags.append([(2 * levels, 1)])
    attended = attend_call(starts, queries, own, tiles[0], lags[0], None, False)
    attended = attend_call(starts, queries, None, sum(tiles[1:], []), sum(lags[1:], []), attended, True)
    return mixed, attended


def solution(mesh):
    in_specs = (
        P(("groups", "tm"), "mp"),
        P(("groups", "tm"), "mp"),
        P(("groups", "tm"), "mp"),
        P(None, "mp"),
        P("mp"),
        P("mp", None, None),
        P("mp", None, None),
        P(None, "mp"),
        P("mp"),
        P("mp", None),
        P("mp", None),
        P("groups"),
    )
    out_specs = (P(("groups", "tm"), "mp"), P(("groups", "tm"), "mp"))
    return jax.shard_map(local, mesh=mesh, in_specs=in_specs, out_specs=out_specs, check_vma=False)
```

```python
import functools
import math

import jax
import jax.numpy as jnp
from jax import lax
from jax.experimental import pallas as pl
from jax.experimental.pallas import tpu as pltpu
from jax.sharding import PartitionSpec as P


HD = 256
CONV = 4
WINDOW = 2048
SCALE_ROWS = 128
DOCS = 4
SEGS = 8
MIX_GROUPS = 2
GROUP = 2
HIST = 4
LOG2E = 1.4426950408889634
LN2 = 0.6931471805599453
SINH = [-0.5 * LN2 ** (2 * k + 1) / math.factorial(2 * k + 1) for k in range(4)]
F32 = jnp.float32
BF16 = jnp.bfloat16


def ring(x, lag):
    n = lax.axis_size("tm")
    return lax.ppermute(x, "tm", [(i, (i + lag) % n) for i in range(n)])


def swap(x):
    n = lax.axis_size("tm")
    return lax.ppermute(x, "tm", [(i, i ^ 1) for i in range(n)])


def partner(x):
    return lax.ppermute(x, "mp", [(0, 1), (1, 0)])


def dequantized(panel, scale):
    rows = panel.shape[0]
    parts = []
    for g in range(rows // SCALE_ROWS):
        part = panel[g * SCALE_ROWS : (g + 1) * SCALE_ROWS, :].astype(F32)
        parts.append((part * scale[g : g + 1, :]).astype(BF16))
    return jnp.concatenate(parts, 0)


def recur_kernel(
    starts_ref,
    x_ref,
    halo_ref,
    cw_ref,
    cb_ref,
    panel_ref,
    scale_ref,
    gb_ref,
    rate_ref,
    h_ref,
    p_ref,
    ends_ref,
    tot_ref,
    keep,
    xs,
    co,
    gate,
):
    rows, width = x_ref.shape
    seg_len = rows // SEGS
    base = lax.axis_index("tm") * rows

    @pl.when(pl.program_id(0) == 0)
    def _():
        def fill(i, carry):
            pos = base + i - 2 + seg_len * lax.broadcasted_iota(jnp.int32, (SEGS, 128), 0)
            hit = pos == starts_ref[0]
            for d in range(1, DOCS):
                hit = hit | (pos == starts_ref[d])
            keep[pl.ds(pl.multiple_of(i * SEGS, SEGS), SEGS), :] = jnp.where(hit, 0.0, 1.0)
            return carry

        lax.fori_loop(0, seg_len + 2, fill, 0)

    pitch = seg_len + HIST
    for c in range(width // 128):
        lanes = slice(c * 128, (c + 1) * 128)
        xs[c, HIST + 1 : 2 * HIST, :] = halo_ref[:, lanes].astype(F32)
        for s in range(1, SEGS):
            past = x_ref[s * seg_len - 2 * HIST : s * seg_len, lanes].astype(F32)
            xs[c, s * pitch : s * pitch + 2 * HIST, :] = past
        for s in range(SEGS):
            rest = x_ref[s * seg_len : (s + 1) * seg_len, lanes].astype(F32)
            xs[c, s * pitch + 2 * HIST : (s + 1) * pitch + HIST, :] = rest

    def mask(i):
        m = keep[pl.ds(pl.multiple_of((i + 2) * SEGS, SEGS), SEGS), :]
        return jnp.concatenate([m] * (width // 128), 1)

    def row(i):
        return jnp.concatenate(
            [xs[c, pl.ds(2 * HIST + i, SEGS, stride=pitch), :] for c in range(width // 128)], 1
        )

    w = [jnp.broadcast_to(cw_ref[j : j + 1, :], (SEGS, width)) for j in range(CONV)]
    bias = jnp.broadcast_to(cb_ref[...], (SEGS, width))

    def conv_step(i, carry):
        a, b, c = carry
        x = row(i)
        m = mask(i)
        d = w[0] * x + m * c + bias
        c = w[1] * x + m * b
        b = w[2] * x + m * a
        a = w[3] * x
        return (a, b, c), d

    x3, x2, x1 = row(-3), row(-2), row(-1)
    a1 = w[3] * x1
    b1 = w[2] * x1 + mask(-1) * (w[3] * x2)
    c1 = w[1] * x1 + mask(-1) * (w[2] * x2 + mask(-2) * (w[3] * x3))

    def conv_pair(k, carry):
        carry, d0 = conv_step(2 * k, carry)
        carry, d1 = conv_step(2 * k + 1, carry)
        co[pl.ds(pl.multiple_of(k * 2 * SEGS, 2 * SEGS), 2 * SEGS), :] = jnp.concatenate([d0, d1], 0).astype(BF16)
        return carry

    lax.fori_loop(0, seg_len // 2, conv_pair, (a1, b1, c1), unroll=8)

    weight = dequantized(panel_ref[0], scale_ref[0]) * BF16(0.5)
    gate[...] = jnp.dot(co[...], weight, preferred_element_type=F32)

    bias_r = jnp.broadcast_to(gb_ref[0:1, :] * 0.5, (SEGS, width))
    bias_i = jnp.broadcast_to(gb_ref[1:2, :] * 0.5, (SEGS, width))
    rate4 = jnp.broadcast_to(rate_ref[...] * (-4.0 * LOG2E), (SEGS, width))

    def scan_step(i, conv, carry):
        h, p = carry
        at = pl.ds(pl.multiple_of(i * SEGS, SEGS), SEGS)
        m = mask(i)
        v = rate4 * (1.0 + jnp.tanh(gate[at, :width] + bias_r))
        ti = 1.0 + jnp.tanh(gate[at, width:] + bias_i)
        decay = jnp.exp2(v)
        s = v * v
        series = ((s * SINH[3] + SINH[2]) * s + SINH[1]) * s + SINH[0]
        quarter = decay * (v * series)
        half = quarter * lax.rsqrt(jnp.maximum(quarter, 1e-37))
        half = jnp.where(m > 0.0, half, 0.5)
        decay = decay * m
        h = decay * h + ti * (conv * half)
        p = p * decay
        for c in range(width // 128):
            h_ref[c, at, :] = h[:, c * 128 : (c + 1) * 128]
            p_ref[c, at, :] = p[:, c * 128 : (c + 1) * 128]
        return h, p

    def scan_pair(k, carry):
        conv = co[pl.ds(pl.multiple_of(k * 2 * SEGS, 2 * SEGS), 2 * SEGS), :].astype(F32)
        carry = scan_step(2 * k, conv[:SEGS], carry)
        return scan_step(2 * k + 1, conv[SEGS:], carry)

    h, p = lax.fori_loop(
        0,
        seg_len // 2,
        scan_pair,
        (jnp.zeros((SEGS, width), F32), jnp.ones((SEGS, width), F32)),
        unroll=8,
    )
    ends_ref[0] = p
    ends_ref[1] = h
    tp, th = p[0:1], h[0:1]
    for s in range(1, SEGS):
        th = p[s : s + 1] * th + h[s : s + 1]
        tp = tp * p[s : s + 1]
    tot_ref[0:1, :] = tp
    tot_ref[1:2, :] = th


def mix_kernel(h_ref, p_ref, ends_ref, in_ref, y_ref, panel_ref, scale_ref, mixed_ref, kv_ref, carry):
    rows, width = y_ref.shape
    seg_len = rows // SEGS

    @pl.when(pl.program_id(0) == 0)
    def _():
        kv_ref[...] = jnp.zeros_like(kv_ref)

    c = in_ref[...]
    for s in range(SEGS):
        carry[s : s + 1, :] = c
        c = ends_ref[0, s : s + 1, :] * c + ends_ref[1, s : s + 1, :]
    weight = dequantized(panel_ref[...], scale_ref[0])

    def natural(ref, g, s):
        return jnp.concatenate(
            [ref[g, pl.ds(s + k * 8 * SEGS, 8, stride=SEGS), :] for k in range(seg_len // 8)], 0
        )

    for s in range(SEGS):
        at = slice(s * seg_len, (s + 1) * seg_len)
        y = y_ref[at, :].astype(F32)
        inner = y * (0.7978845608028654 + (0.7978845608028654 * 0.044715) * (y * y))
        gelu = (0.5 * y) * (1.0 + jnp.tanh(inner))
        local_h = jnp.concatenate([natural(h_ref, g, s) for g in range(width // 128)], 1)
        local_p = jnp.concatenate([natural(p_ref, g, s) for g in range(width // 128)], 1)
        mixed_ref[at, :] = ((local_h + local_p * carry[s : s + 1, :]) * gelu).astype(BF16)
    kv_ref[...] += jnp.dot(mixed_ref[...], weight, preferred_element_type=F32)


def sum_kernel(a_ref, b_ref, own_ref, half_ref):
    both = a_ref[...] + b_ref[...]
    n = both.shape[0] // 2
    core = lax.axis_index("mp")
    for side in range(2):
        keys = both[side * n : (side + 1) * n, :HD].T.astype(BF16)
        values = both[side * n : (side + 1) * n, HD:].astype(BF16)
        own_ref[side, :HD, :] = keys
        own_ref[side, HD:, :] = values
    half_ref[...] = own_ref[core]


def attend_kernel(own, lags, has_prev, final, starts_ref, q_ref, *refs):
    refs = list(refs)
    take = lambda n: [refs.pop(0) for _ in range(n)]
    own_ref = take(1)[0] if own else None
    pairs = [take(2) for _ in lags]
    prev_acc, prev_m, prev_l = take(3) if has_prev else (None, None, None)
    out = take(1) if final else take(3)
    low, score, top = take(3)
    acc, m_ref, l_ref = take(3) if final else out
    rows = q_ref.shape[0]
    half = rows // 2
    me = lax.axis_index("tm")
    first = me * rows
    core = lax.axis_index("mp")
    turn = 2 * (me % 2) - 1
    scale = LOG2E / math.sqrt(HD)

    def lowest(t):
        d0 = jnp.maximum(t - (WINDOW - 1), 0)
        for d in range(DOCS):
            d0 = jnp.maximum(d0, jnp.where(starts_ref[d] <= t, starts_ref[d], 0))
        return d0

    @pl.when(pl.program_id(0) == 0)
    def _():
        low[...] = lowest(first + lax.broadcasted_iota(jnp.int32, (rows, 128), 0))

    lo_first = lowest(first)
    lo_last = lowest(first + rows - 1)

    def keys_of(pair, t):
        return own_ref[t, :HD, :] if pair is None else pair[t][:HD, :]

    def values_of(pair, t):
        return own_ref[t, HD:, :] if pair is None else pair[t][HD:, :]

    def score_pass(j, pair, start, masked):
        for h in range(GROUP):
            for t in range(2):
                r0 = half * t if pair is None else 0
                at = slice(r0, rows)
                s = jnp.dot(
                    q_ref[at, h * HD : (h + 1) * HD], keys_of(pair, t), preferred_element_type=F32
                )
                peak = top[h, at, :]
                for c in range(half // 128):
                    part = s[:, c * 128 : (c + 1) * 128] * scale
                    if masked:
                        side = t if pair is None else jnp.where(core == t, 0, 1)
                        kpos = lax.broadcasted_iota(jnp.int32, part.shape, 1) + (start + side * half + c * 128)
                        ok = kpos >= low[at, :]
                        if pair is None:
                            ok = ok & (kpos <= lax.broadcasted_iota(jnp.int32, part.shape, 0) + (first + r0))
                        part = jnp.where(ok, part, -1e30)
                    score[j, h, t, at, c * 128 : (c + 1) * 128] = part
                    peak = jnp.maximum(peak, part)
                top[h, at, :] = peak

    def value_pass(j, pair):
        for h in range(GROUP):
            spans = [(0, half, 1), (half, rows, 2)] if pair is None else [(0, rows, 2)]
            for r0, r1, n in spans:
                at = slice(r0, r1)
                m = m_ref[at, h * 128 : (h + 1) * 128]
                total = l_ref[at, h * 128 : (h + 1) * 128]
                ps, vs = [], []
                for t in range(n):
                    for c in range(half // 128):
                        p = jnp.exp2(score[j, h, t, at, c * 128 : (c + 1) * 128] - m)
                        total = total + p
                        ps.append(p.astype(BF16))
                    vs.append(values_of(pair, t))
                l_ref[at, h * 128 : (h + 1) * 128] = total
                acc[at, h * HD : (h + 1) * HD] += jnp.dot(
                    jnp.concatenate(ps, 1), jnp.concatenate(vs, 0), preferred_element_type=F32
                )

    tiles = [(None, first)] if own else []
    for k, (even_part, odd_part) in enumerate(lags):
        tiles.append((pairs[k], first - (even_part + odd_part * turn) * rows))
    live = [True if pair is None else (start >= 0) & (start < first) & (start + rows > lo_first) for pair, start in tiles]

    top[...] = jnp.full(top.shape, -1e30, F32)
    for j, (pair, start) in enumerate(tiles):
        if pair is None:
            score_pass(j, pair, start, True)
            continue

        @pl.when(live[j] & (start >= lo_last))
        def _(j=j, pair=pair, start=start):
            score_pass(j, pair, start, False)

        @pl.when(live[j] & (start < lo_last))
        def _(j=j, pair=pair, start=start):
            score_pass(j, pair, start, True)

    for h in range(GROUP):
        lanes = slice(h * 128, (h + 1) * 128)
        wide = slice(h * HD, (h + 1) * HD)
        m = jnp.broadcast_to(jnp.max(top[h], axis=1, keepdims=True), (rows, 128))
        if has_prev:
            m0 = prev_m[:, lanes]
            m = jnp.maximum(m, m0)
            fade = jnp.exp2(m0 - m)
            l_ref[:, lanes] = prev_l[:, lanes] * fade
            acc[:, wide] = prev_acc[:, wide] * jnp.concatenate([fade] * (HD // 128), 1)
        else:
            l_ref[:, lanes] = jnp.zeros((rows, 128), F32)
            acc[:, wide] = jnp.zeros((rows, HD), F32)
        m_ref[:, lanes] = m
    for j, (pair, start) in enumerate(tiles):
        if pair is None:
            value_pass(j, pair)
            continue

        @pl.when(live[j])
        def _(j=j, pair=pair):
            value_pass(j, pair)

    if final:
        for h in range(GROUP):
            total = jnp.sum(l_ref[:, h * 128 : (h + 1) * 128], axis=1, keepdims=True)
            share = jnp.broadcast_to(1.0 / total, (rows, 128))
            wide = slice(h * HD, (h + 1) * HD)
            out[0][:, wide] = (acc[:, wide] * jnp.concatenate([share] * (HD // 128), 1)).astype(BF16)


def recur_call(starts, x, halo, conv_weight, conv_bias, gate_panel, gate_scale, gate_bias, decay_rate):
    rows, channels = x.shape
    blocks, width, _ = gate_panel.shape
    col = lambda b, s: (0, b)
    return pl.pallas_call(
        recur_kernel,
        grid_spec=pltpu.PrefetchScalarGridSpec(
            num_scalar_prefetch=1,
            grid=(blocks,),
            in_specs=[
                pl.BlockSpec((rows, width), col),
                pl.BlockSpec((CONV - 1, width), col),
                pl.BlockSpec((CONV, width), col),
                pl.BlockSpec((1, width), col),
                pl.BlockSpec((1, width, 2 * width), lambda b, s: (b, 0, 0)),
                pl.BlockSpec((1, width // SCALE_ROWS, 2 * width), lambda b, s: (b, 0, 0)),
                pl.BlockSpec((2, width), col),
                pl.BlockSpec((1, width), col),
            ],
            out_specs=[
                pl.BlockSpec((width // 128, rows, 128), lambda b, s: (b, 0, 0)),
                pl.BlockSpec((width // 128, rows, 128), lambda b, s: (b, 0, 0)),
                pl.BlockSpec((2, SEGS, width), lambda b, s: (0, 0, b)),
                pl.BlockSpec((2, width), col),
            ],
            scratch_shapes=[
                pltpu.VMEM((rows + 2 * SEGS, 128), F32),
                pltpu.VMEM((width // 128, rows + HIST * (SEGS + 1), 128), F32),
                pltpu.VMEM((rows, width), BF16),
                pltpu.VMEM((rows, 2 * width), F32),
            ],
        ),
        out_shape=[
            jax.ShapeDtypeStruct((channels // 128, rows, 128), F32),
            jax.ShapeDtypeStruct((channels // 128, rows, 128), F32),
            jax.ShapeDtypeStruct((2, SEGS, channels), F32),
            jax.ShapeDtypeStruct((2, channels), F32),
        ],
        name="recur",
    )(starts, x, halo, conv_weight, conv_bias, gate_panel, gate_scale, gate_bias, decay_rate)


def mix_call(h, p, ends, incoming, y, kv_panel, kv_scale):
    rows, channels = y.shape
    width = MIX_GROUPS * SCALE_ROWS
    col = lambda b: (0, b)
    out = kv_panel.shape[1]
    return pl.pallas_call(
        mix_kernel,
        grid=(channels // width,),
        in_specs=[
            pl.BlockSpec((width // 128, rows, 128), lambda b: (b, 0, 0)),
            pl.BlockSpec((width // 128, rows, 128), lambda b: (b, 0, 0)),
            pl.BlockSpec((2, SEGS, width), lambda b: (0, 0, b)),
            pl.BlockSpec((1, width), col),
            pl.BlockSpec((rows, width), col),
            pl.BlockSpec((width, out), lambda b: (b, 0)),
            pl.BlockSpec((1, MIX_GROUPS, out), lambda b: (b, 0, 0)),
        ],
        out_specs=[pl.BlockSpec((rows, width), col), pl.BlockSpec((rows, out), lambda b: (0, 0))],
        out_shape=[jax.ShapeDtypeStruct((rows, channels), BF16), jax.ShapeDtypeStruct((rows, out), F32)],
        scratch_shapes=[pltpu.VMEM((SEGS, width), F32)],
        name="mix",
    )(h, p, ends, incoming, y, kv_panel, kv_scale.reshape(-1, MIX_GROUPS, out))


def sum_call(a, b):
    rows, _ = a.shape
    half = rows // 2
    return pl.pallas_call(
        sum_kernel,
        out_shape=[
            jax.ShapeDtypeStruct((2, 2 * HD, half), BF16),
            jax.ShapeDtypeStruct((2 * HD, half), BF16),
        ],
        compiler_params=pltpu.CompilerParams(vmem_limit_bytes=16 << 20),
        name="kvsum",
    )(a, b)


def attend_call(starts, q, own, halves, lags, prev, final):
    rows, width = q.shape
    heads = width // HD
    whole = lambda a: pl.BlockSpec(a.shape, lambda h, s: (0,) * a.ndim)
    per_head = lambda h, s: (0, h)
    held = [] if own is None else [own]
    held += halves
    carried = [pl.BlockSpec((rows, GROUP * n), per_head) for n in (HD, 128, 128)]
    tiles = len(lags) + (own is not None)
    if final:
        out_specs = pl.BlockSpec((rows, GROUP * HD), per_head)
        out_shape = jax.ShapeDtypeStruct((rows, width), BF16)
        extra = [pltpu.VMEM((rows, GROUP * n), F32) for n in (HD, 128, 128)]
    else:
        out_specs = carried
        out_shape = [jax.ShapeDtypeStruct((rows, heads * n), F32) for n in (HD, 128, 128)]
        extra = []
    return pl.pallas_call(
        functools.partial(attend_kernel, own is not None, lags, prev is not None, final),
        grid_spec=pltpu.PrefetchScalarGridSpec(
            num_scalar_prefetch=1,
            grid=(heads // GROUP,),
            in_specs=[pl.BlockSpec((rows, GROUP * HD), per_head)]
            + [whole(a) for a in held]
            + (carried if prev is not None else []),
            out_specs=out_specs,
            scratch_shapes=[
                pltpu.VMEM((rows, 128), jnp.int32),
                pltpu.VMEM((tiles, GROUP, 2, rows, rows // 2), F32),
                pltpu.VMEM((GROUP, rows, 128), F32),
            ]
            + extra,
        ),
        out_shape=out_shape,
        cost_estimate=pl.CostEstimate(
            flops=4 * tiles * rows * rows * width,
            bytes_accessed=4 * rows * width,
            transcendentals=tiles * rows * rows * heads,
        ),
        compiler_params=pltpu.CompilerParams(vmem_limit_bytes=32 << 20),
        name="attend_own" if own is not None else "attend_end" if final else "attend_mid",
    )(starts, q, *held, *(prev or []))


def local(
    branch_x,
    branch_y,
    queries,
    conv_weight,
    conv_bias,
    gate_panel,
    gate_scale,
    gate_bias,
    decay_rate,
    kv_panel,
    kv_scale,
    segment_ids,
):
    rows = branch_x.shape[0]
    seq = segment_ids.shape[0]
    me = lax.axis_index("tm")
    halo = ring(branch_x[rows - CONV + 1 :], 1)
    starts = jnp.sum(
        (segment_ids[None, :] < jnp.arange(DOCS, dtype=jnp.int32)[:, None]).astype(jnp.int32), axis=1
    )
    h, p, ends, tot = recur_call(
        starts,
        branch_x,
        halo,
        conv_weight,
        conv_bias[None],
        gate_panel,
        gate_scale,
        gate_bias,
        decay_rate[None],
    )
    odd = (me % 2) == 1
    near = swap(tot)
    lower = jnp.where(odd, near, tot)
    upper = jnp.where(odd, tot, near)
    level = jnp.stack([lower[0] * upper[0], upper[0] * lower[1] + upper[1]])
    levels = -(-(seq // 2) // (2 * rows))
    past = [ring(level, 2 * k) for k in range(1, levels + 1)]
    incoming = jnp.zeros_like(tot[1])
    for k in range(levels, 0, -1):
        got = past[k - 1]
        incoming = jnp.where(me >= 2 * k, got[0] * incoming + got[1], 0.0)
    incoming = jnp.where(odd, near[0] * incoming + near[1], incoming)
    mixed, partial_kv = mix_call(h, p, ends, incoming[None], branch_y, kv_panel, kv_scale)
    own, half = sum_call(partial_kv, partner(partial_kv))

    levels = -(-WINDOW // rows) // 2
    straight, attended = half, None
    for k in range(levels + 1):
        last = k == levels
        beyond = None if last else ring(straight, 2)
        crossed = swap(straight)
        if k == 0:
            attended = attend_call(starts, queries, own, [], [], None, False)
        else:
            attended = attend_call(starts, queries, None, tiles, lags, attended, False)
        tiles, lags = [crossed, partner(crossed)], [(2 * k, 1)]
        if not last:
            tiles += [beyond, partner(beyond)]
            lags.append((2 * k + 2, 0))
        straight = beyond
    attended = attend_call(starts, queries, None, tiles, lags, attended, True)
    return mixed, attended


def solution(mesh):
    in_specs = (
        P(("groups", "tm"), "mp"),
        P(("groups", "tm"), "mp"),
        P(("groups", "tm"), "mp"),
        P(None, "mp"),
        P("mp"),
        P("mp", None, None),
        P("mp", None, None),
        P(None, "mp"),
        P("mp"),
        P("mp", None),
        P("mp", None),
        P("groups"),
    )
    out_specs = (P(("groups", "tm"), "mp"), P(("groups", "tm"), "mp"))
    return jax.shard_map(local, mesh=mesh, in_specs=in_specs, out_specs=out_specs, check_vma=False)
```

```python
import functools
import math

import jax
import jax.numpy as jnp
from jax import lax
from jax.experimental import pallas as pl
from jax.experimental.pallas import tpu as pltpu
from jax.sharding import PartitionSpec as P


HD = 256
CONV = 4
WINDOW = 2048
SCALE_ROWS = 128
DOCS = 4
SEGS = 8
MIX_GROUPS = 4
GROUP = 2
HIST = 4
LOG2E = 1.4426950408889634
LN2 = 0.6931471805599453
SINH = [-0.5 * LN2 ** (2 * k + 1) / math.factorial(2 * k + 1) for k in range(4)]
F32 = jnp.float32
BF16 = jnp.bfloat16


def ring(x, lag):
    n = lax.axis_size("tm")
    return lax.ppermute(x, "tm", [(i, (i + lag) % n) for i in range(n)])


def swap(x):
    n = lax.axis_size("tm")
    return lax.ppermute(x, "tm", [(i, i ^ 1) for i in range(n)])


def partner(x):
    return lax.ppermute(x, "mp", [(0, 1), (1, 0)])


def dequantized(panel, scale):
    rows = panel.shape[0]
    parts = []
    for g in range(rows // SCALE_ROWS):
        part = panel[g * SCALE_ROWS : (g + 1) * SCALE_ROWS, :].astype(F32)
        parts.append((part * scale[g : g + 1, :]).astype(BF16))
    return jnp.concatenate(parts, 0)


def recur_kernel(
    starts_ref,
    x_ref,
    halo_ref,
    cw_ref,
    cb_ref,
    panel_ref,
    scale_ref,
    gb_ref,
    rate_ref,
    h_ref,
    p_ref,
    ends_ref,
    tot_ref,
    keep,
    xs,
    co,
    gate,
):
    rows, width = x_ref.shape
    seg_len = rows // SEGS
    base = lax.axis_index("tm") * rows

    @pl.when(pl.program_id(0) == 0)
    def _():
        def fill(i, carry):
            pos = base + i - 2 + seg_len * lax.broadcasted_iota(jnp.int32, (SEGS, 128), 0)
            hit = pos == starts_ref[0]
            for d in range(1, DOCS):
                hit = hit | (pos == starts_ref[d])
            keep[pl.ds(pl.multiple_of(i * SEGS, SEGS), SEGS), :] = jnp.where(hit, 0.0, 1.0)
            return carry

        lax.fori_loop(0, seg_len + 2, fill, 0)

    pitch = seg_len + HIST
    for c in range(width // 128):
        lanes = slice(c * 128, (c + 1) * 128)
        xs[c, HIST + 1 : 2 * HIST, :] = halo_ref[:, lanes].astype(F32)
        for s in range(1, SEGS):
            past = x_ref[s * seg_len - 2 * HIST : s * seg_len, lanes].astype(F32)
            xs[c, s * pitch : s * pitch + 2 * HIST, :] = past
        for s in range(SEGS):
            rest = x_ref[s * seg_len : (s + 1) * seg_len, lanes].astype(F32)
            xs[c, s * pitch + 2 * HIST : (s + 1) * pitch + HIST, :] = rest

    def mask(i):
        m = keep[pl.ds(pl.multiple_of((i + 2) * SEGS, SEGS), SEGS), :]
        return jnp.concatenate([m] * (width // 128), 1)

    def row(i):
        return jnp.concatenate(
            [xs[c, pl.ds(2 * HIST + i, SEGS, stride=pitch), :] for c in range(width // 128)], 1
        )

    w = [jnp.broadcast_to(cw_ref[j : j + 1, :], (SEGS, width)) for j in range(CONV)]
    bias = jnp.broadcast_to(cb_ref[...], (SEGS, width))

    def conv_step(i, carry):
        a, b, c = carry
        x = row(i)
        m = mask(i)
        d = w[0] * x + m * c + bias
        c = w[1] * x + m * b
        b = w[2] * x + m * a
        a = w[3] * x
        return (a, b, c), d

    x3, x2, x1 = row(-3), row(-2), row(-1)
    a1 = w[3] * x1
    b1 = w[2] * x1 + mask(-1) * (w[3] * x2)
    c1 = w[1] * x1 + mask(-1) * (w[2] * x2 + mask(-2) * (w[3] * x3))

    def conv_pair(k, carry):
        carry, d0 = conv_step(2 * k, carry)
        carry, d1 = conv_step(2 * k + 1, carry)
        co[pl.ds(pl.multiple_of(k * 2 * SEGS, 2 * SEGS), 2 * SEGS), :] = jnp.concatenate([d0, d1], 0).astype(BF16)
        return carry

    lax.fori_loop(0, seg_len // 2, conv_pair, (a1, b1, c1), unroll=8)

    weight = dequantized(panel_ref[0], scale_ref[0]) * BF16(0.5)
    gate[...] = jnp.dot(co[...], weight, preferred_element_type=F32)

    bias_r = jnp.broadcast_to(gb_ref[0:1, :] * 0.5, (SEGS, width))
    bias_i = jnp.broadcast_to(gb_ref[1:2, :] * 0.5, (SEGS, width))
    rate4 = jnp.broadcast_to(rate_ref[...] * (-4.0 * LOG2E), (SEGS, width))

    def scan_step(i, conv, carry):
        h, p = carry
        at = pl.ds(pl.multiple_of(i * SEGS, SEGS), SEGS)
        m = mask(i)
        v = rate4 * (1.0 + jnp.tanh(gate[at, :width] + bias_r))
        ti = 1.0 + jnp.tanh(gate[at, width:] + bias_i)
        decay = jnp.exp2(v)
        s = v * v
        series = ((s * SINH[3] + SINH[2]) * s + SINH[1]) * s + SINH[0]
        quarter = decay * (v * series)
        half = quarter * lax.rsqrt(jnp.maximum(quarter, 1e-37))
        half = jnp.where(m > 0.0, half, 0.5)
        decay = decay * m
        h = decay * h + ti * (conv * half)
        p = p * decay
        for c in range(width // 128):
            h_ref[c, at, :] = h[:, c * 128 : (c + 1) * 128]
            p_ref[c, at, :] = p[:, c * 128 : (c + 1) * 128]
        return h, p

    def scan_pair(k, carry):
        conv = co[pl.ds(pl.multiple_of(k * 2 * SEGS, 2 * SEGS), 2 * SEGS), :].astype(F32)
        carry = scan_step(2 * k, conv[:SEGS], carry)
        return scan_step(2 * k + 1, conv[SEGS:], carry)

    h, p = lax.fori_loop(
        0,
        seg_len // 2,
        scan_pair,
        (jnp.zeros((SEGS, width), F32), jnp.ones((SEGS, width), F32)),
        unroll=8,
    )
    ends_ref[0] = p
    ends_ref[1] = h
    tp, th = p[0:1], h[0:1]
    for s in range(1, SEGS):
        th = p[s : s + 1] * th + h[s : s + 1]
        tp = tp * p[s : s + 1]
    tot_ref[0:1, :] = tp
    tot_ref[1:2, :] = th


def level_kernel(tot_ref, near_ref, level_ref):
    odd = lax.axis_index("tm") % 2 == 1
    tot, near = tot_ref[...], near_ref[...]
    lower = jnp.where(odd, near, tot)
    upper = jnp.where(odd, tot, near)
    level_ref[0:1, :] = lower[0:1] * upper[0:1]
    level_ref[1:2, :] = upper[0:1] * lower[1:2] + upper[1:2]


def mix_kernel(levels, h_ref, p_ref, ends_ref, *refs):
    near_ref, past, rest = refs[0], refs[1 : levels + 1], refs[levels + 1 :]
    y_ref, panel_ref, scale_ref, mixed_ref, kv_ref, carry = rest
    rows, width = y_ref.shape
    me = lax.axis_index("tm")
    seg_len = rows // SEGS

    @pl.when(pl.program_id(0) == 0)
    def _():
        kv_ref[...] = jnp.zeros_like(kv_ref)

    c = jnp.zeros((1, width), F32)
    for k in range(levels, 0, -1):
        c = jnp.where(me >= 2 * k, past[k - 1][0:1, :] * c + past[k - 1][1:2, :], 0.0)
    c = jnp.where(me % 2 == 1, near_ref[0:1, :] * c + near_ref[1:2, :], c)
    for s in range(SEGS):
        carry[s : s + 1, :] = c
        c = ends_ref[0, s : s + 1, :] * c + ends_ref[1, s : s + 1, :]
    groups = width // SCALE_ROWS
    table = scale_ref[...]
    index = lax.broadcasted_iota(jnp.int32, table.shape, 0) - pl.program_id(0) * groups
    scale = [jnp.sum(jnp.where(index == g, table, 0.0), axis=0, keepdims=True) for g in range(groups)]
    weight = dequantized(panel_ref[...], jnp.concatenate(scale, 0))

    def natural(ref, g, s):
        return jnp.concatenate(
            [ref[g, pl.ds(s + k * 8 * SEGS, 8, stride=SEGS), :] for k in range(seg_len // 8)], 0
        )

    for s in range(SEGS):
        at = slice(s * seg_len, (s + 1) * seg_len)
        y = y_ref[at, :].astype(F32)
        inner = y * (0.7978845608028654 + (0.7978845608028654 * 0.044715) * (y * y))
        gelu = (0.5 * y) * (1.0 + jnp.tanh(inner))
        local_h = jnp.concatenate([natural(h_ref, g, s) for g in range(width // 128)], 1)
        local_p = jnp.concatenate([natural(p_ref, g, s) for g in range(width // 128)], 1)
        mixed_ref[at, :] = ((local_h + local_p * carry[s : s + 1, :]) * gelu).astype(BF16)
    kv_ref[...] += jnp.dot(mixed_ref[...], weight, preferred_element_type=F32)


def sum_kernel(a_ref, b_ref, own_ref, half_ref):
    both = a_ref[...] + b_ref[...]
    n = both.shape[0] // 2
    core = lax.axis_index("mp")
    for side in range(2):
        keys = both[side * n : (side + 1) * n, :HD].T.astype(BF16)
        values = both[side * n : (side + 1) * n, HD:].astype(BF16)
        own_ref[side, :HD, :] = keys
        own_ref[side, HD:, :] = values
    half_ref[...] = own_ref[core]


def attend_kernel(own, lags, has_prev, final, starts_ref, q_ref, *refs):
    refs = list(refs)
    take = lambda n: [refs.pop(0) for _ in range(n)]
    own_ref = take(1)[0] if own else None
    pairs = [take(2) for _ in lags]
    prev_acc, prev_m, prev_l = take(3) if has_prev else (None, None, None)
    out = take(1) if final else take(3)
    low, score, top = take(3)
    acc, m_ref, l_ref = take(3) if final else out
    rows = q_ref.shape[0]
    half = rows // 2
    me = lax.axis_index("tm")
    first = me * rows
    core = lax.axis_index("mp")
    turn = 2 * (me % 2) - 1
    scale = LOG2E / math.sqrt(HD)

    def lowest(t):
        d0 = jnp.maximum(t - (WINDOW - 1), 0)
        for d in range(DOCS):
            d0 = jnp.maximum(d0, jnp.where(starts_ref[d] <= t, starts_ref[d], 0))
        return d0

    @pl.when(pl.program_id(0) == 0)
    def _():
        low[...] = lowest(first + lax.broadcasted_iota(jnp.int32, (rows, 128), 0))

    lo_first = lowest(first)
    lo_last = lowest(first + rows - 1)

    def keys_of(pair, t):
        return own_ref[t, :HD, :] if pair is None else pair[t][:HD, :]

    def values_of(pair, t):
        return own_ref[t, HD:, :] if pair is None else pair[t][HD:, :]

    def score_pass(j, pair, start, masked):
        for h in range(GROUP):
            for t in range(2):
                r0 = half * t if pair is None else 0
                at = slice(r0, rows)
                s = jnp.dot(
                    q_ref[at, h * HD : (h + 1) * HD], keys_of(pair, t), preferred_element_type=F32
                )
                peak = top[h, at, :]
                for c in range(half // 128):
                    part = s[:, c * 128 : (c + 1) * 128] * scale
                    if masked:
                        side = t if pair is None else jnp.where(core == t, 0, 1)
                        kpos = lax.broadcasted_iota(jnp.int32, part.shape, 1) + (start + side * half + c * 128)
                        ok = kpos >= low[at, :]
                        if pair is None:
                            ok = ok & (kpos <= lax.broadcasted_iota(jnp.int32, part.shape, 0) + (first + r0))
                        part = jnp.where(ok, part, -1e30)
                    score[j, h, t, at, c * 128 : (c + 1) * 128] = part
                    peak = jnp.maximum(peak, part)
                top[h, at, :] = peak

    def value_pass(j, pair):
        for h in range(GROUP):
            spans = [(0, half, 1), (half, rows, 2)] if pair is None else [(0, rows, 2)]
            for r0, r1, n in spans:
                at = slice(r0, r1)
                m = m_ref[at, h * 128 : (h + 1) * 128]
                total = l_ref[at, h * 128 : (h + 1) * 128]
                ps, vs = [], []
                for t in range(n):
                    for c in range(half // 128):
                        p = jnp.exp2(score[j, h, t, at, c * 128 : (c + 1) * 128] - m)
                        total = total + p
                        ps.append(p.astype(BF16))
                    vs.append(values_of(pair, t))
                l_ref[at, h * 128 : (h + 1) * 128] = total
                acc[at, h * HD : (h + 1) * HD] += jnp.dot(
                    jnp.concatenate(ps, 1), jnp.concatenate(vs, 0), preferred_element_type=F32
                )

    tiles = [(None, first)] if own else []
    for k, (even_part, odd_part) in enumerate(lags):
        tiles.append((pairs[k], first - (even_part + odd_part * turn) * rows))
    live = [True if pair is None else (start >= 0) & (start < first) & (start + rows > lo_first) for pair, start in tiles]

    top[...] = jnp.full(top.shape, -1e30, F32)
    for j, (pair, start) in enumerate(tiles):
        if pair is None:
            score_pass(j, pair, start, True)
            continue

        @pl.when(live[j] & (start >= lo_last))
        def _(j=j, pair=pair, start=start):
            score_pass(j, pair, start, False)

        @pl.when(live[j] & (start < lo_last))
        def _(j=j, pair=pair, start=start):
            score_pass(j, pair, start, True)

    for h in range(GROUP):
        lanes = slice(h * 128, (h + 1) * 128)
        wide = slice(h * HD, (h + 1) * HD)
        m = jnp.broadcast_to(jnp.max(top[h], axis=1, keepdims=True), (rows, 128))
        if has_prev:
            m0 = prev_m[:, lanes]
            m = jnp.maximum(m, m0)
            fade = jnp.exp2(m0 - m)
            l_ref[:, lanes] = prev_l[:, lanes] * fade
            acc[:, wide] = prev_acc[:, wide] * jnp.concatenate([fade] * (HD // 128), 1)
        else:
            l_ref[:, lanes] = jnp.zeros((rows, 128), F32)
            acc[:, wide] = jnp.zeros((rows, HD), F32)
        m_ref[:, lanes] = m
    for j, (pair, start) in enumerate(tiles):
        if pair is None:
            value_pass(j, pair)
            continue

        @pl.when(live[j])
        def _(j=j, pair=pair):
            value_pass(j, pair)

    if final:
        for h in range(GROUP):
            total = jnp.sum(l_ref[:, h * 128 : (h + 1) * 128], axis=1, keepdims=True)
            share = jnp.broadcast_to(1.0 / total, (rows, 128))
            wide = slice(h * HD, (h + 1) * HD)
            out[0][:, wide] = (acc[:, wide] * jnp.concatenate([share] * (HD // 128), 1)).astype(BF16)


def recur_call(starts, x, halo, conv_weight, conv_bias, gate_panel, gate_scale, gate_bias, decay_rate):
    rows, channels = x.shape
    blocks, width, _ = gate_panel.shape
    col = lambda b, s: (0, b)
    return pl.pallas_call(
        recur_kernel,
        grid_spec=pltpu.PrefetchScalarGridSpec(
            num_scalar_prefetch=1,
            grid=(blocks,),
            in_specs=[
                pl.BlockSpec((rows, width), col),
                pl.BlockSpec((CONV - 1, width), col),
                pl.BlockSpec((CONV, width), col),
                pl.BlockSpec((1, width), col),
                pl.BlockSpec((1, width, 2 * width), lambda b, s: (b, 0, 0)),
                pl.BlockSpec((1, width // SCALE_ROWS, 2 * width), lambda b, s: (b, 0, 0)),
                pl.BlockSpec((2, width), col),
                pl.BlockSpec((1, width), col),
            ],
            out_specs=[
                pl.BlockSpec((width // 128, rows, 128), lambda b, s: (b, 0, 0)),
                pl.BlockSpec((width // 128, rows, 128), lambda b, s: (b, 0, 0)),
                pl.BlockSpec((2, SEGS, width), lambda b, s: (0, 0, b)),
                pl.BlockSpec((2, width), col),
            ],
            scratch_shapes=[
                pltpu.VMEM((rows + 2 * SEGS, 128), F32),
                pltpu.VMEM((width // 128, rows + HIST * (SEGS + 1), 128), F32),
                pltpu.VMEM((rows, width), BF16),
                pltpu.VMEM((rows, 2 * width), F32),
            ],
        ),
        out_shape=[
            jax.ShapeDtypeStruct((channels // 128, rows, 128), F32),
            jax.ShapeDtypeStruct((channels // 128, rows, 128), F32),
            jax.ShapeDtypeStruct((2, SEGS, channels), F32),
            jax.ShapeDtypeStruct((2, channels), F32),
        ],
        compiler_params=pltpu.CompilerParams(vmem_limit_bytes=20 << 20),
        name="recur",
    )(starts, x, halo, conv_weight, conv_bias, gate_panel, gate_scale, gate_bias, decay_rate)


def level_call(tot, near):
    return pl.pallas_call(
        level_kernel,
        out_shape=jax.ShapeDtypeStruct(tot.shape, F32),
        compiler_params=pltpu.CompilerParams(vmem_limit_bytes=1 << 20),
        name="level",
    )(tot, near)


def mix_call(h, p, ends, near, past, y, kv_panel, kv_scale):
    rows, channels = y.shape
    width = MIX_GROUPS * SCALE_ROWS
    col = lambda b: (0, b)
    out = kv_panel.shape[1]
    pair = pl.BlockSpec((2, width), col)
    return pl.pallas_call(
        functools.partial(mix_kernel, len(past)),
        grid=(channels // width,),
        in_specs=[
            pl.BlockSpec((width // 128, rows, 128), lambda b: (b, 0, 0)),
            pl.BlockSpec((width // 128, rows, 128), lambda b: (b, 0, 0)),
            pl.BlockSpec((2, SEGS, width), lambda b: (0, 0, b)),
        ]
        + [pair] * (1 + len(past))
        + [
            pl.BlockSpec((rows, width), col),
            pl.BlockSpec((width, out), lambda b: (b, 0)),
            pl.BlockSpec(kv_scale.shape, lambda b: (0, 0)),
        ],
        out_specs=[pl.BlockSpec((rows, width), col), pl.BlockSpec((rows, out), lambda b: (0, 0))],
        out_shape=[jax.ShapeDtypeStruct((rows, channels), BF16), jax.ShapeDtypeStruct((rows, out), F32)],
        scratch_shapes=[pltpu.VMEM((SEGS, width), F32)],
        compiler_params=pltpu.CompilerParams(vmem_limit_bytes=20 << 20),
        name="mix",
    )(h, p, ends, near, *past, y, kv_panel, kv_scale)


def sum_call(a, b):
    rows, _ = a.shape
    half = rows // 2
    return pl.pallas_call(
        sum_kernel,
        out_shape=[
            jax.ShapeDtypeStruct((2, 2 * HD, half), BF16),
            jax.ShapeDtypeStruct((2 * HD, half), BF16),
        ],
        compiler_params=pltpu.CompilerParams(vmem_limit_bytes=16 << 20),
        name="kvsum",
    )(a, b)


def attend_call(starts, q, own, halves, lags, prev, final):
    rows, width = q.shape
    heads = width // HD
    whole = lambda a: pl.BlockSpec(a.shape, lambda h, s: (0,) * a.ndim)
    per_head = lambda h, s: (0, h)
    held = [] if own is None else [own]
    held += halves
    carried = [pl.BlockSpec((rows, GROUP * n), per_head) for n in (HD, 128, 128)]
    tiles = len(lags) + (own is not None)
    if final:
        out_specs = pl.BlockSpec((rows, GROUP * HD), per_head)
        out_shape = jax.ShapeDtypeStruct((rows, width), BF16)
        extra = [pltpu.VMEM((rows, GROUP * n), F32) for n in (HD, 128, 128)]
    else:
        out_specs = carried
        out_shape = [jax.ShapeDtypeStruct((rows, heads * n), F32) for n in (HD, 128, 128)]
        extra = []
    return pl.pallas_call(
        functools.partial(attend_kernel, own is not None, lags, prev is not None, final),
        grid_spec=pltpu.PrefetchScalarGridSpec(
            num_scalar_prefetch=1,
            grid=(heads // GROUP,),
            in_specs=[pl.BlockSpec((rows, GROUP * HD), per_head)]
            + [whole(a) for a in held]
            + (carried if prev is not None else []),
            out_specs=out_specs,
            scratch_shapes=[
                pltpu.VMEM((rows, 128), jnp.int32),
                pltpu.VMEM((tiles, GROUP, 2, rows, rows // 2), F32),
                pltpu.VMEM((GROUP, rows, 128), F32),
            ]
            + extra,
        ),
        out_shape=out_shape,
        cost_estimate=pl.CostEstimate(
            flops=4 * tiles * rows * rows * width,
            bytes_accessed=4 * rows * width,
            transcendentals=tiles * rows * rows * heads,
        ),
        compiler_params=pltpu.CompilerParams(vmem_limit_bytes=32 << 20),
        name="attend_own" if own is not None else "attend_end" if final else "attend_mid",
    )(starts, q, *held, *(prev or []))


def local(
    branch_x,
    branch_y,
    queries,
    conv_weight,
    conv_bias,
    gate_panel,
    gate_scale,
    gate_bias,
    decay_rate,
    kv_panel,
    kv_scale,
    segment_ids,
):
    rows = branch_x.shape[0]
    seq = segment_ids.shape[0]
    halo = ring(branch_x[rows - CONV + 1 :], 1)
    starts = jnp.sum(
        (segment_ids[None, :] < jnp.arange(DOCS, dtype=jnp.int32)[:, None]).astype(jnp.int32), axis=1
    )
    stay = lambda a: pltpu.with_memory_space_constraint(a, pltpu.HBM)
    h, p, ends, tot = recur_call(
        starts,
        stay(branch_x),
        halo,
        stay(conv_weight),
        stay(conv_bias[None]),
        stay(gate_panel),
        stay(gate_scale),
        stay(gate_bias),
        stay(decay_rate[None]),
    )
    near = swap(tot)
    level = level_call(tot, near)
    levels = -(-(seq // 2) // (2 * rows))
    past = [ring(level, 2 * k) for k in range(1, levels + 1)]
    mixed, partial_kv = mix_call(h, p, ends, near, past, branch_y, kv_panel, kv_scale)
    own, half = sum_call(partial_kv, partner(partial_kv))

    levels = -(-WINDOW // rows) // 2
    straight, attended = half, None
    for k in range(levels + 1):
        last = k == levels
        beyond = None if last else ring(straight, 2)
        crossed = swap(straight)
        if k == 0:
            attended = attend_call(starts, queries, own, [], [], None, False)
        else:
            attended = attend_call(starts, queries, None, tiles, lags, attended, False)
        tiles, lags = [crossed, partner(crossed)], [(2 * k, 1)]
        if not last:
            tiles += [beyond, partner(beyond)]
            lags.append((2 * k + 2, 0))
        straight = beyond
    attended = attend_call(starts, queries, None, tiles, lags, attended, True)
    return mixed, attended


def solution(mesh):
    in_specs = (
        P(("groups", "tm"), "mp"),
        P(("groups", "tm"), "mp"),
        P(("groups", "tm"), "mp"),
        P(None, "mp"),
        P("mp"),
        P("mp", None, None),
        P("mp", None, None),
        P(None, "mp"),
        P("mp"),
        P("mp", None),
        P("mp", None),
        P("groups"),
    )
    out_specs = (P(("groups", "tm"), "mp"), P(("groups", "tm"), "mp"))
    return jax.shard_map(local, mesh=mesh, in_specs=in_specs, out_specs=out_specs, check_vma=False)
```

```python
import functools
import math

import jax
import jax.numpy as jnp
from jax import lax
from jax.experimental import pallas as pl
from jax.experimental.pallas import tpu as pltpu
from jax.sharding import PartitionSpec as P


HD = 256
CONV = 4
WINDOW = 2048
SCALE_ROWS = 128
DOCS = 4
SEGS = 8
MIX_GROUPS = 4
GROUP = 2
HIST = 4
LOG2E = 1.4426950408889634
LN2 = 0.6931471805599453
SINH = [-0.5 * LN2 ** (2 * k + 1) / math.factorial(2 * k + 1) for k in range(4)]
F32 = jnp.float32
BF16 = jnp.bfloat16


def ring(x, lag):
    n = lax.axis_size("tm")
    return lax.ppermute(x, "tm", [(i, (i + lag) % n) for i in range(n)])


def swap(x):
    n = lax.axis_size("tm")
    return lax.ppermute(x, "tm", [(i, i ^ 1) for i in range(n)])


def partner(x):
    return lax.ppermute(x, "mp", [(0, 1), (1, 0)])


def dequantized(panel, scale):
    rows = panel.shape[0]
    parts = []
    for g in range(rows // SCALE_ROWS):
        part = panel[g * SCALE_ROWS : (g + 1) * SCALE_ROWS, :].astype(F32)
        parts.append((part * scale[g : g + 1, :]).astype(BF16))
    return jnp.concatenate(parts, 0)


def recur_kernel(
    starts_ref,
    x_ref,
    halo_ref,
    cw_ref,
    cb_ref,
    panel_ref,
    scale_ref,
    gb_ref,
    rate_ref,
    h_ref,
    p_ref,
    ends_ref,
    tot_ref,
    keep,
    xs,
    co,
    gate,
):
    rows, width = x_ref.shape
    seg_len = rows // SEGS
    base = lax.axis_index("tm") * rows

    @pl.when(pl.program_id(0) == 0)
    def _():
        def fill(i, carry):
            pos = base + i - 2 + seg_len * lax.broadcasted_iota(jnp.int32, (SEGS, 128), 0)
            hit = pos == starts_ref[0]
            for d in range(1, DOCS):
                hit = hit | (pos == starts_ref[d])
            keep[pl.ds(pl.multiple_of(i * SEGS, SEGS), SEGS), :] = jnp.where(hit, 0.0, 1.0)
            return carry

        lax.fori_loop(0, seg_len + 2, fill, 0)

    pitch = seg_len + HIST
    for c in range(width // 128):
        lanes = slice(c * 128, (c + 1) * 128)
        xs[c, HIST + 1 : 2 * HIST, :] = halo_ref[:, lanes].astype(F32)
        for s in range(1, SEGS):
            past = x_ref[s * seg_len - 2 * HIST : s * seg_len, lanes].astype(F32)
            xs[c, s * pitch : s * pitch + 2 * HIST, :] = past
        for s in range(SEGS):
            rest = x_ref[s * seg_len : (s + 1) * seg_len, lanes].astype(F32)
            xs[c, s * pitch + 2 * HIST : (s + 1) * pitch + HIST, :] = rest

    def mask(i):
        m = keep[pl.ds(pl.multiple_of((i + 2) * SEGS, SEGS), SEGS), :]
        return jnp.concatenate([m] * (width // 128), 1)

    def row(i):
        return jnp.concatenate(
            [xs[c, pl.ds(2 * HIST + i, SEGS, stride=pitch), :] for c in range(width // 128)], 1
        )

    w = [jnp.broadcast_to(cw_ref[j : j + 1, :], (SEGS, width)) for j in range(CONV)]
    bias = jnp.broadcast_to(cb_ref[...], (SEGS, width))

    def conv_step(i, carry):
        a, b, c = carry
        x = row(i)
        m = mask(i)
        d = w[0] * x + m * c + bias
        c = w[1] * x + m * b
        b = w[2] * x + m * a
        a = w[3] * x
        return (a, b, c), d

    x3, x2, x1 = row(-3), row(-2), row(-1)
    a1 = w[3] * x1
    b1 = w[2] * x1 + mask(-1) * (w[3] * x2)
    c1 = w[1] * x1 + mask(-1) * (w[2] * x2 + mask(-2) * (w[3] * x3))

    def conv_pair(k, carry):
        carry, d0 = conv_step(2 * k, carry)
        carry, d1 = conv_step(2 * k + 1, carry)
        co[pl.ds(pl.multiple_of(k * 2 * SEGS, 2 * SEGS), 2 * SEGS), :] = jnp.concatenate([d0, d1], 0).astype(BF16)
        return carry

    lax.fori_loop(0, seg_len // 2, conv_pair, (a1, b1, c1), unroll=8)

    weight = dequantized(panel_ref[0], scale_ref[0]) * BF16(0.5)
    gate[...] = jnp.dot(co[...], weight, preferred_element_type=F32)

    bias_r = jnp.broadcast_to(gb_ref[0:1, :] * 0.5, (SEGS, width))
    bias_i = jnp.broadcast_to(gb_ref[1:2, :] * 0.5, (SEGS, width))
    rate4 = jnp.broadcast_to(rate_ref[...] * (-4.0 * LOG2E), (SEGS, width))

    def scan_step(i, conv, carry):
        h, p = carry
        at = pl.ds(pl.multiple_of(i * SEGS, SEGS), SEGS)
        m = mask(i)
        v = rate4 * (1.0 + jnp.tanh(gate[at, :width] + bias_r))
        ti = 1.0 + jnp.tanh(gate[at, width:] + bias_i)
        decay = jnp.exp2(v)
        s = v * v
        series = ((s * SINH[3] + SINH[2]) * s + SINH[1]) * s + SINH[0]
        quarter = decay * (v * series)
        half = quarter * lax.rsqrt(jnp.maximum(quarter, 1e-37))
        half = jnp.where(m > 0.0, half, 0.5)
        decay = decay * m
        h = decay * h + ti * (conv * half)
        p = p * decay
        for c in range(width // 128):
            h_ref[c, at, :] = h[:, c * 128 : (c + 1) * 128]
            p_ref[c, at, :] = p[:, c * 128 : (c + 1) * 128]
        return h, p

    def scan_pair(k, carry):
        conv = co[pl.ds(pl.multiple_of(k * 2 * SEGS, 2 * SEGS), 2 * SEGS), :].astype(F32)
        carry = scan_step(2 * k, conv[:SEGS], carry)
        return scan_step(2 * k + 1, conv[SEGS:], carry)

    h, p = lax.fori_loop(
        0,
        seg_len // 2,
        scan_pair,
        (jnp.zeros((SEGS, width), F32), jnp.ones((SEGS, width), F32)),
        unroll=8,
    )
    ends_ref[0] = p
    ends_ref[1] = h
    tp, th = p[0:1], h[0:1]
    for s in range(1, SEGS):
        th = p[s : s + 1] * th + h[s : s + 1]
        tp = tp * p[s : s + 1]
    tot_ref[0:1, :] = tp
    tot_ref[1:2, :] = th


def level_kernel(tot_ref, near_ref, level_ref):
    odd = lax.axis_index("tm") % 2 == 1
    tot, near = tot_ref[...], near_ref[...]
    lower = jnp.where(odd, near, tot)
    upper = jnp.where(odd, tot, near)
    level_ref[0:1, :] = lower[0:1] * upper[0:1]
    level_ref[1:2, :] = upper[0:1] * lower[1:2] + upper[1:2]


def mix_kernel(levels, h_ref, p_ref, ends_ref, *refs):
    near_ref, past, rest = refs[0], refs[1 : levels + 1], refs[levels + 1 :]
    y_ref, panel_ref, scale_ref, mixed_ref, kv_ref, carry = rest
    rows, width = y_ref.shape
    me = lax.axis_index("tm")
    seg_len = rows // SEGS

    @pl.when(pl.program_id(0) == 0)
    def _():
        kv_ref[...] = jnp.zeros_like(kv_ref)

    c = jnp.zeros((1, width), F32)
    for k in range(levels, 0, -1):
        c = jnp.where(me >= 2 * k, past[k - 1][0:1, :] * c + past[k - 1][1:2, :], 0.0)
    c = jnp.where(me % 2 == 1, near_ref[0:1, :] * c + near_ref[1:2, :], c)
    for s in range(SEGS):
        carry[s : s + 1, :] = c
        c = ends_ref[0, s : s + 1, :] * c + ends_ref[1, s : s + 1, :]
    groups = width // SCALE_ROWS
    table = scale_ref[...]
    index = lax.broadcasted_iota(jnp.int32, table.shape, 0) - pl.program_id(0) * groups
    scale = [jnp.sum(jnp.where(index == g, table, 0.0), axis=0, keepdims=True) for g in range(groups)]
    weight = dequantized(panel_ref[...], jnp.concatenate(scale, 0))

    def natural(ref, g, s):
        return jnp.concatenate(
            [ref[g, pl.ds(s + k * 8 * SEGS, 8, stride=SEGS), :] for k in range(seg_len // 8)], 0
        )

    for s in range(SEGS):
        at = slice(s * seg_len, (s + 1) * seg_len)
        y = y_ref[at, :].astype(F32)
        inner = y * (0.7978845608028654 + (0.7978845608028654 * 0.044715) * (y * y))
        gelu = (0.5 * y) * (1.0 + jnp.tanh(inner))
        local_h = jnp.concatenate([natural(h_ref, g, s) for g in range(width // 128)], 1)
        local_p = jnp.concatenate([natural(p_ref, g, s) for g in range(width // 128)], 1)
        mixed_ref[at, :] = ((local_h + local_p * carry[s : s + 1, :]) * gelu).astype(BF16)
    kv_ref[...] += jnp.dot(mixed_ref[...], weight, preferred_element_type=F32)


def sum_kernel(a_ref, b_ref, own_ref, half_ref):
    both = a_ref[...] + b_ref[...]
    n = both.shape[0] // 2
    core = lax.axis_index("mp")
    for side in range(2):
        keys = both[side * n : (side + 1) * n, :HD].T.astype(BF16)
        values = both[side * n : (side + 1) * n, HD:].astype(BF16)
        own_ref[side, :HD, :] = keys
        own_ref[side, HD:, :] = values
    half_ref[...] = own_ref[core]


def attend_kernel(own, lags, final, heads, starts_ref, q_ref, *refs):
    refs = list(refs)
    take = lambda n: [refs.pop(0) for _ in range(n)]
    own_ref = take(1)[0] if own else None
    pairs = [take(2) for _ in lags]
    prev = None if own else take(3)
    out = take(1)[0] if final else None
    acc, m_ref, l_ref = (None, None, None) if final else take(3)
    low, score, top = take(3)
    if final:
        acc, m_ref, l_ref, stage, sems = take(5)
    rows = q_ref.shape[0]
    half = rows // 2
    me = lax.axis_index("tm")
    first = me * rows
    core = lax.axis_index("mp")
    turn = 2 * (me % 2) - 1
    scale = LOG2E / math.sqrt(HD)

    def lowest(t):
        d0 = jnp.maximum(t - (WINDOW - 1), 0)
        for d in range(DOCS):
            d0 = jnp.maximum(d0, jnp.where(starts_ref[d] <= t, starts_ref[d], 0))
        return d0

    lo_first = lowest(first)
    lo_last = lowest(first + rows - 1)
    tiles = [(None, first)] if own else []
    for k, (even_part, odd_part) in enumerate(lags):
        tiles.append((pairs[k], first - (even_part + odd_part * turn) * rows))
    live = [None if pair is None else (start >= 0) & (start < first) & (start + rows > lo_first) for pair, start in tiles]

    def keys_of(pair, t):
        return own_ref[t, :HD, :] if pair is None else pair[t][:HD, :]

    def values_of(pair, t):
        return own_ref[t, HD:, :] if pair is None else pair[t][HD:, :]

    def lanes(g, h, n):
        return pl.ds(pl.multiple_of((g * GROUP + h) * n, n), n)

    def kept(g, h, n):
        return slice(h * n, (h + 1) * n) if final else lanes(g, h, n)

    def score_pass(g, j, pair, start, masked):
        for h in range(GROUP):
            for t in range(2):
                r0 = half * t if pair is None else 0
                at = slice(r0, rows)
                s = jnp.dot(q_ref[at, lanes(g, h, HD)], keys_of(pair, t), preferred_element_type=F32)
                peak = top[h, at, :]
                for c in range(half // 128):
                    part = s[:, c * 128 : (c + 1) * 128] * scale
                    if masked:
                        side = t if pair is None else jnp.where(core == t, 0, 1)
                        kpos = lax.broadcasted_iota(jnp.int32, part.shape, 1) + (start + side * half + c * 128)
                        ok = kpos >= low[at, :]
                        if pair is None:
                            ok = ok & (kpos <= lax.broadcasted_iota(jnp.int32, part.shape, 0) + (first + r0))
                        part = jnp.where(ok, part, -1e30)
                    score[j, h, t, at, c * 128 : (c + 1) * 128] = part
                    peak = jnp.maximum(peak, part)
                top[h, at, :] = peak

    def value_pass(g, j, pair):
        for h in range(GROUP):
            spans = [(0, half, 1), (half, rows, 2)] if pair is None else [(0, rows, 2)]
            for r0, r1, n in spans:
                at = slice(r0, r1)
                m = m_ref[at, kept(g, h, 128)]
                total = l_ref[at, kept(g, h, 128)]
                ps, vs = [], []
                for t in range(n):
                    for c in range(half // 128):
                        p = jnp.exp2(score[j, h, t, at, c * 128 : (c + 1) * 128] - m)
                        total = total + p
                        ps.append(p.astype(BF16))
                    vs.append(values_of(pair, t))
                l_ref[at, kept(g, h, 128)] = total
                acc[at, kept(g, h, HD)] += jnp.dot(
                    jnp.concatenate(ps, 1), jnp.concatenate(vs, 0), preferred_element_type=F32
                )

    def spread(x):
        return jnp.concatenate([x] * (HD // 128), 1)

    def update(g):
        top[...] = jnp.full(top.shape, -1e30, F32)
        for j, (pair, start) in enumerate(tiles):
            if pair is None:
                score_pass(g, j, pair, start, True)
                continue

            @pl.when(live[j] & (start >= lo_last))
            def _(j=j, pair=pair, start=start):
                score_pass(g, j, pair, start, False)

            @pl.when(live[j] & (start < lo_last))
            def _(j=j, pair=pair, start=start):
                score_pass(g, j, pair, start, True)

        for h in range(GROUP):
            m = jnp.broadcast_to(jnp.max(top[h], axis=1, keepdims=True), (rows, 128))
            if own:
                l_ref[:, kept(g, h, 128)] = jnp.zeros((rows, 128), F32)
                acc[:, kept(g, h, HD)] = jnp.zeros((rows, HD), F32)
            else:
                m0 = prev[1][:, lanes(g, h, 128)]
                m = jnp.maximum(m, m0)
                fade = jnp.exp2(m0 - m)
                l_ref[:, kept(g, h, 128)] = prev[2][:, lanes(g, h, 128)] * fade
                acc[:, kept(g, h, HD)] = prev[0][:, lanes(g, h, HD)] * spread(fade)
            m_ref[:, kept(g, h, 128)] = m
        for j, (pair, start) in enumerate(tiles):
            if pair is None:
                value_pass(g, j, pair)
                continue

            @pl.when(live[j])
            def _(j=j, pair=pair):
                value_pass(g, j, pair)

    any_live = None if own else functools.reduce(jnp.logical_or, live)

    def loop(fn):
        def body(g, z):
            fn(g)
            return z

        lax.fori_loop(0, heads // GROUP, body, 0)

    def start_up():
        low[...] = lowest(first + lax.broadcasted_iota(jnp.int32, (rows, 128), 0))

    if own:
        start_up()
        loop(update)
        return
    if not final:

        @pl.when(any_live)
        def _():
            start_up()
            loop(update)

        return

    pl.when(any_live)(start_up)

    def outgoing(g):
        wide = pl.ds(pl.multiple_of(g * GROUP * HD, GROUP * HD), GROUP * HD)
        return pltpu.make_async_copy(stage.at[g], out.at[:, wide], sems.at[g])

    def finish(g):
        pl.when(any_live)(lambda: update(g))

        @pl.when(jnp.logical_not(any_live))
        def _():
            for h in range(GROUP):
                l_ref[:, kept(g, h, 128)] = prev[2][:, lanes(g, h, 128)]
                acc[:, kept(g, h, HD)] = prev[0][:, lanes(g, h, HD)]

        for h in range(GROUP):
            total = jnp.sum(l_ref[:, kept(g, h, 128)], axis=1, keepdims=True)
            share = jnp.broadcast_to(1.0 / total, (rows, 128))
            stage[g, :, h * HD : (h + 1) * HD] = (acc[:, kept(g, h, HD)] * spread(share)).astype(BF16)
        outgoing(g).start()

    loop(finish)
    loop(lambda g: outgoing(g).wait())


def recur_call(starts, x, halo, conv_weight, conv_bias, gate_panel, gate_scale, gate_bias, decay_rate):
    rows, channels = x.shape
    blocks, width, _ = gate_panel.shape
    col = lambda b, s: (0, b)
    return pl.pallas_call(
        recur_kernel,
        grid_spec=pltpu.PrefetchScalarGridSpec(
            num_scalar_prefetch=1,
            grid=(blocks,),
            in_specs=[
                pl.BlockSpec((rows, width), col),
                pl.BlockSpec((CONV - 1, width), col),
                pl.BlockSpec((CONV, width), col),
                pl.BlockSpec((1, width), col),
                pl.BlockSpec((1, width, 2 * width), lambda b, s: (b, 0, 0)),
                pl.BlockSpec((1, width // SCALE_ROWS, 2 * width), lambda b, s: (b, 0, 0)),
                pl.BlockSpec((2, width), col),
                pl.BlockSpec((1, width), col),
            ],
            out_specs=[
                pl.BlockSpec((width // 128, rows, 128), lambda b, s: (b, 0, 0)),
                pl.BlockSpec((width // 128, rows, 128), lambda b, s: (b, 0, 0)),
                pl.BlockSpec((2, SEGS, width), lambda b, s: (0, 0, b)),
                pl.BlockSpec((2, width), col),
            ],
            scratch_shapes=[
                pltpu.VMEM((rows + 2 * SEGS, 128), F32),
                pltpu.VMEM((width // 128, rows + HIST * (SEGS + 1), 128), F32),
                pltpu.VMEM((rows, width), BF16),
                pltpu.VMEM((rows, 2 * width), F32),
            ],
        ),
        out_shape=[
            jax.ShapeDtypeStruct((channels // 128, rows, 128), F32),
            jax.ShapeDtypeStruct((channels // 128, rows, 128), F32),
            jax.ShapeDtypeStruct((2, SEGS, channels), F32),
            jax.ShapeDtypeStruct((2, channels), F32),
        ],
        compiler_params=pltpu.CompilerParams(vmem_limit_bytes=20 << 20),
        name="recur",
    )(starts, x, halo, conv_weight, conv_bias, gate_panel, gate_scale, gate_bias, decay_rate)


def level_call(tot, near):
    return pl.pallas_call(
        level_kernel,
        out_shape=jax.ShapeDtypeStruct(tot.shape, F32),
        compiler_params=pltpu.CompilerParams(vmem_limit_bytes=1 << 20),
        name="level",
    )(tot, near)


def mix_call(h, p, ends, near, past, y, kv_panel, kv_scale):
    rows, channels = y.shape
    width = MIX_GROUPS * SCALE_ROWS
    col = lambda b: (0, b)
    out = kv_panel.shape[1]
    pair = pl.BlockSpec((2, width), col)
    return pl.pallas_call(
        functools.partial(mix_kernel, len(past)),
        grid=(channels // width,),
        in_specs=[
            pl.BlockSpec((width // 128, rows, 128), lambda b: (b, 0, 0)),
            pl.BlockSpec((width // 128, rows, 128), lambda b: (b, 0, 0)),
            pl.BlockSpec((2, SEGS, width), lambda b: (0, 0, b)),
        ]
        + [pair] * (1 + len(past))
        + [
            pl.BlockSpec((rows, width), col),
            pl.BlockSpec((width, out), lambda b: (b, 0)),
            pl.BlockSpec(kv_scale.shape, lambda b: (0, 0)),
        ],
        out_specs=[pl.BlockSpec((rows, width), col), pl.BlockSpec((rows, out), lambda b: (0, 0))],
        out_shape=[jax.ShapeDtypeStruct((rows, channels), BF16), jax.ShapeDtypeStruct((rows, out), F32)],
        scratch_shapes=[pltpu.VMEM((SEGS, width), F32)],
        compiler_params=pltpu.CompilerParams(vmem_limit_bytes=20 << 20),
        name="mix",
    )(h, p, ends, near, *past, y, kv_panel, kv_scale)


def sum_call(a, b):
    rows, _ = a.shape
    half = rows // 2
    return pl.pallas_call(
        sum_kernel,
        out_shape=[
            jax.ShapeDtypeStruct((2, 2 * HD, half), BF16),
            jax.ShapeDtypeStruct((2 * HD, half), BF16),
        ],
        compiler_params=pltpu.CompilerParams(vmem_limit_bytes=16 << 20),
        name="kvsum",
    )(a, b)


def attend_call(starts, q, own, halves, lags, prev, final):
    rows, width = q.shape
    heads = width // HD
    held = [] if own is None else [own]
    held += halves
    held += prev or []
    tiles = len(lags) + (own is not None)
    vmem = pl.BlockSpec(memory_space=pltpu.VMEM)
    scratch = [
        pltpu.VMEM((rows, 128), jnp.int32),
        pltpu.VMEM((tiles, GROUP, 2, rows, rows // 2), F32),
        pltpu.VMEM((GROUP, rows, 128), F32),
    ]
    aliases = {}
    if final:
        out_specs = pl.BlockSpec(memory_space=pl.ANY)
        out_shape = jax.ShapeDtypeStruct((rows, width), BF16)
        scratch += [pltpu.VMEM((rows, GROUP * n), F32) for n in (HD, 128, 128)]
        scratch += [pltpu.VMEM((heads // GROUP, rows, GROUP * HD), BF16), pltpu.SemaphoreType.DMA((heads // GROUP,))]
    else:
        out_specs = [vmem] * 3
        out_shape = [jax.ShapeDtypeStruct((rows, heads * n), F32) for n in (HD, 128, 128)]
        if prev:
            aliases = {2 + len(halves) + k: k for k in range(3)}
    return pl.pallas_call(
        functools.partial(attend_kernel, own is not None, lags, final, heads),
        in_specs=[pl.BlockSpec(memory_space=pltpu.SMEM), vmem] + [vmem] * len(held),
        out_specs=out_specs,
        scratch_shapes=scratch,
        out_shape=out_shape,
        input_output_aliases=aliases,
        cost_estimate=pl.CostEstimate(
            flops=4 * tiles * rows * rows * width,
            bytes_accessed=4 * rows * width,
            transcendentals=tiles * rows * rows * heads,
        ),
        compiler_params=pltpu.CompilerParams(vmem_limit_bytes=32 << 20),
        name="attend_own" if own is not None else "attend_end" if final else "attend_mid",
    )(starts, q, *held)


def local(
    branch_x,
    branch_y,
    queries,
    conv_weight,
    conv_bias,
    gate_panel,
    gate_scale,
    gate_bias,
    decay_rate,
    kv_panel,
    kv_scale,
    segment_ids,
):
    rows = branch_x.shape[0]
    seq = segment_ids.shape[0]
    halo = ring(branch_x[rows - CONV + 1 :], 1)
    starts = jnp.sum(
        (segment_ids[None, :] < jnp.arange(DOCS, dtype=jnp.int32)[:, None]).astype(jnp.int32), axis=1
    )
    stay = lambda a: pltpu.with_memory_space_constraint(a, pltpu.HBM)
    h, p, ends, tot = recur_call(
        starts,
        stay(branch_x),
        halo,
        stay(conv_weight),
        stay(conv_bias[None]),
        stay(gate_panel),
        stay(gate_scale),
        stay(gate_bias),
        stay(decay_rate[None]),
    )
    near = swap(tot)
    level = level_call(tot, near)
    levels = -(-(seq // 2) // (2 * rows))
    past = [ring(level, 2 * k) for k in range(1, levels + 1)]
    mixed, partial_kv = mix_call(h, p, ends, near, past, branch_y, kv_panel, kv_scale)
    own, half = sum_call(partial_kv, partner(partial_kv))

    levels = -(-WINDOW // rows) // 2
    straight, attended = half, None
    for k in range(levels + 1):
        last = k == levels
        beyond = None if last else ring(straight, 2)
        crossed = swap(straight)
        if k == 0:
            attended = attend_call(starts, queries, own, [], [], None, False)
        else:
            attended = attend_call(starts, queries, None, tiles, lags, attended, False)
        tiles, lags = [crossed, partner(crossed)], [(2 * k, 1)]
        if not last:
            tiles += [beyond, partner(beyond)]
            lags.append((2 * k + 2, 0))
        straight = beyond
    attended = attend_call(starts, queries, None, tiles, lags, attended, True)
    return mixed, attended


def solution(mesh):
    in_specs = (
        P(("groups", "tm"), "mp"),
        P(("groups", "tm"), "mp"),
        P(("groups", "tm"), "mp"),
        P(None, "mp"),
        P("mp"),
        P("mp", None, None),
        P("mp", None, None),
        P(None, "mp"),
        P("mp"),
        P("mp", None),
        P("mp", None),
        P("groups"),
    )
    out_specs = (P(("groups", "tm"), "mp"), P(("groups", "tm"), "mp"))
    return jax.shard_map(local, mesh=mesh, in_specs=in_specs, out_specs=out_specs, check_vma=False)
```

```python
import functools
import math

import jax
import jax.numpy as jnp
from jax import lax
from jax.experimental import pallas as pl
from jax.experimental.pallas import tpu as pltpu
from jax.sharding import PartitionSpec as P


HD = 256
CONV = 4
WINDOW = 2048
SCALE_ROWS = 128
DOCS = 4
SEGS = 8
MIX_GROUPS = 4
GROUP = 2
HIST = 4
LOG2E = 1.4426950408889634
LN2 = 0.6931471805599453
SINH = [-0.5 * LN2 ** (2 * k + 1) / math.factorial(2 * k + 1) for k in range(4)]
F32 = jnp.float32
BF16 = jnp.bfloat16


def ring(x, lag):
    n = lax.axis_size("tm")
    return lax.ppermute(x, "tm", [(i, (i + lag) % n) for i in range(n)])


def swap(x):
    n = lax.axis_size("tm")
    return lax.ppermute(x, "tm", [(i, i ^ 1) for i in range(n)])


def partner(x):
    return lax.ppermute(x, "mp", [(0, 1), (1, 0)])


def dequantized(panel, scale):
    rows = panel.shape[0]
    parts = []
    for g in range(rows // SCALE_ROWS):
        part = panel[g * SCALE_ROWS : (g + 1) * SCALE_ROWS, :].astype(F32)
        parts.append((part * scale[g : g + 1, :]).astype(BF16))
    return jnp.concatenate(parts, 0)


def recur_kernel(
    starts_ref,
    x_ref,
    halo_ref,
    cw_ref,
    cb_ref,
    panel_ref,
    scale_ref,
    gb_ref,
    rate_ref,
    h_ref,
    p_ref,
    ends_ref,
    tot_ref,
    keep,
    xs,
    co,
    gate,
):
    rows, width = x_ref.shape
    seg_len = rows // SEGS
    base = lax.axis_index("tm") * rows

    @pl.when(pl.program_id(0) == 0)
    def _():
        def fill(i, carry):
            pos = base + i - 2 + seg_len * lax.broadcasted_iota(jnp.int32, (SEGS, 128), 0)
            hit = pos == starts_ref[0]
            for d in range(1, DOCS):
                hit = hit | (pos == starts_ref[d])
            keep[pl.ds(pl.multiple_of(i * SEGS, SEGS), SEGS), :] = jnp.where(hit, 0.0, 1.0)
            return carry

        lax.fori_loop(0, seg_len + 2, fill, 0)

    pitch = seg_len + HIST
    for c in range(width // 128):
        lanes = slice(c * 128, (c + 1) * 128)
        xs[c, HIST + 1 : 2 * HIST, :] = halo_ref[:, lanes].astype(F32)
        for s in range(1, SEGS):
            past = x_ref[s * seg_len - 2 * HIST : s * seg_len, lanes].astype(F32)
            xs[c, s * pitch : s * pitch + 2 * HIST, :] = past
        for s in range(SEGS):
            rest = x_ref[s * seg_len : (s + 1) * seg_len, lanes].astype(F32)
            xs[c, s * pitch + 2 * HIST : (s + 1) * pitch + HIST, :] = rest

    def mask(i):
        m = keep[pl.ds(pl.multiple_of((i + 2) * SEGS, SEGS), SEGS), :]
        return jnp.concatenate([m] * (width // 128), 1)

    def row(i):
        return jnp.concatenate(
            [xs[c, pl.ds(2 * HIST + i, SEGS, stride=pitch), :] for c in range(width // 128)], 1
        )

    w = [jnp.broadcast_to(cw_ref[j : j + 1, :], (SEGS, width)) for j in range(CONV)]
    bias = jnp.broadcast_to(cb_ref[...], (SEGS, width))

    def conv_step(i, carry):
        a, b, c = carry
        x = row(i)
        m = mask(i)
        d = w[0] * x + m * c + bias
        c = w[1] * x + m * b
        b = w[2] * x + m * a
        a = w[3] * x
        return (a, b, c), d

    x3, x2, x1 = row(-3), row(-2), row(-1)
    a1 = w[3] * x1
    b1 = w[2] * x1 + mask(-1) * (w[3] * x2)
    c1 = w[1] * x1 + mask(-1) * (w[2] * x2 + mask(-2) * (w[3] * x3))

    def conv_pair(k, carry):
        carry, d0 = conv_step(2 * k, carry)
        carry, d1 = conv_step(2 * k + 1, carry)
        co[pl.ds(pl.multiple_of(k * 2 * SEGS, 2 * SEGS), 2 * SEGS), :] = jnp.concatenate([d0, d1], 0).astype(BF16)
        return carry

    lax.fori_loop(0, seg_len // 2, conv_pair, (a1, b1, c1), unroll=8)

    weight = dequantized(panel_ref[0], scale_ref[0]) * BF16(0.5)
    gate[...] = jnp.dot(co[...], weight, preferred_element_type=F32)

    bias_r = jnp.broadcast_to(gb_ref[0:1, :] * 0.5, (SEGS, width))
    bias_i = jnp.broadcast_to(gb_ref[1:2, :] * 0.5, (SEGS, width))
    rate4 = jnp.broadcast_to(rate_ref[...] * (-4.0 * LOG2E), (SEGS, width))

    def scan_step(i, conv, carry):
        h, p = carry
        at = pl.ds(pl.multiple_of(i * SEGS, SEGS), SEGS)
        m = mask(i)
        v = rate4 * (1.0 + jnp.tanh(gate[at, :width] + bias_r))
        ti = 1.0 + jnp.tanh(gate[at, width:] + bias_i)
        decay = jnp.exp2(v)
        s = v * v
        series = ((s * SINH[3] + SINH[2]) * s + SINH[1]) * s + SINH[0]
        quarter = decay * (v * series)
        half = quarter * lax.rsqrt(jnp.maximum(quarter, 1e-37))
        half = jnp.where(m > 0.0, half, 0.5)
        decay = decay * m
        h = decay * h + ti * (conv * half)
        p = p * decay
        for c in range(width // 128):
            h_ref[c, at, :] = h[:, c * 128 : (c + 1) * 128]
            p_ref[c, at, :] = p[:, c * 128 : (c + 1) * 128]
        return h, p

    def scan_pair(k, carry):
        conv = co[pl.ds(pl.multiple_of(k * 2 * SEGS, 2 * SEGS), 2 * SEGS), :].astype(F32)
        carry = scan_step(2 * k, conv[:SEGS], carry)
        return scan_step(2 * k + 1, conv[SEGS:], carry)

    h, p = lax.fori_loop(
        0,
        seg_len // 2,
        scan_pair,
        (jnp.zeros((SEGS, width), F32), jnp.ones((SEGS, width), F32)),
        unroll=8,
    )
    ends_ref[0] = p
    ends_ref[1] = h
    tp, th = p[0:1], h[0:1]
    for s in range(1, SEGS):
        th = p[s : s + 1] * th + h[s : s + 1]
        tp = tp * p[s : s + 1]
    tot_ref[0:1, :] = tp
    tot_ref[1:2, :] = th


def level_kernel(tot_ref, near_ref, level_ref):
    odd = lax.axis_index("tm") % 2 == 1
    tot, near = tot_ref[...], near_ref[...]
    lower = jnp.where(odd, near, tot)
    upper = jnp.where(odd, tot, near)
    level_ref[0:1, :] = lower[0:1] * upper[0:1]
    level_ref[1:2, :] = upper[0:1] * lower[1:2] + upper[1:2]


def mix_kernel(levels, h_ref, p_ref, ends_ref, *refs):
    near_ref, past, rest = refs[0], refs[1 : levels + 1], refs[levels + 1 :]
    y_ref, panel_ref, scale_ref, mixed_ref, kv_ref, carry = rest
    rows, width = y_ref.shape
    me = lax.axis_index("tm")
    seg_len = rows // SEGS

    @pl.when(pl.program_id(0) == 0)
    def _():
        kv_ref[...] = jnp.zeros_like(kv_ref)

    c = jnp.zeros((1, width), F32)
    for k in range(levels, 0, -1):
        c = jnp.where(me >= 2 * k, past[k - 1][0:1, :] * c + past[k - 1][1:2, :], 0.0)
    c = jnp.where(me % 2 == 1, near_ref[0:1, :] * c + near_ref[1:2, :], c)
    for s in range(SEGS):
        carry[s : s + 1, :] = c
        c = ends_ref[0, s : s + 1, :] * c + ends_ref[1, s : s + 1, :]
    groups = width // SCALE_ROWS
    table = scale_ref[...]
    index = lax.broadcasted_iota(jnp.int32, table.shape, 0) - pl.program_id(0) * groups
    scale = [jnp.sum(jnp.where(index == g, table, 0.0), axis=0, keepdims=True) for g in range(groups)]
    weight = dequantized(panel_ref[...], jnp.concatenate(scale, 0))

    def natural(ref, g, s):
        return jnp.concatenate(
            [ref[g, pl.ds(s + k * 8 * SEGS, 8, stride=SEGS), :] for k in range(seg_len // 8)], 0
        )

    for s in range(SEGS):
        at = slice(s * seg_len, (s + 1) * seg_len)
        y = y_ref[at, :].astype(F32)
        inner = y * (0.7978845608028654 + (0.7978845608028654 * 0.044715) * (y * y))
        gelu = (0.5 * y) * (1.0 + jnp.tanh(inner))
        local_h = jnp.concatenate([natural(h_ref, g, s) for g in range(width // 128)], 1)
        local_p = jnp.concatenate([natural(p_ref, g, s) for g in range(width // 128)], 1)
        mixed_ref[at, :] = ((local_h + local_p * carry[s : s + 1, :]) * gelu).astype(BF16)
    kv_ref[...] += jnp.dot(mixed_ref[...], weight, preferred_element_type=F32)


def sum_kernel(a_ref, b_ref, own_ref, half_ref):
    both = a_ref[...] + b_ref[...]
    n = both.shape[0] // 2
    core = lax.axis_index("mp")
    for side in range(2):
        keys = both[side * n : (side + 1) * n, :HD].T.astype(BF16)
        values = both[side * n : (side + 1) * n, HD:].astype(BF16)
        own_ref[side, :HD, :] = keys
        own_ref[side, HD:, :] = values
    half_ref[...] = own_ref[core]


def attend_kernel(own, lags, final, heads, starts_ref, q_ref, *refs):
    refs = list(refs)
    take = lambda n: [refs.pop(0) for _ in range(n)]
    own_ref = take(1)[0] if own else None
    pairs = [take(2) for _ in lags]
    prev = None if own else take(3)
    out = take(1)[0] if final else None
    acc, m_ref, l_ref = (None, None, None) if final else take(3)
    low, score, top = take(3)
    if final:
        acc, m_ref, l_ref, stage, sems = take(5)
    prob, l_new, excess = (None, None, None) if own else take(3)
    rows = q_ref.shape[0]
    half = rows // 2
    me = lax.axis_index("tm")
    first = me * rows
    core = lax.axis_index("mp")
    turn = 2 * (me % 2) - 1
    scale = LOG2E / math.sqrt(HD)

    def lowest(t):
        d0 = jnp.maximum(t - (WINDOW - 1), 0)
        for d in range(DOCS):
            d0 = jnp.maximum(d0, jnp.where(starts_ref[d] <= t, starts_ref[d], 0))
        return d0

    lo_first = lowest(first)
    lo_last = lowest(first + rows - 1)
    tiles = [(None, first)] if own else []
    for k, (even_part, odd_part) in enumerate(lags):
        tiles.append((pairs[k], first - (even_part + odd_part * turn) * rows))
    live = [None if pair is None else (start >= 0) & (start < first) & (start + rows > lo_first) for pair, start in tiles]

    def keys_of(pair, t):
        return own_ref[t, :HD, :] if pair is None else pair[t][:HD, :]

    def values_of(pair, t):
        return own_ref[t, HD:, :] if pair is None else pair[t][HD:, :]

    def lanes(g, h, n):
        return pl.ds(pl.multiple_of((g * GROUP + h) * n, n), n)

    def kept(g, h, n):
        return slice(h * n, (h + 1) * n) if final else lanes(g, h, n)

    def score_pass(g, j, pair, start, masked):
        for h in range(GROUP):
            for t in range(2):
                r0 = half * t if pair is None else 0
                at = slice(r0, rows)
                s = jnp.dot(q_ref[at, lanes(g, h, HD)], keys_of(pair, t), preferred_element_type=F32)
                peak = top[h, at, :]
                for c in range(half // 128):
                    part = s[:, c * 128 : (c + 1) * 128] * scale
                    if masked:
                        side = t if pair is None else jnp.where(core == t, 0, 1)
                        kpos = lax.broadcasted_iota(jnp.int32, part.shape, 1) + (start + side * half + c * 128)
                        ok = kpos >= low[at, :]
                        if pair is None:
                            ok = ok & (kpos <= lax.broadcasted_iota(jnp.int32, part.shape, 0) + (first + r0))
                        part = jnp.where(ok, part, -1e30)
                    score[j, h, t, at, c * 128 : (c + 1) * 128] = part
                    peak = jnp.maximum(peak, part)
                top[h, at, :] = peak

    def value_pass(g, j, pair):
        for h in range(GROUP):
            spans = [(0, half, 1), (half, rows, 2)] if pair is None else [(0, rows, 2)]
            for r0, r1, n in spans:
                at = slice(r0, r1)
                m = m_ref[at, kept(g, h, 128)]
                total = l_ref[at, kept(g, h, 128)]
                ps, vs = [], []
                for t in range(n):
                    for c in range(half // 128):
                        p = jnp.exp2(score[j, h, t, at, c * 128 : (c + 1) * 128] - m)
                        total = total + p
                        ps.append(p.astype(BF16))
                    vs.append(values_of(pair, t))
                l_ref[at, kept(g, h, 128)] = total
                acc[at, kept(g, h, HD)] += jnp.dot(
                    jnp.concatenate(ps, 1), jnp.concatenate(vs, 0), preferred_element_type=F32
                )

    def spread(x):
        return jnp.concatenate([x] * (HD // 128), 1)

    def update(g):
        top[...] = jnp.full(top.shape, -1e30, F32)
        for j, (pair, start) in enumerate(tiles):
            if pair is None:
                score_pass(g, j, pair, start, True)
                continue

            @pl.when(live[j] & (start >= lo_last))
            def _(j=j, pair=pair, start=start):
                score_pass(g, j, pair, start, False)

            @pl.when(live[j] & (start < lo_last))
            def _(j=j, pair=pair, start=start):
                score_pass(g, j, pair, start, True)

        for h in range(GROUP):
            m = jnp.broadcast_to(jnp.max(top[h], axis=1, keepdims=True), (rows, 128))
            if own:
                l_ref[:, kept(g, h, 128)] = jnp.zeros((rows, 128), F32)
                acc[:, kept(g, h, HD)] = jnp.zeros((rows, HD), F32)
            else:
                m0 = prev[1][:, lanes(g, h, 128)]
                m = jnp.maximum(m, m0)
                fade = jnp.exp2(m0 - m)
                l_ref[:, kept(g, h, 128)] = prev[2][:, lanes(g, h, 128)] * fade
                acc[:, kept(g, h, HD)] = prev[0][:, lanes(g, h, HD)] * spread(fade)
            m_ref[:, kept(g, h, 128)] = m
        for j, (pair, start) in enumerate(tiles):
            if pair is None:
                value_pass(g, j, pair)
                continue

            @pl.when(live[j])
            def _(j=j, pair=pair):
                value_pass(g, j, pair)

    def loop(fn):
        def body(g, z):
            fn(g)
            return z

        lax.fori_loop(0, heads // GROUP, body, 0)

    def start_up():
        low[...] = lowest(first + lax.broadcasted_iota(jnp.int32, (rows, 128), 0))

    if own:
        start_up()
        loop(update)
        return

    def exp_pass(g, j, pair, start, masked):
        for h in range(GROUP):
            m = prev[1][:, lanes(g, h, 128)]
            total = l_new[:, lanes(g, h, 128)]
            worst = excess[...]
            for t in range(2):
                s = jnp.dot(q_ref[:, lanes(g, h, HD)], keys_of(pair, t), preferred_element_type=F32)
                for c in range(half // 128):
                    part = s[:, c * 128 : (c + 1) * 128] * scale
                    if masked:
                        side = jnp.where(core == t, 0, 1)
                        kpos = lax.broadcasted_iota(jnp.int32, part.shape, 1) + (start + side * half + c * 128)
                        part = jnp.where(kpos >= low[...], part, -1e30)
                    part = part - m
                    worst = jnp.maximum(worst, part)
                    p = jnp.exp2(part)
                    total = total + p
                    at = t * half + c * 128
                    prob[j, g * GROUP + h, :, at : at + 128] = p.astype(BF16)
            l_new[:, lanes(g, h, 128)] = total
            excess[...] = worst

    def weighted(g, h, j, pair):
        values = jnp.concatenate([values_of(pair, t) for t in range(2)], 0)
        return jnp.dot(prob[j, g * GROUP + h], values, preferred_element_type=F32)

    def exp_all(g):
        for j, (pair, start) in enumerate(tiles):

            @pl.when(live[j] & (start >= lo_last))
            def _(j=j, pair=pair, start=start):
                exp_pass(g, j, pair, start, False)

            @pl.when(live[j] & (start < lo_last))
            def _(j=j, pair=pair, start=start):
                exp_pass(g, j, pair, start, True)

    any_live = functools.reduce(jnp.logical_or, live)

    @pl.when(any_live)
    def _():
        start_up()
        l_new[...] = prev[2][...]
        excess[...] = jnp.full(excess.shape, -1e30, F32)
        loop(exp_all)

    within = jnp.max(excess[...]) <= 64.0
    fast = any_live & within
    slow = any_live & jnp.logical_not(within)

    if not final:

        def add_all(g):
            for j, (pair, start) in enumerate(tiles):

                @pl.when(live[j])
                def _(j=j, pair=pair):
                    for h in range(GROUP):
                        acc[:, lanes(g, h, HD)] += weighted(g, h, j, pair)

        @pl.when(fast)
        def _():
            l_ref[...] = l_new[...]
            loop(add_all)

        @pl.when(slow)
        def _():
            loop(update)

        return

    def outgoing(g):
        wide = pl.ds(pl.multiple_of(g * GROUP * HD, GROUP * HD), GROUP * HD)
        return pltpu.make_async_copy(stage.at[g], out.at[:, wide], sems.at[g])

    def settle(g, h, top_sum, below):
        share = jnp.broadcast_to(1.0 / jnp.sum(below, axis=1, keepdims=True), (rows, 128))
        stage[g, :, h * HD : (h + 1) * HD] = (top_sum * spread(share)).astype(BF16)

    def finish(g):
        @pl.when(fast)
        def _():
            for h in range(GROUP):
                sums = prev[0][:, lanes(g, h, HD)] + weighted(g, h, 0, tiles[0][0])
                settle(g, h, sums, l_new[:, lanes(g, h, 128)])

        @pl.when(slow)
        def _():
            update(g)
            for h in range(GROUP):
                settle(g, h, acc[:, kept(g, h, HD)], l_ref[:, kept(g, h, 128)])

        @pl.when(jnp.logical_not(any_live))
        def _():
            for h in range(GROUP):
                settle(g, h, prev[0][:, lanes(g, h, HD)], prev[2][:, lanes(g, h, 128)])

        outgoing(g).start()

    loop(finish)
    loop(lambda g: outgoing(g).wait())


def recur_call(starts, x, halo, conv_weight, conv_bias, gate_panel, gate_scale, gate_bias, decay_rate):
    rows, channels = x.shape
    blocks, width, _ = gate_panel.shape
    col = lambda b, s: (0, b)
    return pl.pallas_call(
        recur_kernel,
        grid_spec=pltpu.PrefetchScalarGridSpec(
            num_scalar_prefetch=1,
            grid=(blocks,),
            in_specs=[
                pl.BlockSpec((rows, width), col),
                pl.BlockSpec((CONV - 1, width), col),
                pl.BlockSpec((CONV, width), col),
                pl.BlockSpec((1, width), col),
                pl.BlockSpec((1, width, 2 * width), lambda b, s: (b, 0, 0)),
                pl.BlockSpec((1, width // SCALE_ROWS, 2 * width), lambda b, s: (b, 0, 0)),
                pl.BlockSpec((2, width), col),
                pl.BlockSpec((1, width), col),
            ],
            out_specs=[
                pl.BlockSpec((width // 128, rows, 128), lambda b, s: (b, 0, 0)),
                pl.BlockSpec((width // 128, rows, 128), lambda b, s: (b, 0, 0)),
                pl.BlockSpec((2, SEGS, width), lambda b, s: (0, 0, b)),
                pl.BlockSpec((2, width), col),
            ],
            scratch_shapes=[
                pltpu.VMEM((rows + 2 * SEGS, 128), F32),
                pltpu.VMEM((width // 128, rows + HIST * (SEGS + 1), 128), F32),
                pltpu.VMEM((rows, width), BF16),
                pltpu.VMEM((rows, 2 * width), F32),
            ],
        ),
        out_shape=[
            jax.ShapeDtypeStruct((channels // 128, rows, 128), F32),
            jax.ShapeDtypeStruct((channels // 128, rows, 128), F32),
            jax.ShapeDtypeStruct((2, SEGS, channels), F32),
            jax.ShapeDtypeStruct((2, channels), F32),
        ],
        compiler_params=pltpu.CompilerParams(vmem_limit_bytes=20 << 20),
        name="recur",
    )(starts, x, halo, conv_weight, conv_bias, gate_panel, gate_scale, gate_bias, decay_rate)


def level_call(tot, near):
    return pl.pallas_call(
        level_kernel,
        out_shape=jax.ShapeDtypeStruct(tot.shape, F32),
        compiler_params=pltpu.CompilerParams(vmem_limit_bytes=1 << 20),
        name="level",
    )(tot, near)


def mix_call(h, p, ends, near, past, y, kv_panel, kv_scale):
    rows, channels = y.shape
    width = MIX_GROUPS * SCALE_ROWS
    col = lambda b: (0, b)
    out = kv_panel.shape[1]
    pair = pl.BlockSpec((2, width), col)
    return pl.pallas_call(
        functools.partial(mix_kernel, len(past)),
        grid=(channels // width,),
        in_specs=[
            pl.BlockSpec((width // 128, rows, 128), lambda b: (b, 0, 0)),
            pl.BlockSpec((width // 128, rows, 128), lambda b: (b, 0, 0)),
            pl.BlockSpec((2, SEGS, width), lambda b: (0, 0, b)),
        ]
        + [pair] * (1 + len(past))
        + [
            pl.BlockSpec((rows, width), col),
            pl.BlockSpec((width, out), lambda b: (b, 0)),
            pl.BlockSpec(kv_scale.shape, lambda b: (0, 0)),
        ],
        out_specs=[pl.BlockSpec((rows, width), col), pl.BlockSpec((rows, out), lambda b: (0, 0))],
        out_shape=[jax.ShapeDtypeStruct((rows, channels), BF16), jax.ShapeDtypeStruct((rows, out), F32)],
        scratch_shapes=[pltpu.VMEM((SEGS, width), F32)],
        compiler_params=pltpu.CompilerParams(vmem_limit_bytes=20 << 20),
        name="mix",
    )(h, p, ends, near, *past, y, kv_panel, kv_scale)


def sum_call(a, b):
    rows, _ = a.shape
    half = rows // 2
    return pl.pallas_call(
        sum_kernel,
        out_shape=[
            jax.ShapeDtypeStruct((2, 2 * HD, half), BF16),
            jax.ShapeDtypeStruct((2 * HD, half), BF16),
        ],
        compiler_params=pltpu.CompilerParams(vmem_limit_bytes=16 << 20),
        name="kvsum",
    )(a, b)


def attend_call(starts, q, own, halves, lags, prev, final):
    rows, width = q.shape
    heads = width // HD
    held = [] if own is None else [own]
    held += halves
    held += prev or []
    tiles = len(lags) + (own is not None)
    vmem = pl.BlockSpec(memory_space=pltpu.VMEM)
    scratch = [
        pltpu.VMEM((rows, 128), jnp.int32),
        pltpu.VMEM((tiles, GROUP, 2, rows, rows // 2), F32),
        pltpu.VMEM((GROUP, rows, 128), F32),
    ]
    aliases = {}
    if final:
        out_specs = pl.BlockSpec(memory_space=pl.ANY)
        out_shape = jax.ShapeDtypeStruct((rows, width), BF16)
        scratch += [pltpu.VMEM((rows, GROUP * n), F32) for n in (HD, 128, 128)]
        scratch += [pltpu.VMEM((heads // GROUP, rows, GROUP * HD), BF16), pltpu.SemaphoreType.DMA((heads // GROUP,))]
    if own is None:
        scratch += [
            pltpu.VMEM((tiles, heads, rows, rows), BF16),
            pltpu.VMEM((rows, heads * 128), F32),
            pltpu.VMEM((rows, 128), F32),
        ]
    if not final:
        out_specs = [vmem] * 3
        out_shape = [jax.ShapeDtypeStruct((rows, heads * n), F32) for n in (HD, 128, 128)]
        if prev:
            aliases = {2 + len(halves) + k: k for k in range(3)}
    return pl.pallas_call(
        functools.partial(attend_kernel, own is not None, lags, final, heads),
        in_specs=[pl.BlockSpec(memory_space=pltpu.SMEM), vmem] + [vmem] * len(held),
        out_specs=out_specs,
        scratch_shapes=scratch,
        out_shape=out_shape,
        input_output_aliases=aliases,
        cost_estimate=pl.CostEstimate(
            flops=4 * tiles * rows * rows * width,
            bytes_accessed=4 * rows * width,
            transcendentals=tiles * rows * rows * heads,
        ),
        compiler_params=pltpu.CompilerParams(vmem_limit_bytes=32 << 20),
        name="attend_own" if own is not None else "attend_end" if final else "attend_mid",
    )(starts, q, *held)


def local(
    branch_x,
    branch_y,
    queries,
    conv_weight,
    conv_bias,
    gate_panel,
    gate_scale,
    gate_bias,
    decay_rate,
    kv_panel,
    kv_scale,
    segment_ids,
):
    rows = branch_x.shape[0]
    seq = segment_ids.shape[0]
    halo = ring(branch_x[rows - CONV + 1 :], 1)
    starts = jnp.sum(
        (segment_ids[None, :] < jnp.arange(DOCS, dtype=jnp.int32)[:, None]).astype(jnp.int32), axis=1
    )
    stay = lambda a: pltpu.with_memory_space_constraint(a, pltpu.HBM)
    h, p, ends, tot = recur_call(
        starts,
        stay(branch_x),
        halo,
        stay(conv_weight),
        stay(conv_bias[None]),
        stay(gate_panel),
        stay(gate_scale),
        stay(gate_bias),
        stay(decay_rate[None]),
    )
    near = swap(tot)
    level = level_call(tot, near)
    levels = -(-(seq // 2) // (2 * rows))
    past = [ring(level, 2 * k) for k in range(1, levels + 1)]
    mixed, partial_kv = mix_call(h, p, ends, near, past, branch_y, kv_panel, kv_scale)
    own, half = sum_call(partial_kv, partner(partial_kv))

    levels = -(-WINDOW // rows) // 2
    straight, attended = half, None
    for k in range(levels + 1):
        last = k == levels
        beyond = None if last else ring(straight, 2)
        crossed = swap(straight)
        if k == 0:
            attended = attend_call(starts, queries, own, [], [], None, False)
        else:
            attended = attend_call(starts, queries, None, tiles, lags, attended, False)
        tiles, lags = [crossed, partner(crossed)], [(2 * k, 1)]
        if not last:
            tiles += [beyond, partner(beyond)]
            lags.append((2 * k + 2, 0))
        straight = beyond
    attended = attend_call(starts, queries, None, tiles, lags, attended, True)
    return mixed, attended


def solution(mesh):
    in_specs = (
        P(("groups", "tm"), "mp"),
        P(("groups", "tm"), "mp"),
        P(("groups", "tm"), "mp"),
        P(None, "mp"),
        P("mp"),
        P("mp", None, None),
        P("mp", None, None),
        P(None, "mp"),
        P("mp"),
        P("mp", None),
        P("mp", None),
        P("groups"),
    )
    out_specs = (P(("groups", "tm"), "mp"), P(("groups", "tm"), "mp"))
    return jax.shard_map(local, mesh=mesh, in_specs=in_specs, out_specs=out_specs, check_vma=False)
```

```python
import functools
import math

import jax
import jax.numpy as jnp
from jax import lax
from jax.experimental import pallas as pl
from jax.experimental.pallas import tpu as pltpu
from jax.sharding import PartitionSpec as P


HD = 256
CONV = 4
WINDOW = 2048
SCALE_ROWS = 128
DOCS = 4
SEGS = 8
MIX_GROUPS = 4
GROUP = 2
HIST = 4
LOG2E = 1.4426950408889634
LN2 = 0.6931471805599453
SINH = [-0.5 * LN2 ** (2 * k + 1) / math.factorial(2 * k + 1) for k in range(4)]
F32 = jnp.float32
BF16 = jnp.bfloat16


def ring(x, lag):
    n = lax.axis_size("tm")
    return lax.ppermute(x, "tm", [(i, (i + lag) % n) for i in range(n)])


def swap(x):
    n = lax.axis_size("tm")
    return lax.ppermute(x, "tm", [(i, i ^ 1) for i in range(n)])


def partner(x):
    return lax.ppermute(x, "mp", [(0, 1), (1, 0)])


def dequantized(panel, scale):
    rows = panel.shape[0]
    parts = []
    for g in range(rows // SCALE_ROWS):
        part = panel[g * SCALE_ROWS : (g + 1) * SCALE_ROWS, :].astype(F32)
        parts.append((part * scale[g : g + 1, :]).astype(BF16))
    return jnp.concatenate(parts, 0)


def recur_kernel(
    starts_ref,
    x_ref,
    halo_ref,
    cw_ref,
    cb_ref,
    panel_ref,
    scale_ref,
    gb_ref,
    rate_ref,
    h_ref,
    p_ref,
    ends_ref,
    tot_ref,
    keep,
    xs,
    co,
    gate,
):
    rows, width = x_ref.shape
    seg_len = rows // SEGS
    base = lax.axis_index("tm") * rows

    @pl.when(pl.program_id(0) == 0)
    def _():
        def fill(i, carry):
            pos = base + i - 2 + seg_len * lax.broadcasted_iota(jnp.int32, (SEGS, 128), 0)
            hit = pos == starts_ref[0]
            for d in range(1, DOCS):
                hit = hit | (pos == starts_ref[d])
            keep[pl.ds(pl.multiple_of(i * SEGS, SEGS), SEGS), :] = jnp.where(hit, 0.0, 1.0)
            return carry

        lax.fori_loop(0, seg_len + 2, fill, 0)

    pitch = seg_len + HIST
    for c in range(width // 128):
        lanes = slice(c * 128, (c + 1) * 128)
        xs[c, HIST + 1 : 2 * HIST, :] = halo_ref[:, lanes].astype(F32)
        for s in range(1, SEGS):
            past = x_ref[s * seg_len - 2 * HIST : s * seg_len, lanes].astype(F32)
            xs[c, s * pitch : s * pitch + 2 * HIST, :] = past
        for s in range(SEGS):
            rest = x_ref[s * seg_len : (s + 1) * seg_len, lanes].astype(F32)
            xs[c, s * pitch + 2 * HIST : (s + 1) * pitch + HIST, :] = rest

    def mask(i):
        m = keep[pl.ds(pl.multiple_of((i + 2) * SEGS, SEGS), SEGS), :]
        return jnp.concatenate([m] * (width // 128), 1)

    def row(i):
        return jnp.concatenate(
            [xs[c, pl.ds(2 * HIST + i, SEGS, stride=pitch), :] for c in range(width // 128)], 1
        )

    w = [jnp.broadcast_to(cw_ref[j : j + 1, :], (SEGS, width)) for j in range(CONV)]
    bias = jnp.broadcast_to(cb_ref[...], (SEGS, width))

    def conv_step(i, carry):
        a, b, c = carry
        x = row(i)
        m = mask(i)
        d = w[0] * x + m * c + bias
        c = w[1] * x + m * b
        b = w[2] * x + m * a
        a = w[3] * x
        return (a, b, c), d

    x3, x2, x1 = row(-3), row(-2), row(-1)
    a1 = w[3] * x1
    b1 = w[2] * x1 + mask(-1) * (w[3] * x2)
    c1 = w[1] * x1 + mask(-1) * (w[2] * x2 + mask(-2) * (w[3] * x3))

    def conv_pair(k, carry):
        carry, d0 = conv_step(2 * k, carry)
        carry, d1 = conv_step(2 * k + 1, carry)
        d = jnp.concatenate([d0, d1], 0).astype(BF16)
        for c in range(width // 128):
            co[c, pl.ds(pl.multiple_of(k * 2 * SEGS, 2 * SEGS), 2 * SEGS), :] = d[:, c * 128 : (c + 1) * 128]
        return carry

    lax.fori_loop(0, seg_len // 2, conv_pair, (a1, b1, c1), unroll=8)

    weight = dequantized(panel_ref[0], scale_ref[0]) * BF16(0.5)
    conv_out = jnp.concatenate([co[c] for c in range(width // 128)], 1)
    gate[...] = jnp.dot(conv_out, weight, preferred_element_type=F32)

    bias_r = jnp.broadcast_to(gb_ref[0:1, :] * 0.5, (SEGS, width))
    bias_i = jnp.broadcast_to(gb_ref[1:2, :] * 0.5, (SEGS, width))
    rate4 = jnp.broadcast_to(rate_ref[...] * (-4.0 * LOG2E), (SEGS, width))

    def scan_step(i, conv, carry):
        h, p = carry
        at = pl.ds(pl.multiple_of(i * SEGS, SEGS), SEGS)
        m = mask(i)
        v = rate4 * (1.0 + jnp.tanh(gate[at, :width] + bias_r))
        ti = 1.0 + jnp.tanh(gate[at, width:] + bias_i)
        decay = jnp.exp2(v)
        s = v * v
        series = ((s * SINH[3] + SINH[2]) * s + SINH[1]) * s + SINH[0]
        quarter = decay * (v * series)
        half = quarter * lax.rsqrt(jnp.maximum(quarter, 1e-37))
        half = jnp.where(m > 0.0, half, 0.5)
        decay = decay * m
        h = decay * h + ti * (conv * half)
        p = p * decay
        for c in range(width // 128):
            h_ref[c, at, :] = h[:, c * 128 : (c + 1) * 128]
            p_ref[c, at, :] = p[:, c * 128 : (c + 1) * 128]
        return h, p

    def scan_pair(k, carry):
        at = pl.ds(pl.multiple_of(k * 2 * SEGS, 2 * SEGS), 2 * SEGS)
        conv = jnp.concatenate([co[c, at, :].astype(F32) for c in range(width // 128)], 1)
        carry = scan_step(2 * k, conv[:SEGS], carry)
        return scan_step(2 * k + 1, conv[SEGS:], carry)

    h, p = lax.fori_loop(
        0,
        seg_len // 2,
        scan_pair,
        (jnp.zeros((SEGS, width), F32), jnp.ones((SEGS, width), F32)),
        unroll=8,
    )
    ends_ref[0] = p
    ends_ref[1] = h
    tp, th = p[0:1], h[0:1]
    for s in range(1, SEGS):
        th = p[s : s + 1] * th + h[s : s + 1]
        tp = tp * p[s : s + 1]
    tot_ref[0:1, :] = tp
    tot_ref[1:2, :] = th


def level_kernel(tot_ref, near_ref, level_ref):
    odd = lax.axis_index("tm") % 2 == 1
    tot, near = tot_ref[...], near_ref[...]
    lower = jnp.where(odd, near, tot)
    upper = jnp.where(odd, tot, near)
    level_ref[0:1, :] = lower[0:1] * upper[0:1]
    level_ref[1:2, :] = upper[0:1] * lower[1:2] + upper[1:2]


def mix_kernel(levels, h_ref, p_ref, ends_ref, *refs):
    near_ref, past, rest = refs[0], refs[1 : levels + 1], refs[levels + 1 :]
    y_ref, panel_ref, scale_ref, mixed_ref, kv_ref, carry = rest
    rows, width = y_ref.shape
    me = lax.axis_index("tm")
    seg_len = rows // SEGS

    @pl.when(pl.program_id(0) == 0)
    def _():
        kv_ref[...] = jnp.zeros_like(kv_ref)

    c = jnp.zeros((1, width), F32)
    for k in range(levels, 0, -1):
        c = jnp.where(me >= 2 * k, past[k - 1][0:1, :] * c + past[k - 1][1:2, :], 0.0)
    c = jnp.where(me % 2 == 1, near_ref[0:1, :] * c + near_ref[1:2, :], c)
    for s in range(SEGS):
        carry[s : s + 1, :] = c
        c = ends_ref[0, s : s + 1, :] * c + ends_ref[1, s : s + 1, :]
    groups = width // SCALE_ROWS
    table = scale_ref[...]
    index = lax.broadcasted_iota(jnp.int32, table.shape, 0) - pl.program_id(0) * groups
    scale = [jnp.sum(jnp.where(index == g, table, 0.0), axis=0, keepdims=True) for g in range(groups)]
    weight = dequantized(panel_ref[...], jnp.concatenate(scale, 0))

    def natural(ref, g, s):
        return jnp.concatenate(
            [ref[g, pl.ds(s + k * 8 * SEGS, 8, stride=SEGS), :] for k in range(seg_len // 8)], 0
        )

    for s in range(SEGS):
        at = slice(s * seg_len, (s + 1) * seg_len)
        y = y_ref[at, :].astype(F32)
        inner = y * (0.7978845608028654 + (0.7978845608028654 * 0.044715) * (y * y))
        gelu = (0.5 * y) * (1.0 + jnp.tanh(inner))
        local_h = jnp.concatenate([natural(h_ref, g, s) for g in range(width // 128)], 1)
        local_p = jnp.concatenate([natural(p_ref, g, s) for g in range(width // 128)], 1)
        mixed_ref[at, :] = ((local_h + local_p * carry[s : s + 1, :]) * gelu).astype(BF16)
    kv_ref[...] += jnp.dot(mixed_ref[...], weight, preferred_element_type=F32)


def sum_kernel(a_ref, b_ref, own_ref, half_ref):
    both = a_ref[...] + b_ref[...]
    n = both.shape[0] // 2
    core = lax.axis_index("mp")
    for side in range(2):
        keys = both[side * n : (side + 1) * n, :HD].T.astype(BF16)
        values = both[side * n : (side + 1) * n, HD:].astype(BF16)
        own_ref[side, :HD, :] = keys
        own_ref[side, HD:, :] = values
    half_ref[...] = own_ref[core]


def attend_kernel(own, lags, final, heads, starts_ref, q_ref, *refs):
    refs = list(refs)
    take = lambda n: [refs.pop(0) for _ in range(n)]
    own_ref = take(1)[0] if own else None
    pairs = [take(2) for _ in lags]
    prev = None if own else take(3)
    out = take(1)[0] if final else None
    acc, m_ref, l_ref = (None, None, None) if final else take(3)
    low, score, top = take(3)
    if final:
        acc, m_ref, l_ref, stage, sems = take(5)
    prob, l_new = (None, None) if own else take(2)
    rows = q_ref.shape[0]
    half = rows // 2
    me = lax.axis_index("tm")
    first = me * rows
    core = lax.axis_index("mp")
    turn = 2 * (me % 2) - 1
    scale = LOG2E / math.sqrt(HD)

    def lowest(t):
        d0 = jnp.maximum(t - (WINDOW - 1), 0)
        for d in range(DOCS):
            d0 = jnp.maximum(d0, jnp.where(starts_ref[d] <= t, starts_ref[d], 0))
        return d0

    lo_first = lowest(first)
    lo_last = lowest(first + rows - 1)
    tiles = [(None, first)] if own else []
    for k, (even_part, odd_part) in enumerate(lags):
        tiles.append((pairs[k], first - (even_part + odd_part * turn) * rows))
    live = [None if pair is None else (start >= 0) & (start < first) & (start + rows > lo_first) for pair, start in tiles]

    def keys_of(pair, t):
        return own_ref[t, :HD, :] if pair is None else pair[t][:HD, :]

    def values_of(pair, t):
        return own_ref[t, HD:, :] if pair is None else pair[t][HD:, :]

    def lanes(g, h, n):
        return pl.ds(pl.multiple_of((g * GROUP + h) * n, n), n)

    def kept(g, h, n):
        return slice(h * n, (h + 1) * n) if final else lanes(g, h, n)

    def score_pass(g, j, pair, start, masked):
        for h in range(GROUP):
            for t in range(2):
                r0 = half * t if pair is None else 0
                at = slice(r0, rows)
                s = jnp.dot(q_ref[at, lanes(g, h, HD)], keys_of(pair, t), preferred_element_type=F32)
                peak = top[h, at, :]
                for c in range(half // 128):
                    part = s[:, c * 128 : (c + 1) * 128] * scale
                    if masked:
                        side = t if pair is None else jnp.where(core == t, 0, 1)
                        kpos = lax.broadcasted_iota(jnp.int32, part.shape, 1) + (start + side * half + c * 128)
                        ok = kpos >= low[at, :]
                        if pair is None:
                            ok = ok & (kpos <= lax.broadcasted_iota(jnp.int32, part.shape, 0) + (first + r0))
                        part = jnp.where(ok, part, -1e30)
                    score[j, h, t, at, c * 128 : (c + 1) * 128] = part
                    peak = jnp.maximum(peak, part)
                top[h, at, :] = peak

    def value_pass(g, j, pair):
        for h in range(GROUP):
            spans = [(0, half, 1), (half, rows, 2)] if pair is None else [(0, rows, 2)]
            for r0, r1, n in spans:
                at = slice(r0, r1)
                m = m_ref[at, kept(g, h, 128)]
                total = l_ref[at, kept(g, h, 128)]
                ps, vs = [], []
                for t in range(n):
                    for c in range(half // 128):
                        p = jnp.exp2(score[j, h, t, at, c * 128 : (c + 1) * 128] - m)
                        total = total + p
                        ps.append(p.astype(BF16))
                    vs.append(values_of(pair, t))
                l_ref[at, kept(g, h, 128)] = total
                acc[at, kept(g, h, HD)] += jnp.dot(
                    jnp.concatenate(ps, 1), jnp.concatenate(vs, 0), preferred_element_type=F32
                )

    def spread(x):
        return jnp.concatenate([x] * (HD // 128), 1)

    def update(g):
        top[...] = jnp.full(top.shape, -1e30, F32)
        for j, (pair, start) in enumerate(tiles):
            if pair is None:
                score_pass(g, j, pair, start, True)
                continue

            @pl.when(live[j] & (start >= lo_last))
            def _(j=j, pair=pair, start=start):
                score_pass(g, j, pair, start, False)

            @pl.when(live[j] & (start < lo_last))
            def _(j=j, pair=pair, start=start):
                score_pass(g, j, pair, start, True)

        for h in range(GROUP):
            m = jnp.broadcast_to(jnp.max(top[h], axis=1, keepdims=True), (rows, 128))
            if own:
                l_ref[:, kept(g, h, 128)] = jnp.zeros((rows, 128), F32)
                acc[:, kept(g, h, HD)] = jnp.zeros((rows, HD), F32)
            else:
                m0 = prev[1][:, lanes(g, h, 128)]
                m = jnp.maximum(m, m0)
                fade = jnp.exp2(m0 - m)
                l_ref[:, kept(g, h, 128)] = prev[2][:, lanes(g, h, 128)] * fade
                acc[:, kept(g, h, HD)] = prev[0][:, lanes(g, h, HD)] * spread(fade)
            m_ref[:, kept(g, h, 128)] = m
        for j, (pair, start) in enumerate(tiles):
            if pair is None:
                value_pass(g, j, pair)
                continue

            @pl.when(live[j])
            def _(j=j, pair=pair):
                value_pass(g, j, pair)

    def loop(fn):
        def body(g, z):
            fn(g)
            return z

        lax.fori_loop(0, heads // GROUP, body, 0)

    def start_up():
        low[...] = lowest(first + lax.broadcasted_iota(jnp.int32, (rows, 128), 0))

    if own:
        start_up()
        loop(update)
        return

    def exp_pass(g, j, pair, start, masked):
        for h in range(GROUP):
            m = prev[1][:, lanes(g, h, 128)]
            total = l_new[:, lanes(g, h, 128)]
            for t in range(2):
                s = jnp.dot(q_ref[:, lanes(g, h, HD)], keys_of(pair, t), preferred_element_type=F32)
                for c in range(half // 128):
                    part = s[:, c * 128 : (c + 1) * 128] * scale
                    if masked:
                        side = jnp.where(core == t, 0, 1)
                        kpos = lax.broadcasted_iota(jnp.int32, part.shape, 1) + (start + side * half + c * 128)
                        part = jnp.where(kpos >= low[...], part, -1e30)
                    p = jnp.exp2(part - m)
                    total = total + p
                    prob[j, g * GROUP + h, (t * half) // 128 + c] = p.astype(BF16)
            l_new[:, lanes(g, h, 128)] = total

    def weighted(g, h, j, pair):
        values = jnp.concatenate([values_of(pair, t) for t in range(2)], 0)
        shares = jnp.concatenate([prob[j, g * GROUP + h, c] for c in range(rows // 128)], 1)
        return jnp.dot(shares, values, preferred_element_type=F32)

    def exp_all(g):
        for j, (pair, start) in enumerate(tiles):

            @pl.when(live[j] & (start >= lo_last))
            def _(j=j, pair=pair, start=start):
                exp_pass(g, j, pair, start, False)

            @pl.when(live[j] & (start < lo_last))
            def _(j=j, pair=pair, start=start):
                exp_pass(g, j, pair, start, True)

    any_live = functools.reduce(jnp.logical_or, live)

    @pl.when(any_live)
    def _():
        start_up()
        l_new[...] = prev[2][...]
        loop(exp_all)

    within = jnp.max(l_new[...]) <= 2.0**64
    fast = any_live & within
    slow = any_live & jnp.logical_not(within)

    if not final:

        def add_all(g):
            for j, (pair, start) in enumerate(tiles):

                @pl.when(live[j])
                def _(j=j, pair=pair):
                    for h in range(GROUP):
                        acc[:, lanes(g, h, HD)] += weighted(g, h, j, pair)

        @pl.when(fast)
        def _():
            l_ref[...] = l_new[...]
            loop(add_all)

        @pl.when(slow)
        def _():
            loop(update)

        return

    def outgoing(g):
        wide = pl.ds(pl.multiple_of(g * GROUP * HD, GROUP * HD), GROUP * HD)
        return pltpu.make_async_copy(stage.at[g], out.at[:, wide], sems.at[g])

    def settle(g, h, top_sum, below):
        share = jnp.broadcast_to(1.0 / jnp.sum(below, axis=1, keepdims=True), (rows, 128))
        stage[g, :, h * HD : (h + 1) * HD] = (top_sum * spread(share)).astype(BF16)

    def finish(g):
        @pl.when(fast)
        def _():
            for h in range(GROUP):
                sums = prev[0][:, lanes(g, h, HD)] + weighted(g, h, 0, tiles[0][0])
                settle(g, h, sums, l_new[:, lanes(g, h, 128)])

        @pl.when(slow)
        def _():
            update(g)
            for h in range(GROUP):
                settle(g, h, acc[:, kept(g, h, HD)], l_ref[:, kept(g, h, 128)])

        @pl.when(jnp.logical_not(any_live))
        def _():
            for h in range(GROUP):
                settle(g, h, prev[0][:, lanes(g, h, HD)], prev[2][:, lanes(g, h, 128)])

        outgoing(g).start()

    loop(finish)
    loop(lambda g: outgoing(g).wait())


def recur_call(starts, x, halo, conv_weight, conv_bias, gate_panel, gate_scale, gate_bias, decay_rate):
    rows, channels = x.shape
    blocks, width, _ = gate_panel.shape
    col = lambda b, s: (0, b)
    return pl.pallas_call(
        recur_kernel,
        grid_spec=pltpu.PrefetchScalarGridSpec(
            num_scalar_prefetch=1,
            grid=(blocks,),
            in_specs=[
                pl.BlockSpec((rows, width), col),
                pl.BlockSpec((CONV - 1, width), col),
                pl.BlockSpec((CONV, width), col),
                pl.BlockSpec((1, width), col),
                pl.BlockSpec((1, width, 2 * width), lambda b, s: (b, 0, 0)),
                pl.BlockSpec((1, width // SCALE_ROWS, 2 * width), lambda b, s: (b, 0, 0)),
                pl.BlockSpec((2, width), col),
                pl.BlockSpec((1, width), col),
            ],
            out_specs=[
                pl.BlockSpec((width // 128, rows, 128), lambda b, s: (b, 0, 0)),
                pl.BlockSpec((width // 128, rows, 128), lambda b, s: (b, 0, 0)),
                pl.BlockSpec((2, SEGS, width), lambda b, s: (0, 0, b)),
                pl.BlockSpec((2, width), col),
            ],
            scratch_shapes=[
                pltpu.VMEM((rows + 2 * SEGS, 128), F32),
                pltpu.VMEM((width // 128, rows + HIST * (SEGS + 1), 128), F32),
                pltpu.VMEM((width // 128, rows, 128), BF16),
                pltpu.VMEM((rows, 2 * width), F32),
            ],
        ),
        out_shape=[
            jax.ShapeDtypeStruct((channels // 128, rows, 128), F32),
            jax.ShapeDtypeStruct((channels // 128, rows, 128), F32),
            jax.ShapeDtypeStruct((2, SEGS, channels), F32),
            jax.ShapeDtypeStruct((2, channels), F32),
        ],
        compiler_params=pltpu.CompilerParams(vmem_limit_bytes=20 << 20),
        name="recur",
    )(starts, x, halo, conv_weight, conv_bias, gate_panel, gate_scale, gate_bias, decay_rate)


def level_call(tot, near):
    return pl.pallas_call(
        level_kernel,
        out_shape=jax.ShapeDtypeStruct(tot.shape, F32),
        compiler_params=pltpu.CompilerParams(vmem_limit_bytes=1 << 20),
        name="level",
    )(tot, near)


def mix_call(h, p, ends, near, past, y, kv_panel, kv_scale):
    rows, channels = y.shape
    width = MIX_GROUPS * SCALE_ROWS
    col = lambda b: (0, b)
    out = kv_panel.shape[1]
    pair = pl.BlockSpec((2, width), col)
    return pl.pallas_call(
        functools.partial(mix_kernel, len(past)),
        grid=(channels // width,),
        in_specs=[
            pl.BlockSpec((width // 128, rows, 128), lambda b: (b, 0, 0)),
            pl.BlockSpec((width // 128, rows, 128), lambda b: (b, 0, 0)),
            pl.BlockSpec((2, SEGS, width), lambda b: (0, 0, b)),
        ]
        + [pair] * (1 + len(past))
        + [
            pl.BlockSpec((rows, width), col),
            pl.BlockSpec((width, out), lambda b: (b, 0)),
            pl.BlockSpec(kv_scale.shape, lambda b: (0, 0)),
        ],
        out_specs=[pl.BlockSpec((rows, width), col), pl.BlockSpec((rows, out), lambda b: (0, 0))],
        out_shape=[jax.ShapeDtypeStruct((rows, channels), BF16), jax.ShapeDtypeStruct((rows, out), F32)],
        scratch_shapes=[pltpu.VMEM((SEGS, width), F32)],
        compiler_params=pltpu.CompilerParams(vmem_limit_bytes=20 << 20),
        name="mix",
    )(h, p, ends, near, *past, y, kv_panel, kv_scale)


def sum_call(a, b):
    rows, _ = a.shape
    half = rows // 2
    return pl.pallas_call(
        sum_kernel,
        out_shape=[
            jax.ShapeDtypeStruct((2, 2 * HD, half), BF16),
            jax.ShapeDtypeStruct((2 * HD, half), BF16),
        ],
        compiler_params=pltpu.CompilerParams(vmem_limit_bytes=16 << 20),
        name="kvsum",
    )(a, b)


def attend_call(starts, q, own, halves, lags, prev, final):
    rows, width = q.shape
    heads = width // HD
    held = [] if own is None else [own]
    held += halves
    held += prev or []
    tiles = len(lags) + (own is not None)
    vmem = pl.BlockSpec(memory_space=pltpu.VMEM)
    scratch = [
        pltpu.VMEM((rows, 128), jnp.int32),
        pltpu.VMEM((tiles, GROUP, 2, rows, rows // 2), F32),
        pltpu.VMEM((GROUP, rows, 128), F32),
    ]
    aliases = {}
    if final:
        out_specs = pl.BlockSpec(memory_space=pl.ANY)
        out_shape = jax.ShapeDtypeStruct((rows, width), BF16)
        scratch += [pltpu.VMEM((rows, GROUP * n), F32) for n in (HD, 128, 128)]
        scratch += [pltpu.VMEM((heads // GROUP, rows, GROUP * HD), BF16), pltpu.SemaphoreType.DMA((heads // GROUP,))]
    if own is None:
        scratch += [
            pltpu.VMEM((tiles, heads, rows // 128, rows, 128), BF16),
            pltpu.VMEM((rows, heads * 128), F32),
        ]
    if not final:
        out_specs = [vmem] * 3
        out_shape = [jax.ShapeDtypeStruct((rows, heads * n), F32) for n in (HD, 128, 128)]
        if prev:
            aliases = {2 + len(halves) + k: k for k in range(3)}
    return pl.pallas_call(
        functools.partial(attend_kernel, own is not None, lags, final, heads),
        in_specs=[pl.BlockSpec(memory_space=pltpu.SMEM), vmem] + [vmem] * len(held),
        out_specs=out_specs,
        scratch_shapes=scratch,
        out_shape=out_shape,
        input_output_aliases=aliases,
        cost_estimate=pl.CostEstimate(
            flops=4 * tiles * rows * rows * width,
            bytes_accessed=4 * rows * width,
            transcendentals=tiles * rows * rows * heads,
        ),
        compiler_params=pltpu.CompilerParams(vmem_limit_bytes=32 << 20),
        name="attend_own" if own is not None else "attend_end" if final else "attend_mid",
    )(starts, q, *held)


def local(
    branch_x,
    branch_y,
    queries,
    conv_weight,
    conv_bias,
    gate_panel,
    gate_scale,
    gate_bias,
    decay_rate,
    kv_panel,
    kv_scale,
    segment_ids,
):
    rows = branch_x.shape[0]
    seq = segment_ids.shape[0]
    halo = ring(branch_x[rows - CONV + 1 :], 1)
    starts = jnp.sum(
        (segment_ids[None, :] < jnp.arange(DOCS, dtype=jnp.int32)[:, None]).astype(jnp.int32), axis=1
    )
    stay = lambda a: pltpu.with_memory_space_constraint(a, pltpu.HBM)
    h, p, ends, tot = recur_call(
        starts,
        stay(branch_x),
        halo,
        stay(conv_weight),
        stay(conv_bias[None]),
        stay(gate_panel),
        stay(gate_scale),
        stay(gate_bias),
        stay(decay_rate[None]),
    )
    near = swap(tot)
    level = level_call(tot, near)
    levels = -(-(seq // 2) // (2 * rows))
    past = [ring(level, 2 * k) for k in range(1, levels + 1)]
    mixed, partial_kv = mix_call(h, p, ends, near, past, branch_y, kv_panel, kv_scale)
    own, half = sum_call(partial_kv, partner(partial_kv))

    levels = -(-WINDOW // rows) // 2
    straight, attended = half, None
    for k in range(levels + 1):
        last = k == levels
        beyond = None if last else ring(straight, 2)
        crossed = swap(straight)
        if k == 0:
            attended = attend_call(starts, queries, own, [], [], None, False)
        else:
            attended = attend_call(starts, queries, None, tiles, lags, attended, False)
        tiles, lags = [crossed, partner(crossed)], [(2 * k, 1)]
        if not last:
            tiles += [beyond, partner(beyond)]
            lags.append((2 * k + 2, 0))
        straight = beyond
    attended = attend_call(starts, queries, None, tiles, lags, attended, True)
    return mixed, attended


def solution(mesh):
    in_specs = (
        P(("groups", "tm"), "mp"),
        P(("groups", "tm"), "mp"),
        P(("groups", "tm"), "mp"),
        P(None, "mp"),
        P("mp"),
        P("mp", None, None),
        P("mp", None, None),
        P(None, "mp"),
        P("mp"),
        P("mp", None),
        P("mp", None),
        P("groups"),
    )
    out_specs = (P(("groups", "tm"), "mp"), P(("groups", "tm"), "mp"))
    return jax.shard_map(local, mesh=mesh, in_specs=in_specs, out_specs=out_specs, check_vma=False)
```

```python
import functools
import math

import jax
import jax.numpy as jnp
from jax import lax
from jax.experimental import pallas as pl
from jax.experimental.pallas import tpu as pltpu
from jax.sharding import PartitionSpec as P


HD = 256
CONV = 4
WINDOW = 2048
SCALE_ROWS = 128
DOCS = 4
SEGS = 8
MIX_GROUPS = 4
GROUP = 2
HIST = 4
LOG2E = 1.4426950408889634
LN2 = 0.6931471805599453
SINH = [-0.5 * LN2 ** (2 * k + 1) / math.factorial(2 * k + 1) for k in range(4)]
F32 = jnp.float32
BF16 = jnp.bfloat16


def ring(x, lag):
    n = lax.axis_size("tm")
    return lax.ppermute(x, "tm", [(i, (i + lag) % n) for i in range(n)])


def swap(x):
    n = lax.axis_size("tm")
    return lax.ppermute(x, "tm", [(i, i ^ 1) for i in range(n)])


def partner(x):
    return lax.ppermute(x, "mp", [(0, 1), (1, 0)])


def dequantized(panel, scale):
    rows = panel.shape[0]
    parts = []
    for g in range(rows // SCALE_ROWS):
        part = panel[g * SCALE_ROWS : (g + 1) * SCALE_ROWS, :].astype(F32)
        parts.append((part * scale[g : g + 1, :]).astype(BF16))
    return jnp.concatenate(parts, 0)


def recur_kernel(
    starts_ref,
    x_hbm,
    halo_all,
    cw_hbm,
    cb_hbm,
    panel_hbm,
    scale_hbm,
    gb_hbm,
    rate_hbm,
    h_ref,
    p_ref,
    ends_ref,
    tot_ref,
    keep,
    xs,
    co,
    gate,
    x_buf,
    panel_buf,
    cw_all,
    cb_all,
    scale_all,
    gb_all,
    rate_all,
    sems,
    small_sems,
):
    blocks, width, _ = panel_hbm.shape
    rows = x_hbm.shape[0]
    seg_len = rows // SEGS
    base = lax.axis_index("tm") * rows

    def fetch_x(b):
        at = pl.ds(pl.multiple_of(b * width, width), width)
        return pltpu.make_async_copy(x_hbm.at[:, at], x_buf.at[b % 2], sems.at[0, b % 2])

    def fetch_panel(b):
        return pltpu.make_async_copy(panel_hbm.at[b], panel_buf.at[b % 2], sems.at[1, b % 2])

    fetch_x(0).start()
    fetch_panel(0).start()
    sources = (cw_hbm, cb_hbm, scale_hbm, gb_hbm, rate_hbm)
    targets = (cw_all, cb_all, scale_all, gb_all, rate_all)
    smalls = [
        pltpu.make_async_copy(src, dst, small_sems.at[k]) for k, (src, dst) in enumerate(zip(sources, targets))
    ]
    for copy in smalls:
        copy.start()

    def fill(i, carry):
        pos = base + i - 2 + seg_len * lax.broadcasted_iota(jnp.int32, (SEGS, 128), 0)
        hit = pos == starts_ref[0]
        for d in range(1, DOCS):
            hit = hit | (pos == starts_ref[d])
        keep[pl.ds(pl.multiple_of(i * SEGS, SEGS), SEGS), :] = jnp.where(hit, 0.0, 1.0)
        return carry

    lax.fori_loop(0, seg_len + 2, fill, 0)
    for copy in smalls:
        copy.wait()

    def block(b, z):
        fetch_x(b).wait()
        fetch_panel(b).wait()

        @pl.when(b + 1 < blocks)
        def _():
            fetch_x(b + 1).start()
            fetch_panel(b + 1).start()

        wide = pl.ds(pl.multiple_of(b * width, width), width)
        recur_block(
            b,
            x_buf.at[b % 2],
            halo_all.at[:, wide],
            cw_all.at[:, wide],
            cb_all.at[:, wide],
            panel_buf[b % 2],
            scale_all[b],
            gb_all.at[:, wide],
            rate_all.at[:, wide],
            h_ref,
            p_ref,
            ends_ref.at[:, :, wide],
            tot_ref.at[:, wide],
            keep,
            xs,
            co,
            gate,
        )
        return z

    lax.fori_loop(0, blocks, block, 0)


def recur_block(
    b,
    x_ref,
    halo_ref,
    cw_ref,
    cb_ref,
    panel,
    scale,
    gb_ref,
    rate_ref,
    h_ref,
    p_ref,
    ends_ref,
    tot_ref,
    keep,
    xs,
    co,
    gate,
):
    rows, width = x_ref.shape
    seg_len = rows // SEGS
    pitch = seg_len + HIST
    for c in range(width // 128):
        lanes = slice(c * 128, (c + 1) * 128)
        xs[c, HIST + 1 : 2 * HIST, :] = halo_ref[:, lanes].astype(F32)
        for s in range(1, SEGS):
            past = x_ref[s * seg_len - 2 * HIST : s * seg_len, lanes].astype(F32)
            xs[c, s * pitch : s * pitch + 2 * HIST, :] = past
        for s in range(SEGS):
            rest = x_ref[s * seg_len : (s + 1) * seg_len, lanes].astype(F32)
            xs[c, s * pitch + 2 * HIST : (s + 1) * pitch + HIST, :] = rest

    def mask(i):
        m = keep[pl.ds(pl.multiple_of((i + 2) * SEGS, SEGS), SEGS), :]
        return jnp.concatenate([m] * (width // 128), 1)

    def row(i):
        return jnp.concatenate(
            [xs[c, pl.ds(2 * HIST + i, SEGS, stride=pitch), :] for c in range(width // 128)], 1
        )

    w = [jnp.broadcast_to(cw_ref[j : j + 1, :], (SEGS, width)) for j in range(CONV)]
    bias = jnp.broadcast_to(cb_ref[...], (SEGS, width))

    def conv_step(i, carry):
        a, b, c = carry
        x = row(i)
        m = mask(i)
        d = w[0] * x + m * c + bias
        c = w[1] * x + m * b
        b = w[2] * x + m * a
        a = w[3] * x
        return (a, b, c), d

    x3, x2, x1 = row(-3), row(-2), row(-1)
    a1 = w[3] * x1
    b1 = w[2] * x1 + mask(-1) * (w[3] * x2)
    c1 = w[1] * x1 + mask(-1) * (w[2] * x2 + mask(-2) * (w[3] * x3))

    def conv_pair(k, carry):
        carry, d0 = conv_step(2 * k, carry)
        carry, d1 = conv_step(2 * k + 1, carry)
        d = jnp.concatenate([d0, d1], 0).astype(BF16)
        for c in range(width // 128):
            co[c, pl.ds(pl.multiple_of(k * 2 * SEGS, 2 * SEGS), 2 * SEGS), :] = d[:, c * 128 : (c + 1) * 128]
        return carry

    lax.fori_loop(0, seg_len // 2, conv_pair, (a1, b1, c1), unroll=8)

    weight = dequantized(panel, scale) * BF16(0.5)
    conv_out = jnp.concatenate([co[c] for c in range(width // 128)], 1)
    gate[...] = jnp.dot(conv_out, weight, preferred_element_type=F32)

    bias_r = jnp.broadcast_to(gb_ref[0:1, :] * 0.5, (SEGS, width))
    bias_i = jnp.broadcast_to(gb_ref[1:2, :] * 0.5, (SEGS, width))
    rate4 = jnp.broadcast_to(rate_ref[...] * (-4.0 * LOG2E), (SEGS, width))

    def scan_step(i, conv, carry):
        h, p = carry
        at = pl.ds(pl.multiple_of(i * SEGS, SEGS), SEGS)
        m = mask(i)
        v = rate4 * (1.0 + jnp.tanh(gate[at, :width] + bias_r))
        ti = 1.0 + jnp.tanh(gate[at, width:] + bias_i)
        decay = jnp.exp2(v)
        s = v * v
        series = ((s * SINH[3] + SINH[2]) * s + SINH[1]) * s + SINH[0]
        quarter = decay * (v * series)
        half = quarter * lax.rsqrt(jnp.maximum(quarter, 1e-37))
        half = jnp.where(m > 0.0, half, 0.5)
        decay = decay * m
        h = decay * h + ti * (conv * half)
        p = p * decay
        for c in range(width // 128):
            h_ref[b * (width // 128) + c, at, :] = h[:, c * 128 : (c + 1) * 128]
            p_ref[b * (width // 128) + c, at, :] = p[:, c * 128 : (c + 1) * 128]
        return h, p

    def scan_pair(k, carry):
        at = pl.ds(pl.multiple_of(k * 2 * SEGS, 2 * SEGS), 2 * SEGS)
        conv = jnp.concatenate([co[c, at, :].astype(F32) for c in range(width // 128)], 1)
        carry = scan_step(2 * k, conv[:SEGS], carry)
        return scan_step(2 * k + 1, conv[SEGS:], carry)

    h, p = lax.fori_loop(
        0,
        seg_len // 2,
        scan_pair,
        (jnp.zeros((SEGS, width), F32), jnp.ones((SEGS, width), F32)),
        unroll=8,
    )
    ends_ref[0] = p
    ends_ref[1] = h
    tp, th = p[0:1], h[0:1]
    for s in range(1, SEGS):
        th = p[s : s + 1] * th + h[s : s + 1]
        tp = tp * p[s : s + 1]
    tot_ref[0:1, :] = tp
    tot_ref[1:2, :] = th


def level_kernel(tot_ref, near_ref, level_ref):
    odd = lax.axis_index("tm") % 2 == 1
    tot, near = tot_ref[...], near_ref[...]
    lower = jnp.where(odd, near, tot)
    upper = jnp.where(odd, tot, near)
    level_ref[0:1, :] = lower[0:1] * upper[0:1]
    level_ref[1:2, :] = upper[0:1] * lower[1:2] + upper[1:2]


def ready_kernel(h_ref, p_ref, y_ref, panel_ref, scale_ref, hg_ref, pg_ref, w_ref):
    rows, channels = y_ref.shape
    seg_len = rows // SEGS
    width = MIX_GROUPS * SCALE_ROWS

    def natural(ref, c, s):
        return jnp.concatenate(
            [ref[c, pl.ds(s + k * 8 * SEGS, 8, stride=SEGS), :] for k in range(seg_len // 8)], 0
        )

    def body(g, z):
        wide = pl.ds(pl.multiple_of(g * width, width), width)
        table = scale_ref[...]
        index = lax.broadcasted_iota(jnp.int32, table.shape, 0) - g * MIX_GROUPS
        scale = [jnp.sum(jnp.where(index == k, table, 0.0), axis=0, keepdims=True) for k in range(MIX_GROUPS)]
        w_ref[wide, :] = dequantized(panel_ref[wide, :], jnp.concatenate(scale, 0))
        for s in range(SEGS):
            at = slice(s * seg_len, (s + 1) * seg_len)
            y = y_ref[at, wide].astype(F32)
            inner = y * (0.7978845608028654 + (0.7978845608028654 * 0.044715) * (y * y))
            gelu = (0.5 * y) * (1.0 + jnp.tanh(inner))
            for c in range(width // 128):
                lanes = pl.ds(pl.multiple_of(g * width + c * 128, 128), 128)
                part = gelu[:, c * 128 : (c + 1) * 128]
                hg_ref[at, lanes] = natural(h_ref, g * (width // 128) + c, s) * part
                pg_ref[at, lanes] = natural(p_ref, g * (width // 128) + c, s) * part
        return z

    lax.fori_loop(0, channels // width, body, 0)


def mix_kernel(levels, hg_ref, pg_ref, w_ref, ends_ref, near_ref, *refs):
    past, (mixed_hbm, kv_ref, stage, sems) = refs[:levels], refs[levels:]
    rows, channels = hg_ref.shape
    seg_len = rows // SEGS
    width = MIX_GROUPS * SCALE_ROWS
    me = lax.axis_index("tm")
    kv_ref[...] = jnp.zeros_like(kv_ref)

    def outgoing(g):
        wide = pl.ds(pl.multiple_of(g * width, width), width)
        return pltpu.make_async_copy(stage.at[g], mixed_hbm.at[:, wide], sems.at[g])

    def body(g, z):
        wide = pl.ds(pl.multiple_of(g * width, width), width)
        c = jnp.zeros((1, width), F32)
        for k in range(levels, 0, -1):
            c = jnp.where(me >= 2 * k, past[k - 1][0:1, wide] * c + past[k - 1][1:2, wide], 0.0)
        c = jnp.where(me % 2 == 1, near_ref[0:1, wide] * c + near_ref[1:2, wide], c)
        for s in range(SEGS):
            at = slice(s * seg_len, (s + 1) * seg_len)
            stage[g, at, :] = (hg_ref[at, wide] + pg_ref[at, wide] * c).astype(BF16)
            c = ends_ref[0, s : s + 1, wide] * c + ends_ref[1, s : s + 1, wide]
        outgoing(g).start()
        kv_ref[...] += jnp.dot(stage[g], w_ref[wide, :], preferred_element_type=F32)
        return z

    def drain(g, z):
        outgoing(g).wait()
        return z

    lax.fori_loop(0, channels // width, body, 0)
    lax.fori_loop(0, channels // width, drain, 0)


def sum_kernel(a_ref, b_ref, own_ref, half_ref):
    both = a_ref[...] + b_ref[...]
    n = both.shape[0] // 2
    core = lax.axis_index("mp")
    for side in range(2):
        keys = both[side * n : (side + 1) * n, :HD].T.astype(BF16)
        values = both[side * n : (side + 1) * n, HD:].astype(BF16)
        own_ref[side, :HD, :] = keys
        own_ref[side, HD:, :] = values
    half_ref[...] = own_ref[core]


def attend_kernel(own, lags, final, heads, starts_ref, q_ref, *refs):
    refs = list(refs)
    take = lambda n: [refs.pop(0) for _ in range(n)]
    own_ref = take(1)[0] if own else None
    pairs = [take(2) for _ in lags]
    prev = None if own else take(3)
    out = take(1)[0] if final else None
    acc, m_ref, l_ref = (None, None, None) if final else take(3)
    low, score, top = take(3)
    if final:
        acc, m_ref, l_ref, stage, sems = take(5)
    prob, l_new = (None, None) if own else take(2)
    rows = q_ref.shape[0]
    half = rows // 2
    me = lax.axis_index("tm")
    first = me * rows
    core = lax.axis_index("mp")
    turn = 2 * (me % 2) - 1
    scale = LOG2E / math.sqrt(HD)

    def lowest(t):
        d0 = jnp.maximum(t - (WINDOW - 1), 0)
        for d in range(DOCS):
            d0 = jnp.maximum(d0, jnp.where(starts_ref[d] <= t, starts_ref[d], 0))
        return d0

    lo_first = lowest(first)
    lo_last = lowest(first + rows - 1)
    tiles = [(None, first)] if own else []
    for k, (even_part, odd_part) in enumerate(lags):
        tiles.append((pairs[k], first - (even_part + odd_part * turn) * rows))
    live = [None if pair is None else (start >= 0) & (start < first) & (start + rows > lo_first) for pair, start in tiles]

    def keys_of(pair, t):
        return own_ref[t, :HD, :] if pair is None else pair[t][:HD, :]

    def values_of(pair, t):
        return own_ref[t, HD:, :] if pair is None else pair[t][HD:, :]

    def lanes(g, h, n):
        return pl.ds(pl.multiple_of((g * GROUP + h) * n, n), n)

    def kept(g, h, n):
        return slice(h * n, (h + 1) * n) if final else lanes(g, h, n)

    def score_pass(g, j, pair, start, masked):
        for h in range(GROUP):
            for t in range(2):
                r0 = half * t if pair is None else 0
                at = slice(r0, rows)
                s = jnp.dot(q_ref[at, lanes(g, h, HD)], keys_of(pair, t), preferred_element_type=F32)
                peak = top[h, at, :]
                for c in range(half // 128):
                    part = s[:, c * 128 : (c + 1) * 128] * scale
                    if masked:
                        side = t if pair is None else jnp.where(core == t, 0, 1)
                        kpos = lax.broadcasted_iota(jnp.int32, part.shape, 1) + (start + side * half + c * 128)
                        ok = kpos >= low[at, :]
                        if pair is None:
                            ok = ok & (kpos <= lax.broadcasted_iota(jnp.int32, part.shape, 0) + (first + r0))
                        part = jnp.where(ok, part, -1e30)
                    score[j, h, t, at, c * 128 : (c + 1) * 128] = part
                    peak = jnp.maximum(peak, part)
                top[h, at, :] = peak

    def value_pass(g, j, pair):
        for h in range(GROUP):
            spans = [(0, half, 1), (half, rows, 2)] if pair is None else [(0, rows, 2)]
            for r0, r1, n in spans:
                at = slice(r0, r1)
                m = m_ref[at, kept(g, h, 128)]
                total = l_ref[at, kept(g, h, 128)]
                ps, vs = [], []
                for t in range(n):
                    for c in range(half // 128):
                        p = jnp.exp2(score[j, h, t, at, c * 128 : (c + 1) * 128] - m)
                        total = total + p
                        ps.append(p.astype(BF16))
                    vs.append(values_of(pair, t))
                l_ref[at, kept(g, h, 128)] = total
                acc[at, kept(g, h, HD)] += jnp.dot(
                    jnp.concatenate(ps, 1), jnp.concatenate(vs, 0), preferred_element_type=F32
                )

    def spread(x):
        return jnp.concatenate([x] * (HD // 128), 1)

    def update(g):
        top[...] = jnp.full(top.shape, -1e30, F32)
        for j, (pair, start) in enumerate(tiles):
            if pair is None:
                score_pass(g, j, pair, start, True)
                continue

            @pl.when(live[j] & (start >= lo_last))
            def _(j=j, pair=pair, start=start):
                score_pass(g, j, pair, start, False)

            @pl.when(live[j] & (start < lo_last))
            def _(j=j, pair=pair, start=start):
                score_pass(g, j, pair, start, True)

        for h in range(GROUP):
            m = jnp.broadcast_to(jnp.max(top[h], axis=1, keepdims=True), (rows, 128))
            if own:
                l_ref[:, kept(g, h, 128)] = jnp.zeros((rows, 128), F32)
                acc[:, kept(g, h, HD)] = jnp.zeros((rows, HD), F32)
            else:
                m0 = prev[1][:, lanes(g, h, 128)]
                m = jnp.maximum(m, m0)
                fade = jnp.exp2(m0 - m)
                l_ref[:, kept(g, h, 128)] = prev[2][:, lanes(g, h, 128)] * fade
                acc[:, kept(g, h, HD)] = prev[0][:, lanes(g, h, HD)] * spread(fade)
            m_ref[:, kept(g, h, 128)] = m
        for j, (pair, start) in enumerate(tiles):
            if pair is None:
                value_pass(g, j, pair)
                continue

            @pl.when(live[j])
            def _(j=j, pair=pair):
                value_pass(g, j, pair)

    def loop(fn):
        def body(g, z):
            fn(g)
            return z

        lax.fori_loop(0, heads // GROUP, body, 0)

    def start_up():
        low[...] = lowest(first + lax.broadcasted_iota(jnp.int32, (rows, 128), 0))

    if own:
        start_up()
        loop(update)
        return

    def exp_pass(g, j, pair, start, masked):
        for h in range(GROUP):
            m = prev[1][:, lanes(g, h, 128)]
            total = l_new[:, lanes(g, h, 128)]
            for t in range(2):
                s = jnp.dot(q_ref[:, lanes(g, h, HD)], keys_of(pair, t), preferred_element_type=F32)
                for c in range(half // 128):
                    part = s[:, c * 128 : (c + 1) * 128] * scale
                    if masked:
                        side = jnp.where(core == t, 0, 1)
                        kpos = lax.broadcasted_iota(jnp.int32, part.shape, 1) + (start + side * half + c * 128)
                        part = jnp.where(kpos >= low[...], part, -1e30)
                    p = jnp.exp2(part - m)
                    total = total + p
                    prob[j, g * GROUP + h, (t * half) // 128 + c] = p.astype(BF16)
            l_new[:, lanes(g, h, 128)] = total

    def weighted(g, h, j, pair):
        values = jnp.concatenate([values_of(pair, t) for t in range(2)], 0)
        shares = jnp.concatenate([prob[j, g * GROUP + h, c] for c in range(rows // 128)], 1)
        return jnp.dot(shares, values, preferred_element_type=F32)

    def exp_all(g):
        for j, (pair, start) in enumerate(tiles):

            @pl.when(live[j] & (start >= lo_last))
            def _(j=j, pair=pair, start=start):
                exp_pass(g, j, pair, start, False)

            @pl.when(live[j] & (start < lo_last))
            def _(j=j, pair=pair, start=start):
                exp_pass(g, j, pair, start, True)

    any_live = functools.reduce(jnp.logical_or, live)

    @pl.when(any_live)
    def _():
        start_up()
        l_new[...] = prev[2][...]
        loop(exp_all)

    within = jnp.max(l_new[...]) <= 2.0**64
    fast = any_live & within
    slow = any_live & jnp.logical_not(within)

    if not final:

        def add_all(g):
            for j, (pair, start) in enumerate(tiles):

                @pl.when(live[j])
                def _(j=j, pair=pair):
                    for h in range(GROUP):
                        acc[:, lanes(g, h, HD)] += weighted(g, h, j, pair)

        @pl.when(fast)
        def _():
            l_ref[...] = l_new[...]
            loop(add_all)

        @pl.when(slow)
        def _():
            loop(update)

        return

    def outgoing(g):
        wide = pl.ds(pl.multiple_of(g * GROUP * HD, GROUP * HD), GROUP * HD)
        return pltpu.make_async_copy(stage.at[g], out.at[:, wide], sems.at[g])

    def settle(g, h, top_sum, below):
        share = jnp.broadcast_to(1.0 / jnp.sum(below, axis=1, keepdims=True), (rows, 128))
        stage[g, :, h * HD : (h + 1) * HD] = (top_sum * spread(share)).astype(BF16)

    def finish(g):
        @pl.when(fast)
        def _():
            for h in range(GROUP):
                sums = prev[0][:, lanes(g, h, HD)] + weighted(g, h, 0, tiles[0][0])
                settle(g, h, sums, l_new[:, lanes(g, h, 128)])

        @pl.when(slow)
        def _():
            update(g)
            for h in range(GROUP):
                settle(g, h, acc[:, kept(g, h, HD)], l_ref[:, kept(g, h, 128)])

        @pl.when(jnp.logical_not(any_live))
        def _():
            for h in range(GROUP):
                settle(g, h, prev[0][:, lanes(g, h, HD)], prev[2][:, lanes(g, h, 128)])

        outgoing(g).start()

    loop(finish)
    loop(lambda g: outgoing(g).wait())


def recur_call(starts, x, halo, *params):
    rows, channels = x.shape
    _, width, _ = params[2].shape
    conv_weight, conv_bias, _, gate_scale, gate_bias, decay_rate = params
    vmem = pl.BlockSpec(memory_space=pltpu.VMEM)
    hbm = pl.BlockSpec(memory_space=pl.ANY)
    return pl.pallas_call(
        recur_kernel,
        in_specs=[pl.BlockSpec(memory_space=pltpu.SMEM), hbm, vmem] + [hbm] * 6,
        out_specs=[vmem] * 4,
        scratch_shapes=[
            pltpu.VMEM((rows + 2 * SEGS, 128), F32),
            pltpu.VMEM((width // 128, rows + HIST * (SEGS + 1), 128), F32),
            pltpu.VMEM((width // 128, rows, 128), BF16),
            pltpu.VMEM((rows, 2 * width), F32),
            pltpu.VMEM((2, rows, width), BF16),
            pltpu.VMEM((2, width, 2 * width), BF16),
        ]
        + [pltpu.VMEM(a.shape, F32) for a in (conv_weight, conv_bias, gate_scale, gate_bias, decay_rate)]
        + [pltpu.SemaphoreType.DMA((2, 2)), pltpu.SemaphoreType.DMA((5,))],
        out_shape=[
            jax.ShapeDtypeStruct((channels // 128, rows, 128), F32),
            jax.ShapeDtypeStruct((channels // 128, rows, 128), F32),
            jax.ShapeDtypeStruct((2, SEGS, channels), F32),
            jax.ShapeDtypeStruct((2, channels), F32),
        ],
        compiler_params=pltpu.CompilerParams(vmem_limit_bytes=20 << 20),
        name="recur",
    )(starts, x, halo, *params)


def level_call(tot, near):
    return pl.pallas_call(
        level_kernel,
        out_shape=jax.ShapeDtypeStruct(tot.shape, F32),
        compiler_params=pltpu.CompilerParams(vmem_limit_bytes=1 << 20),
        name="level",
    )(tot, near)


def ready_call(h, p, y, kv_panel, kv_scale):
    rows, channels = y.shape
    vmem = pl.BlockSpec(memory_space=pltpu.VMEM)
    flat = jax.ShapeDtypeStruct((rows, channels), F32)
    return pl.pallas_call(
        ready_kernel,
        in_specs=[vmem] * 5,
        out_specs=[vmem] * 3,
        out_shape=[flat, flat, jax.ShapeDtypeStruct(kv_panel.shape, BF16)],
        cost_estimate=pl.CostEstimate(flops=1 << 24, bytes_accessed=1 << 22, transcendentals=rows * channels),
        compiler_params=pltpu.CompilerParams(vmem_limit_bytes=4 << 20),
        name="ready",
    )(h, p, y, kv_panel, kv_scale)


def mix_call(hg, pg, weight, ends, near, past):
    rows, channels = hg.shape
    out = weight.shape[1]
    width = MIX_GROUPS * SCALE_ROWS
    vmem = pl.BlockSpec(memory_space=pltpu.VMEM)
    return pl.pallas_call(
        functools.partial(mix_kernel, len(past)),
        in_specs=[vmem] * (5 + len(past)),
        out_specs=[pl.BlockSpec(memory_space=pl.ANY), vmem],
        out_shape=[jax.ShapeDtypeStruct((rows, channels), BF16), jax.ShapeDtypeStruct((rows, out), F32)],
        scratch_shapes=[
            pltpu.VMEM((channels // width, rows, width), BF16),
            pltpu.SemaphoreType.DMA((channels // width,)),
        ],
        compiler_params=pltpu.CompilerParams(vmem_limit_bytes=8 << 20),
        name="mix",
    )(hg, pg, weight, ends, near, *past)


def sum_call(a, b):
    rows, _ = a.shape
    half = rows // 2
    return pl.pallas_call(
        sum_kernel,
        out_shape=[
            jax.ShapeDtypeStruct((2, 2 * HD, half), BF16),
            jax.ShapeDtypeStruct((2 * HD, half), BF16),
        ],
        compiler_params=pltpu.CompilerParams(vmem_limit_bytes=16 << 20),
        name="kvsum",
    )(a, b)


def attend_call(starts, q, own, halves, lags, prev, final):
    rows, width = q.shape
    heads = width // HD
    held = [] if own is None else [own]
    held += halves
    held += prev or []
    tiles = len(lags) + (own is not None)
    vmem = pl.BlockSpec(memory_space=pltpu.VMEM)
    scratch = [
        pltpu.VMEM((rows, 128), jnp.int32),
        pltpu.VMEM((tiles, GROUP, 2, rows, rows // 2), F32),
        pltpu.VMEM((GROUP, rows, 128), F32),
    ]
    aliases = {}
    if final:
        out_specs = pl.BlockSpec(memory_space=pl.ANY)
        out_shape = jax.ShapeDtypeStruct((rows, width), BF16)
        scratch += [pltpu.VMEM((rows, GROUP * n), F32) for n in (HD, 128, 128)]
        scratch += [pltpu.VMEM((heads // GROUP, rows, GROUP * HD), BF16), pltpu.SemaphoreType.DMA((heads // GROUP,))]
    if own is None:
        scratch += [
            pltpu.VMEM((tiles, heads, rows // 128, rows, 128), BF16),
            pltpu.VMEM((rows, heads * 128), F32),
        ]
    if not final:
        out_specs = [vmem] * 3
        out_shape = [jax.ShapeDtypeStruct((rows, heads * n), F32) for n in (HD, 128, 128)]
        if prev:
            aliases = {2 + len(halves) + k: k for k in range(3)}
    return pl.pallas_call(
        functools.partial(attend_kernel, own is not None, lags, final, heads),
        in_specs=[pl.BlockSpec(memory_space=pltpu.SMEM), vmem] + [vmem] * len(held),
        out_specs=out_specs,
        scratch_shapes=scratch,
        out_shape=out_shape,
        input_output_aliases=aliases,
        cost_estimate=pl.CostEstimate(
            flops=4 * tiles * rows * rows * width,
            bytes_accessed=4 * rows * width,
            transcendentals=tiles * rows * rows * heads,
        ),
        compiler_params=pltpu.CompilerParams(vmem_limit_bytes=32 << 20),
        name="attend_own" if own is not None else "attend_end" if final else "attend_mid",
    )(starts, q, *held)


def local(
    branch_x,
    branch_y,
    queries,
    conv_weight,
    conv_bias,
    gate_panel,
    gate_scale,
    gate_bias,
    decay_rate,
    kv_panel,
    kv_scale,
    segment_ids,
):
    rows = branch_x.shape[0]
    seq = segment_ids.shape[0]
    halo = ring(branch_x[rows - CONV + 1 :], 1)
    starts = jnp.sum(
        (segment_ids[None, :] < jnp.arange(DOCS, dtype=jnp.int32)[:, None]).astype(jnp.int32), axis=1
    )
    stay = lambda a: pltpu.with_memory_space_constraint(a, pltpu.HBM)
    h, p, ends, tot = recur_call(
        starts,
        stay(branch_x),
        halo,
        stay(conv_weight),
        stay(conv_bias[None]),
        stay(gate_panel),
        stay(gate_scale),
        stay(gate_bias),
        stay(decay_rate[None]),
    )
    near = swap(tot)
    hg, pg, weight = ready_call(h, p, branch_y, kv_panel, kv_scale)
    level = level_call(tot, near)
    levels = -(-(seq // 2) // (2 * rows))
    past = [ring(level, 2 * k) for k in range(1, levels + 1)]
    mixed, partial_kv = mix_call(hg, pg, weight, ends, near, past)
    own, half = sum_call(partial_kv, partner(partial_kv))

    levels = -(-WINDOW // rows) // 2
    straight, attended = half, None
    for k in range(levels + 1):
        last = k == levels
        beyond = None if last else ring(straight, 2)
        crossed = swap(straight)
        if k == 0:
            attended = attend_call(starts, queries, own, [], [], None, False)
        else:
            attended = attend_call(starts, queries, None, tiles, lags, attended, False)
        tiles, lags = [crossed, partner(crossed)], [(2 * k, 1)]
        if not last:
            tiles += [beyond, partner(beyond)]
            lags.append((2 * k + 2, 0))
        straight = beyond
    attended = attend_call(starts, queries, None, tiles, lags, attended, True)
    return mixed, attended


def solution(mesh):
    in_specs = (
        P(("groups", "tm"), "mp"),
        P(("groups", "tm"), "mp"),
        P(("groups", "tm"), "mp"),
        P(None, "mp"),
        P("mp"),
        P("mp", None, None),
        P("mp", None, None),
        P(None, "mp"),
        P("mp"),
        P("mp", None),
        P("mp", None),
        P("groups"),
    )
    out_specs = (P(("groups", "tm"), "mp"), P(("groups", "tm"), "mp"))
    return jax.shard_map(local, mesh=mesh, in_specs=in_specs, out_specs=out_specs, check_vma=False)
```

```python
import functools
import math

import jax
import jax.numpy as jnp
from jax import lax
from jax.experimental import pallas as pl
from jax.experimental.pallas import tpu as pltpu
from jax.sharding import PartitionSpec as P


HD = 256
CONV = 4
WINDOW = 2048
SCALE_ROWS = 128
DOCS = 4
SEGS = 8
MIX_GROUPS = 4
GROUP = 2
CHUNK = 16
HIST = 4
LOG2E = 1.4426950408889634
LN2 = 0.6931471805599453
SPAN = 0.16
SINH = [
    -0.5 * LN2 * (1.0 + SPAN**3 / (32 * 5040)),
    -0.5 * LN2**3 * (1.0 / 6 - 9 * SPAN**2 / (16 * 5040)),
    -0.5 * LN2**5 * (1.0 / 120 + 1.5 * SPAN / 5040),
]
F32 = jnp.float32
BF16 = jnp.bfloat16


def ring(x, lag):
    n = lax.axis_size("tm")
    return lax.ppermute(x, "tm", [(i, (i + lag) % n) for i in range(n)])


def swap(x):
    n = lax.axis_size("tm")
    return lax.ppermute(x, "tm", [(i, i ^ 1) for i in range(n)])


def partner(x):
    return lax.ppermute(x, "mp", [(0, 1), (1, 0)])


def dequantized(panel, scale):
    rows = panel.shape[0]
    parts = []
    for g in range(rows // SCALE_ROWS):
        part = panel[g * SCALE_ROWS : (g + 1) * SCALE_ROWS, :].astype(F32)
        parts.append((part * scale[g : g + 1, :]).astype(BF16))
    return jnp.concatenate(parts, 0)


def recur_kernel(
    starts_ref,
    x_hbm,
    halo_all,
    cw_hbm,
    cb_hbm,
    panel_hbm,
    scale_hbm,
    gb_hbm,
    rate_hbm,
    h_ref,
    p_ref,
    ends_ref,
    tot_ref,
    keep,
    xs,
    co,
    gate,
    x_buf,
    panel_buf,
    cw_all,
    cb_all,
    scale_all,
    gb_all,
    rate_all,
    sems,
    small_sems,
):
    blocks, width, _ = panel_hbm.shape
    rows = x_hbm.shape[0]
    seg_len = rows // SEGS
    base = lax.axis_index("tm") * rows

    def fetch_x(b):
        at = pl.ds(pl.multiple_of(b * width, width), width)
        return pltpu.make_async_copy(x_hbm.at[:, at], x_buf.at[b % 2], sems.at[0, b % 2])

    def fetch_panel(b):
        return pltpu.make_async_copy(panel_hbm.at[b], panel_buf.at[b % 2], sems.at[1, b % 2])

    fetch_x(0).start()
    fetch_panel(0).start()
    sources = (cw_hbm, cb_hbm, scale_hbm, gb_hbm, rate_hbm)
    targets = (cw_all, cb_all, scale_all, gb_all, rate_all)
    smalls = [
        pltpu.make_async_copy(src, dst, small_sems.at[k]) for k, (src, dst) in enumerate(zip(sources, targets))
    ]
    for copy in smalls:
        copy.start()

    def fill(i, carry):
        pos = base + i - 2 + seg_len * lax.broadcasted_iota(jnp.int32, (SEGS, 128), 0)
        hit = pos == starts_ref[0]
        for d in range(1, DOCS):
            hit = hit | (pos == starts_ref[d])
        keep[pl.ds(pl.multiple_of(i * SEGS, SEGS), SEGS), :] = jnp.where(hit, 0.0, 1.0)
        return carry

    lax.fori_loop(0, seg_len + 2, fill, 0)
    for copy in smalls:
        copy.wait()

    def hit(k):
        found = False
        for d in range(DOCS):
            off = starts_ref[d] - base
            found = found | ((off >= 0) & (off < rows) & ((off % seg_len) // CHUNK == k))
        return found

    def block(b, z):
        fetch_x(b).wait()
        fetch_panel(b).wait()

        @pl.when(b + 1 < blocks)
        def _():
            fetch_x(b + 1).start()
            fetch_panel(b + 1).start()

        wide = pl.ds(pl.multiple_of(b * width, width), width)
        recur_block(
            hit,
            b,
            x_buf.at[b % 2],
            halo_all.at[:, wide],
            cw_all.at[:, wide],
            cb_all.at[:, wide],
            panel_buf[b % 2],
            scale_all[b],
            gb_all.at[:, wide],
            rate_all.at[:, wide],
            h_ref,
            p_ref,
            ends_ref.at[:, :, wide],
            tot_ref.at[:, wide],
            keep,
            xs,
            co,
            gate,
        )
        return z

    lax.fori_loop(0, blocks, block, 0)


def recur_block(
    hit,
    b,
    x_ref,
    halo_ref,
    cw_ref,
    cb_ref,
    panel,
    scale,
    gb_ref,
    rate_ref,
    h_ref,
    p_ref,
    ends_ref,
    tot_ref,
    keep,
    xs,
    co,
    gate,
):
    rows, width = x_ref.shape
    seg_len = rows // SEGS
    pitch = seg_len + HIST
    for c in range(width // 128):
        lanes = slice(c * 128, (c + 1) * 128)
        xs[c, HIST + 1 : 2 * HIST, :] = halo_ref[:, lanes].astype(F32)
        for s in range(1, SEGS):
            past = x_ref[s * seg_len - 2 * HIST : s * seg_len, lanes].astype(F32)
            xs[c, s * pitch : s * pitch + 2 * HIST, :] = past
        for s in range(SEGS):
            rest = x_ref[s * seg_len : (s + 1) * seg_len, lanes].astype(F32)
            xs[c, s * pitch + 2 * HIST : (s + 1) * pitch + HIST, :] = rest

    def mask(i):
        m = keep[pl.ds(pl.multiple_of((i + 2) * SEGS, SEGS), SEGS), :]
        return jnp.concatenate([m] * (width // 128), 1)

    def row(i):
        return jnp.concatenate(
            [xs[c, pl.ds(2 * HIST + i, SEGS, stride=pitch), :] for c in range(width // 128)], 1
        )

    w = [jnp.broadcast_to(cw_ref[j : j + 1, :], (SEGS, width)) for j in range(CONV)]
    bias = jnp.broadcast_to(cb_ref[...], (SEGS, width))

    def chunked(step, carry):
        def chunk(masked, k, carry):
            for u in range(CHUNK // 2):
                carry = step(k * (CHUNK // 2) + u, carry, masked)
            return carry

        def body(k, carry):
            return lax.cond(hit(k), functools.partial(chunk, True), functools.partial(chunk, False), k, carry)

        return lax.fori_loop(0, seg_len // CHUNK, body, carry)

    def conv_step(i, carry, masked):
        ka, kb, kc = carry
        x = row(i)
        if masked:
            m = mask(i)
            ka, kb, kc = m * ka, m * kb, m * kc
        return (w[3] * x, w[2] * x + ka, w[1] * x + kb), w[0] * x + kc + bias

    x3, x2, x1 = row(-3), row(-2), row(-1)
    a1 = w[3] * x1
    b1 = w[2] * x1 + mask(-1) * (w[3] * x2)
    c1 = w[1] * x1 + mask(-1) * (w[2] * x2 + mask(-2) * (w[3] * x3))

    def conv_pair(k, carry, masked):
        carry, d0 = conv_step(2 * k, carry, masked)
        carry, d1 = conv_step(2 * k + 1, carry, masked)
        d = jnp.concatenate([d0, d1], 0).astype(BF16)
        for c in range(width // 128):
            co[c, pl.ds(pl.multiple_of(k * 2 * SEGS, 2 * SEGS), 2 * SEGS), :] = d[:, c * 128 : (c + 1) * 128]
        return carry

    chunked(conv_pair, (a1, b1, c1))

    weight = dequantized(panel, scale) * BF16(0.5)
    conv_out = jnp.concatenate([co[c] for c in range(width // 128)], 1)
    gate[...] = jnp.dot(conv_out, weight, preferred_element_type=F32)

    bias_r = jnp.broadcast_to(gb_ref[0:1, :] * 0.5, (SEGS, width))
    bias_i = jnp.broadcast_to(gb_ref[1:2, :] * 0.5, (SEGS, width))
    rate4 = jnp.broadcast_to(rate_ref[...] * (-4.0 * LOG2E), (SEGS, width))

    def scan_step(i, conv, carry, masked):
        h, p = carry
        at = pl.ds(pl.multiple_of(i * SEGS, SEGS), SEGS)
        v = rate4 * (1.0 + jnp.tanh(gate[at, :width] + bias_r))
        ti = 1.0 + jnp.tanh(gate[at, width:] + bias_i)
        decay = jnp.exp2(v)
        s = v * v
        series = (s * SINH[2] + SINH[1]) * s + SINH[0]
        quarter = decay * (v * series)
        half = quarter * lax.rsqrt(jnp.maximum(quarter, 1e-37))
        if masked:
            m = mask(i)
            half = jnp.where(m > 0.0, half, 0.5)
            decay = decay * m
        h = decay * h + ti * (conv * half)
        p = p * decay
        for c in range(width // 128):
            h_ref[b * (width // 128) + c, at, :] = h[:, c * 128 : (c + 1) * 128]
            p_ref[b * (width // 128) + c, at, :] = p[:, c * 128 : (c + 1) * 128]
        return h, p

    def scan_pair(k, carry, masked):
        at = pl.ds(pl.multiple_of(k * 2 * SEGS, 2 * SEGS), 2 * SEGS)
        conv = jnp.concatenate([co[c, at, :].astype(F32) for c in range(width // 128)], 1)
        carry = scan_step(2 * k, conv[:SEGS], carry, masked)
        return scan_step(2 * k + 1, conv[SEGS:], carry, masked)

    h, p = chunked(scan_pair, (jnp.zeros((SEGS, width), F32), jnp.ones((SEGS, width), F32)))
    ends_ref[0] = p
    ends_ref[1] = h
    tp, th = p[0:1], h[0:1]
    for s in range(1, SEGS):
        th = p[s : s + 1] * th + h[s : s + 1]
        tp = tp * p[s : s + 1]
    tot_ref[0:1, :] = tp
    tot_ref[1:2, :] = th


def level_kernel(tot_ref, near_ref, level_ref):
    odd = lax.axis_index("tm") % 2 == 1
    tot, near = tot_ref[...], near_ref[...]
    lower = jnp.where(odd, near, tot)
    upper = jnp.where(odd, tot, near)
    level_ref[0:1, :] = lower[0:1] * upper[0:1]
    level_ref[1:2, :] = upper[0:1] * lower[1:2] + upper[1:2]


def ready_kernel(h_ref, p_ref, y_ref, panel_ref, scale_ref, hg_ref, pg_ref, w_ref):
    rows, channels = y_ref.shape
    seg_len = rows // SEGS
    width = MIX_GROUPS * SCALE_ROWS

    def natural(ref, c, s):
        return jnp.concatenate(
            [ref[c, pl.ds(s + k * 8 * SEGS, 8, stride=SEGS), :] for k in range(seg_len // 8)], 0
        )

    def body(g, z):
        wide = pl.ds(pl.multiple_of(g * width, width), width)
        table = scale_ref[...]
        index = lax.broadcasted_iota(jnp.int32, table.shape, 0) - g * MIX_GROUPS
        scale = [jnp.sum(jnp.where(index == k, table, 0.0), axis=0, keepdims=True) for k in range(MIX_GROUPS)]
        w_ref[wide, :] = dequantized(panel_ref[wide, :], jnp.concatenate(scale, 0))
        for s in range(SEGS):
            at = slice(s * seg_len, (s + 1) * seg_len)
            y = y_ref[at, wide].astype(F32)
            inner = y * (0.7978845608028654 + (0.7978845608028654 * 0.044715) * (y * y))
            gelu = (0.5 * y) * (1.0 + jnp.tanh(inner))
            for c in range(width // 128):
                lanes = pl.ds(pl.multiple_of(g * width + c * 128, 128), 128)
                part = gelu[:, c * 128 : (c + 1) * 128]
                hg_ref[at, lanes] = natural(h_ref, g * (width // 128) + c, s) * part
                pg_ref[at, lanes] = natural(p_ref, g * (width // 128) + c, s) * part
        return z

    lax.fori_loop(0, channels // width, body, 0)


def mix_kernel(levels, hg_ref, pg_ref, w_ref, ends_ref, near_ref, *refs):
    past, (mixed_hbm, kv_ref, stage, sems) = refs[:levels], refs[levels:]
    rows, channels = hg_ref.shape
    seg_len = rows // SEGS
    width = MIX_GROUPS * SCALE_ROWS
    me = lax.axis_index("tm")
    kv_ref[...] = jnp.zeros_like(kv_ref)

    def outgoing(g):
        wide = pl.ds(pl.multiple_of(g * width, width), width)
        return pltpu.make_async_copy(stage.at[g], mixed_hbm.at[:, wide], sems.at[g])

    def body(g, z):
        wide = pl.ds(pl.multiple_of(g * width, width), width)
        c = jnp.zeros((1, width), F32)
        for k in range(levels, 0, -1):
            c = jnp.where(me >= 2 * k, past[k - 1][0:1, wide] * c + past[k - 1][1:2, wide], 0.0)
        c = jnp.where(me % 2 == 1, near_ref[0:1, wide] * c + near_ref[1:2, wide], c)
        for s in range(SEGS):
            at = slice(s * seg_len, (s + 1) * seg_len)
            stage[g, at, :] = (hg_ref[at, wide] + pg_ref[at, wide] * c).astype(BF16)
            c = ends_ref[0, s : s + 1, wide] * c + ends_ref[1, s : s + 1, wide]
        outgoing(g).start()
        kv_ref[...] += jnp.dot(stage[g], w_ref[wide, :], preferred_element_type=F32)
        return z

    def drain(g, z):
        outgoing(g).wait()
        return z

    lax.fori_loop(0, channels // width, body, 0)
    lax.fori_loop(0, channels // width, drain, 0)


def sum_kernel(a_ref, b_ref, own_ref, half_ref):
    both = a_ref[...] + b_ref[...]
    n = both.shape[0] // 2
    core = lax.axis_index("mp")
    for side in range(2):
        keys = both[side * n : (side + 1) * n, :HD].T.astype(BF16)
        values = both[side * n : (side + 1) * n, HD:].astype(BF16)
        own_ref[side, :HD, :] = keys
        own_ref[side, HD:, :] = values
    half_ref[...] = own_ref[core]


def attend_kernel(own, lags, final, heads, starts_ref, q_ref, *refs):
    refs = list(refs)
    take = lambda n: [refs.pop(0) for _ in range(n)]
    own_ref = take(1)[0] if own else None
    pairs = [take(2) for _ in lags]
    prev = None if own else take(3)
    out = take(1)[0] if final else None
    acc, m_ref, l_ref = (None, None, None) if final else take(3)
    low, score, top = take(3)
    if final:
        acc, m_ref, l_ref, stage, sems = take(5)
    prob, l_new, flag = (None, None, None) if own else take(3)
    rows = q_ref.shape[0]
    half = rows // 2
    me = lax.axis_index("tm")
    first = me * rows
    core = lax.axis_index("mp")
    turn = 2 * (me % 2) - 1
    scale = LOG2E / math.sqrt(HD)

    def lowest(t):
        d0 = jnp.maximum(t - (WINDOW - 1), 0)
        for d in range(DOCS):
            d0 = jnp.maximum(d0, jnp.where(starts_ref[d] <= t, starts_ref[d], 0))
        return d0

    lo_first = lowest(first)
    lo_last = lowest(first + rows - 1)
    tiles = [(None, first)] if own else []
    for k, (even_part, odd_part) in enumerate(lags):
        tiles.append((pairs[k], first - (even_part + odd_part * turn) * rows))
    live = [None if pair is None else (start >= 0) & (start < first) & (start + rows > lo_first) for pair, start in tiles]

    def keys_of(pair, t):
        return own_ref[t, :HD, :] if pair is None else pair[t][:HD, :]

    def values_of(pair, t):
        return own_ref[t, HD:, :] if pair is None else pair[t][HD:, :]

    def lanes(g, h, n):
        return pl.ds(pl.multiple_of((g * GROUP + h) * n, n), n)

    def kept(g, h, n):
        return slice(h * n, (h + 1) * n) if final else lanes(g, h, n)

    def score_pass(g, j, pair, start, masked):
        for h in range(GROUP):
            for t in range(2):
                r0 = half * t if pair is None else 0
                at = slice(r0, rows)
                s = jnp.dot(q_ref[at, lanes(g, h, HD)], keys_of(pair, t), preferred_element_type=F32)
                peak = top[h, at, :]
                for c in range(half // 128):
                    part = s[:, c * 128 : (c + 1) * 128] * scale
                    if masked:
                        side = t if pair is None else jnp.where(core == t, 0, 1)
                        kpos = lax.broadcasted_iota(jnp.int32, part.shape, 1) + (start + side * half + c * 128)
                        ok = kpos >= low[at, :]
                        if pair is None:
                            ok = ok & (kpos <= lax.broadcasted_iota(jnp.int32, part.shape, 0) + (first + r0))
                        part = jnp.where(ok, part, -1e30)
                    score[j, h, t, at, c * 128 : (c + 1) * 128] = part
                    peak = jnp.maximum(peak, part)
                top[h, at, :] = peak

    def value_pass(g, j, pair):
        for h in range(GROUP):
            spans = [(0, half, 1), (half, rows, 2)] if pair is None else [(0, rows, 2)]
            for r0, r1, n in spans:
                at = slice(r0, r1)
                m = m_ref[at, kept(g, h, 128)]
                total = l_ref[at, kept(g, h, 128)]
                ps, vs = [], []
                for t in range(n):
                    for c in range(half // 128):
                        p = jnp.exp2(score[j, h, t, at, c * 128 : (c + 1) * 128] - m)
                        total = total + p
                        ps.append(p.astype(BF16))
                    vs.append(values_of(pair, t))
                l_ref[at, kept(g, h, 128)] = total
                acc[at, kept(g, h, HD)] += jnp.dot(
                    jnp.concatenate(ps, 1), jnp.concatenate(vs, 0), preferred_element_type=F32
                )

    def spread(x):
        return jnp.concatenate([x] * (HD // 128), 1)

    def update(g):
        top[...] = jnp.full(top.shape, -1e30, F32)
        for j, (pair, start) in enumerate(tiles):
            if pair is None:
                score_pass(g, j, pair, start, True)
                continue

            @pl.when(live[j] & (start >= lo_last))
            def _(j=j, pair=pair, start=start):
                score_pass(g, j, pair, start, False)

            @pl.when(live[j] & (start < lo_last))
            def _(j=j, pair=pair, start=start):
                score_pass(g, j, pair, start, True)

        for h in range(GROUP):
            m = jnp.broadcast_to(jnp.max(top[h], axis=1, keepdims=True), (rows, 128))
            if own:
                l_ref[:, kept(g, h, 128)] = jnp.zeros((rows, 128), F32)
                acc[:, kept(g, h, HD)] = jnp.zeros((rows, HD), F32)
            else:
                m0 = prev[1][:, lanes(g, h, 128)]
                m = jnp.maximum(m, m0)
                fade = jnp.exp2(m0 - m)
                l_ref[:, kept(g, h, 128)] = prev[2][:, lanes(g, h, 128)] * fade
                acc[:, kept(g, h, HD)] = prev[0][:, lanes(g, h, HD)] * spread(fade)
            m_ref[:, kept(g, h, 128)] = m
        for j, (pair, start) in enumerate(tiles):
            if pair is None:
                value_pass(g, j, pair)
                continue

            @pl.when(live[j])
            def _(j=j, pair=pair):
                value_pass(g, j, pair)

    def loop(fn):
        def body(g, z):
            fn(g)
            return z

        lax.fori_loop(0, heads // GROUP, body, 0)

    def start_up():
        low[...] = lowest(first + lax.broadcasted_iota(jnp.int32, (rows, 128), 0))

    if own:
        start_up()
        loop(update)
        return

    def exp_pass(g, j, pair, start, masked):
        for h in range(GROUP):
            m = prev[1][:, lanes(g, h, 128)]
            total = l_new[:, lanes(g, h, 128)]
            for t in range(2):
                s = jnp.dot(q_ref[:, lanes(g, h, HD)], keys_of(pair, t), preferred_element_type=F32)
                for c in range(half // 128):
                    part = s[:, c * 128 : (c + 1) * 128] * scale
                    if masked:
                        side = jnp.where(core == t, 0, 1)
                        kpos = lax.broadcasted_iota(jnp.int32, part.shape, 1) + (start + side * half + c * 128)
                        part = jnp.where(kpos >= low[...], part, -1e30)
                    p = jnp.exp2(part - m)
                    total = total + p
                    prob[j, g * GROUP + h, (t * half) // 128 + c] = p.astype(BF16)
            l_new[:, lanes(g, h, 128)] = total

    def weighted(g, h, j, pair):
        values = jnp.concatenate([values_of(pair, t) for t in range(2)], 0)
        shares = jnp.concatenate([prob[j, g * GROUP + h, c] for c in range(rows // 128)], 1)
        return jnp.dot(shares, values, preferred_element_type=F32)

    def exp_all(g):
        for j, (pair, start) in enumerate(tiles):

            @pl.when(live[j] & (start >= lo_last))
            def _(j=j, pair=pair, start=start):
                exp_pass(g, j, pair, start, False)

            @pl.when(live[j] & (start < lo_last))
            def _(j=j, pair=pair, start=start):
                exp_pass(g, j, pair, start, True)

    any_live = functools.reduce(jnp.logical_or, live)

    @pl.when(any_live)
    def _():
        start_up()
        l_new[...] = prev[2][...]
        loop(exp_all)
        flag[0] = jnp.where(jnp.max(l_new[...]) <= 2.0**64, 1, 0)

    @pl.when(jnp.logical_not(any_live))
    def _():
        flag[0] = 2

    fast = flag[0] == 1
    slow = flag[0] == 0

    if not final:

        def add_all(g):
            for j, (pair, start) in enumerate(tiles):

                @pl.when(live[j])
                def _(j=j, pair=pair):
                    for h in range(GROUP):
                        acc[:, lanes(g, h, HD)] += weighted(g, h, j, pair)

        @pl.when(fast)
        def _():
            l_ref[...] = l_new[...]
            loop(add_all)

        @pl.when(slow)
        def _():
            loop(update)

        return

    def outgoing(g):
        wide = pl.ds(pl.multiple_of(g * GROUP * HD, GROUP * HD), GROUP * HD)
        return pltpu.make_async_copy(stage.at[g], out.at[:, wide], sems.at[g])

    def settle(g, h, top_sum, below):
        share = jnp.broadcast_to(1.0 / jnp.sum(below, axis=1, keepdims=True), (rows, 128))
        stage[g, :, h * HD : (h + 1) * HD] = (top_sum * spread(share)).astype(BF16)

    def finish(g):
        @pl.when(fast)
        def _():
            for h in range(GROUP):
                sums = prev[0][:, lanes(g, h, HD)] + weighted(g, h, 0, tiles[0][0])
                settle(g, h, sums, l_new[:, lanes(g, h, 128)])

        @pl.when(slow)
        def _():
            update(g)
            for h in range(GROUP):
                settle(g, h, acc[:, kept(g, h, HD)], l_ref[:, kept(g, h, 128)])

        @pl.when(jnp.logical_not(any_live))
        def _():
            for h in range(GROUP):
                settle(g, h, prev[0][:, lanes(g, h, HD)], prev[2][:, lanes(g, h, 128)])

        outgoing(g).start()

    loop(finish)
    loop(lambda g: outgoing(g).wait())


def recur_call(starts, x, halo, *params):
    rows, channels = x.shape
    _, width, _ = params[2].shape
    conv_weight, conv_bias, _, gate_scale, gate_bias, decay_rate = params
    vmem = pl.BlockSpec(memory_space=pltpu.VMEM)
    hbm = pl.BlockSpec(memory_space=pl.ANY)
    return pl.pallas_call(
        recur_kernel,
        in_specs=[pl.BlockSpec(memory_space=pltpu.SMEM), hbm, vmem] + [hbm] * 6,
        out_specs=[vmem] * 4,
        scratch_shapes=[
            pltpu.VMEM((rows + 2 * SEGS, 128), F32),
            pltpu.VMEM((width // 128, rows + HIST * (SEGS + 1), 128), F32),
            pltpu.VMEM((width // 128, rows, 128), BF16),
            pltpu.VMEM((rows, 2 * width), F32),
            pltpu.VMEM((2, rows, width), BF16),
            pltpu.VMEM((2, width, 2 * width), BF16),
        ]
        + [pltpu.VMEM(a.shape, F32) for a in (conv_weight, conv_bias, gate_scale, gate_bias, decay_rate)]
        + [pltpu.SemaphoreType.DMA((2, 2)), pltpu.SemaphoreType.DMA((5,))],
        out_shape=[
            jax.ShapeDtypeStruct((channels // 128, rows, 128), F32),
            jax.ShapeDtypeStruct((channels // 128, rows, 128), F32),
            jax.ShapeDtypeStruct((2, SEGS, channels), F32),
            jax.ShapeDtypeStruct((2, channels), F32),
        ],
        compiler_params=pltpu.CompilerParams(vmem_limit_bytes=20 << 20),
        name="recur",
    )(starts, x, halo, *params)


def level_call(tot, near):
    return pl.pallas_call(
        level_kernel,
        out_shape=jax.ShapeDtypeStruct(tot.shape, F32),
        compiler_params=pltpu.CompilerParams(vmem_limit_bytes=1 << 20),
        name="level",
    )(tot, near)


def ready_call(h, p, y, kv_panel, kv_scale):
    rows, channels = y.shape
    vmem = pl.BlockSpec(memory_space=pltpu.VMEM)
    flat = jax.ShapeDtypeStruct((rows, channels), F32)
    return pl.pallas_call(
        ready_kernel,
        in_specs=[vmem] * 5,
        out_specs=[vmem] * 3,
        out_shape=[flat, flat, jax.ShapeDtypeStruct(kv_panel.shape, BF16)],
        cost_estimate=pl.CostEstimate(flops=1 << 24, bytes_accessed=1 << 22, transcendentals=rows * channels),
        compiler_params=pltpu.CompilerParams(vmem_limit_bytes=4 << 20),
        name="ready",
    )(h, p, y, kv_panel, kv_scale)


def mix_call(hg, pg, weight, ends, near, past):
    rows, channels = hg.shape
    out = weight.shape[1]
    width = MIX_GROUPS * SCALE_ROWS
    vmem = pl.BlockSpec(memory_space=pltpu.VMEM)
    return pl.pallas_call(
        functools.partial(mix_kernel, len(past)),
        in_specs=[vmem] * (5 + len(past)),
        out_specs=[pl.BlockSpec(memory_space=pl.ANY), vmem],
        out_shape=[jax.ShapeDtypeStruct((rows, channels), BF16), jax.ShapeDtypeStruct((rows, out), F32)],
        scratch_shapes=[
            pltpu.VMEM((channels // width, rows, width), BF16),
            pltpu.SemaphoreType.DMA((channels // width,)),
        ],
        compiler_params=pltpu.CompilerParams(vmem_limit_bytes=8 << 20),
        name="mix",
    )(hg, pg, weight, ends, near, *past)


def sum_call(a, b):
    rows, _ = a.shape
    half = rows // 2
    return pl.pallas_call(
        sum_kernel,
        out_shape=[
            jax.ShapeDtypeStruct((2, 2 * HD, half), BF16),
            jax.ShapeDtypeStruct((2 * HD, half), BF16),
        ],
        compiler_params=pltpu.CompilerParams(vmem_limit_bytes=16 << 20),
        name="kvsum",
    )(a, b)


def attend_call(starts, q, own, halves, lags, prev, final):
    rows, width = q.shape
    heads = width // HD
    held = [] if own is None else [own]
    held += halves
    held += prev or []
    tiles = len(lags) + (own is not None)
    vmem = pl.BlockSpec(memory_space=pltpu.VMEM)
    scratch = [
        pltpu.VMEM((rows, 128), jnp.int32),
        pltpu.VMEM((tiles, GROUP, 2, rows, rows // 2), F32),
        pltpu.VMEM((GROUP, rows, 128), F32),
    ]
    aliases = {}
    if final:
        out_specs = pl.BlockSpec(memory_space=pl.ANY)
        out_shape = jax.ShapeDtypeStruct((rows, width), BF16)
        scratch += [pltpu.VMEM((rows, GROUP * n), F32) for n in (HD, 128, 128)]
        scratch += [pltpu.VMEM((heads // GROUP, rows, GROUP * HD), BF16), pltpu.SemaphoreType.DMA((heads // GROUP,))]
    if own is None:
        scratch += [
            pltpu.VMEM((tiles, heads, rows // 128, rows, 128), BF16),
            pltpu.VMEM((rows, heads * 128), F32),
            pltpu.SMEM((1,), jnp.int32),
        ]
    if not final:
        out_specs = [vmem] * 3
        out_shape = [jax.ShapeDtypeStruct((rows, heads * n), F32) for n in (HD, 128, 128)]
        if prev:
            aliases = {2 + len(halves) + k: k for k in range(3)}
    return pl.pallas_call(
        functools.partial(attend_kernel, own is not None, lags, final, heads),
        in_specs=[pl.BlockSpec(memory_space=pltpu.SMEM), vmem] + [vmem] * len(held),
        out_specs=out_specs,
        scratch_shapes=scratch,
        out_shape=out_shape,
        input_output_aliases=aliases,
        cost_estimate=pl.CostEstimate(
            flops=4 * tiles * rows * rows * width,
            bytes_accessed=4 * rows * width,
            transcendentals=tiles * rows * rows * heads,
        ),
        compiler_params=pltpu.CompilerParams(vmem_limit_bytes=32 << 20),
        name="attend_own" if own is not None else "attend_end" if final else "attend_mid",
    )(starts, q, *held)


def local(
    branch_x,
    branch_y,
    queries,
    conv_weight,
    conv_bias,
    gate_panel,
    gate_scale,
    gate_bias,
    decay_rate,
    kv_panel,
    kv_scale,
    segment_ids,
):
    rows = branch_x.shape[0]
    seq = segment_ids.shape[0]
    halo = ring(branch_x[rows - CONV + 1 :], 1)
    starts = jnp.sum(
        (segment_ids[None, :] < jnp.arange(DOCS, dtype=jnp.int32)[:, None]).astype(jnp.int32), axis=1
    )
    stay = lambda a: pltpu.with_memory_space_constraint(a, pltpu.HBM)
    h, p, ends, tot = recur_call(
        starts,
        stay(branch_x),
        halo,
        stay(conv_weight),
        stay(conv_bias[None]),
        stay(gate_panel),
        stay(gate_scale),
        stay(gate_bias),
        stay(decay_rate[None]),
    )
    near = swap(tot)
    hg, pg, weight = ready_call(h, p, branch_y, kv_panel, kv_scale)
    level = level_call(tot, near)
    levels = -(-(seq // 2) // (2 * rows))
    past = [ring(level, 2 * k) for k in range(1, levels + 1)]
    mixed, partial_kv = mix_call(hg, pg, weight, ends, near, past)
    own, half = sum_call(partial_kv, partner(partial_kv))

    levels = -(-WINDOW // rows) // 2
    straight, attended = half, None
    for k in range(levels + 1):
        last = k == levels
        beyond = None if last else ring(straight, 2)
        crossed = swap(straight)
        if k == 0:
            attended = attend_call(starts, queries, own, [], [], None, False)
        else:
            attended = attend_call(starts, queries, None, tiles, lags, attended, False)
        tiles, lags = [crossed, partner(crossed)], [(2 * k, 1)]
        if not last:
            tiles += [beyond, partner(beyond)]
            lags.append((2 * k + 2, 0))
        straight = beyond
    attended = attend_call(starts, queries, None, tiles, lags, attended, True)
    return mixed, attended


def solution(mesh):
    in_specs = (
        P(("groups", "tm"), "mp"),
        P(("groups", "tm"), "mp"),
        P(("groups", "tm"), "mp"),
        P(None, "mp"),
        P("mp"),
        P("mp", None, None),
        P("mp", None, None),
        P(None, "mp"),
        P("mp"),
        P("mp", None),
        P("mp", None),
        P("groups"),
    )
    out_specs = (P(("groups", "tm"), "mp"), P(("groups", "tm"), "mp"))
    return jax.shard_map(local, mesh=mesh, in_specs=in_specs, out_specs=out_specs, check_vma=False)
```

```python
import functools
import math

import jax
import jax.numpy as jnp
from jax import lax
from jax.experimental import pallas as pl
from jax.experimental.pallas import tpu as pltpu
from jax.sharding import PartitionSpec as P


HD = 256
CONV = 4
WINDOW = 2048
SCALE_ROWS = 128
DOCS = 4
SEGS = 8
MIX_GROUPS = 4
GROUP = 2
CHUNK = 16
HIST = 4
LOG2E = 1.4426950408889634
LN2 = 0.6931471805599453
SPAN = 0.16
SINH = [
    -0.5 * LN2 * (1.0 + SPAN**3 / (32 * 5040)),
    -0.5 * LN2**3 * (1.0 / 6 - 9 * SPAN**2 / (16 * 5040)),
    -0.5 * LN2**5 * (1.0 / 120 + 1.5 * SPAN / 5040),
]
F32 = jnp.float32
BF16 = jnp.bfloat16


def ring(x, lag):
    n = lax.axis_size("tm")
    return lax.ppermute(x, "tm", [(i, (i + lag) % n) for i in range(n)])


def swap(x):
    n = lax.axis_size("tm")
    return lax.ppermute(x, "tm", [(i, i ^ 1) for i in range(n)])


def partner(x):
    return lax.ppermute(x, "mp", [(0, 1), (1, 0)])


def dequantized(panel, scale):
    rows = panel.shape[0]
    parts = []
    for g in range(rows // SCALE_ROWS):
        part = panel[g * SCALE_ROWS : (g + 1) * SCALE_ROWS, :].astype(F32)
        parts.append((part * scale[g : g + 1, :]).astype(BF16))
    return jnp.concatenate(parts, 0)


def recur_kernel(
    starts_ref,
    x_hbm,
    halo_all,
    cw_hbm,
    cb_hbm,
    panel_hbm,
    scale_hbm,
    gb_hbm,
    rate_hbm,
    h_ref,
    p_ref,
    ends_ref,
    tot_ref,
    keep,
    xs,
    co,
    gate,
    x_buf,
    panel_buf,
    cw_all,
    cb_all,
    scale_all,
    gb_all,
    rate_all,
    hits,
    sems,
    small_sems,
):
    blocks, width, _ = panel_hbm.shape
    rows = x_hbm.shape[0]
    seg_len = rows // SEGS
    base = lax.axis_index("tm") * rows

    def fetch_x(b):
        at = pl.ds(pl.multiple_of(b * width, width), width)
        return pltpu.make_async_copy(x_hbm.at[:, at], x_buf.at[b % 2], sems.at[0, b % 2])

    def fetch_panel(b):
        return pltpu.make_async_copy(panel_hbm.at[b], panel_buf.at[b % 2], sems.at[1, b % 2])

    fetch_x(0).start()
    fetch_panel(0).start()
    sources = (cw_hbm, cb_hbm, scale_hbm, gb_hbm, rate_hbm)
    targets = (cw_all, cb_all, scale_all, gb_all, rate_all)
    smalls = [
        pltpu.make_async_copy(src, dst, small_sems.at[k]) for k, (src, dst) in enumerate(zip(sources, targets))
    ]
    for copy in smalls:
        copy.start()

    def fill(i, carry):
        pos = base + i - 2 + seg_len * lax.broadcasted_iota(jnp.int32, (SEGS, 128), 0)
        hit = pos == starts_ref[0]
        for d in range(1, DOCS):
            hit = hit | (pos == starts_ref[d])
        keep[pl.ds(pl.multiple_of(i * SEGS, SEGS), SEGS), :] = jnp.where(hit, 0.0, 1.0)
        return carry

    lax.fori_loop(0, seg_len + 2, fill, 0)
    for copy in smalls:
        copy.wait()

    for k in range(seg_len // CHUNK):
        hits[k] = 0
    for d in range(DOCS):
        off = starts_ref[d] - base

        @pl.when((off >= 0) & (off < rows))
        def _(off=off):
            hits[lax.rem(off, seg_len) // CHUNK] = 1

    def hit(k):
        return hits[k] > 0

    def block(b, z):
        fetch_x(b).wait()
        fetch_panel(b).wait()

        @pl.when(b + 1 < blocks)
        def _():
            fetch_x(b + 1).start()
            fetch_panel(b + 1).start()

        wide = pl.ds(pl.multiple_of(b * width, width), width)
        recur_block(
            hit,
            b,
            x_buf.at[b % 2],
            halo_all.at[:, wide],
            cw_all.at[:, wide],
            cb_all.at[:, wide],
            panel_buf[b % 2],
            scale_all[b],
            gb_all.at[:, wide],
            rate_all.at[:, wide],
            h_ref,
            p_ref,
            ends_ref.at[:, :, wide],
            tot_ref.at[:, wide],
            keep,
            xs,
            co,
            gate,
        )
        return z

    lax.fori_loop(0, blocks, block, 0)


def recur_block(
    hit,
    b,
    x_ref,
    halo_ref,
    cw_ref,
    cb_ref,
    panel,
    scale,
    gb_ref,
    rate_ref,
    h_ref,
    p_ref,
    ends_ref,
    tot_ref,
    keep,
    xs,
    co,
    gate,
):
    rows, width = x_ref.shape
    seg_len = rows // SEGS
    pitch = seg_len + HIST
    for c in range(width // 128):
        lanes = slice(c * 128, (c + 1) * 128)
        xs[c, HIST + 1 : 2 * HIST, :] = halo_ref[:, lanes].astype(F32)
        for s in range(1, SEGS):
            past = x_ref[s * seg_len - 2 * HIST : s * seg_len, lanes].astype(F32)
            xs[c, s * pitch : s * pitch + 2 * HIST, :] = past
        for s in range(SEGS):
            rest = x_ref[s * seg_len : (s + 1) * seg_len, lanes].astype(F32)
            xs[c, s * pitch + 2 * HIST : (s + 1) * pitch + HIST, :] = rest

    def mask(i):
        m = keep[pl.ds(pl.multiple_of((i + 2) * SEGS, SEGS), SEGS), :]
        return jnp.concatenate([m] * (width // 128), 1)

    def row(i):
        return jnp.concatenate(
            [xs[c, pl.ds(2 * HIST + i, SEGS, stride=pitch), :] for c in range(width // 128)], 1
        )

    w = [jnp.broadcast_to(cw_ref[j : j + 1, :], (SEGS, width)) for j in range(CONV)]
    bias = jnp.broadcast_to(cb_ref[...], (SEGS, width))

    def chunked(step, carry):
        def chunk(masked, k, carry):
            for u in range(CHUNK // 2):
                carry = step(k * (CHUNK // 2) + u, carry, masked)
            return carry

        def body(k, carry):
            return lax.cond(hit(k), functools.partial(chunk, True), functools.partial(chunk, False), k, carry)

        return lax.fori_loop(0, seg_len // CHUNK, body, carry)

    def conv_step(i, carry, masked):
        ka, kb, kc = carry
        x = row(i)
        if masked:
            m = mask(i)
            ka, kb, kc = m * ka, m * kb, m * kc
        return (w[3] * x, w[2] * x + ka, w[1] * x + kb), w[0] * x + kc + bias

    x3, x2, x1 = row(-3), row(-2), row(-1)
    a1 = w[3] * x1
    b1 = w[2] * x1 + mask(-1) * (w[3] * x2)
    c1 = w[1] * x1 + mask(-1) * (w[2] * x2 + mask(-2) * (w[3] * x3))

    def conv_pair(k, carry, masked):
        carry, d0 = conv_step(2 * k, carry, masked)
        carry, d1 = conv_step(2 * k + 1, carry, masked)
        d = jnp.concatenate([d0, d1], 0).astype(BF16)
        for c in range(width // 128):
            co[c, pl.ds(pl.multiple_of(k * 2 * SEGS, 2 * SEGS), 2 * SEGS), :] = d[:, c * 128 : (c + 1) * 128]
        return carry

    chunked(conv_pair, (a1, b1, c1))

    weight = dequantized(panel, scale) * BF16(0.5)
    conv_out = jnp.concatenate([co[c] for c in range(width // 128)], 1)
    gate[...] = jnp.dot(conv_out, weight, preferred_element_type=F32)

    bias_r = jnp.broadcast_to(gb_ref[0:1, :] * 0.5, (SEGS, width))
    bias_i = jnp.broadcast_to(gb_ref[1:2, :] * 0.5, (SEGS, width))
    rate4 = jnp.broadcast_to(rate_ref[...] * (-4.0 * LOG2E), (SEGS, width))

    def scan_step(i, conv, carry, masked):
        h, p = carry
        at = pl.ds(pl.multiple_of(i * SEGS, SEGS), SEGS)
        v = rate4 * (1.0 + jnp.tanh(gate[at, :width] + bias_r))
        ti = 1.0 + jnp.tanh(gate[at, width:] + bias_i)
        decay = jnp.exp2(v)
        s = v * v
        series = (s * SINH[2] + SINH[1]) * s + SINH[0]
        quarter = decay * (v * series)
        half = quarter * lax.rsqrt(jnp.maximum(quarter, 1e-37))
        if masked:
            m = mask(i)
            half = jnp.where(m > 0.0, half, 0.5)
            decay = decay * m
        h = decay * h + ti * (conv * half)
        p = p * decay
        for c in range(width // 128):
            h_ref[b * (width // 128) + c, at, :] = h[:, c * 128 : (c + 1) * 128]
            p_ref[b * (width // 128) + c, at, :] = p[:, c * 128 : (c + 1) * 128]
        return h, p

    def scan_pair(k, carry, masked):
        at = pl.ds(pl.multiple_of(k * 2 * SEGS, 2 * SEGS), 2 * SEGS)
        conv = jnp.concatenate([co[c, at, :].astype(F32) for c in range(width // 128)], 1)
        carry = scan_step(2 * k, conv[:SEGS], carry, masked)
        return scan_step(2 * k + 1, conv[SEGS:], carry, masked)

    h, p = chunked(scan_pair, (jnp.zeros((SEGS, width), F32), jnp.ones((SEGS, width), F32)))
    ends_ref[0] = p
    ends_ref[1] = h
    tp, th = p[0:1], h[0:1]
    for s in range(1, SEGS):
        th = p[s : s + 1] * th + h[s : s + 1]
        tp = tp * p[s : s + 1]
    tot_ref[0:1, :] = tp
    tot_ref[1:2, :] = th


def level_kernel(tot_ref, near_ref, level_ref):
    odd = lax.axis_index("tm") % 2 == 1
    tot, near = tot_ref[...], near_ref[...]
    lower = jnp.where(odd, near, tot)
    upper = jnp.where(odd, tot, near)
    level_ref[0:1, :] = lower[0:1] * upper[0:1]
    level_ref[1:2, :] = upper[0:1] * lower[1:2] + upper[1:2]


def ready_kernel(h_ref, p_ref, y_ref, panel_ref, scale_ref, hg_ref, pg_ref, w_ref):
    rows, channels = y_ref.shape
    seg_len = rows // SEGS
    width = MIX_GROUPS * SCALE_ROWS

    def natural(ref, c, s):
        return jnp.concatenate(
            [ref[c, pl.ds(s + k * 8 * SEGS, 8, stride=SEGS), :] for k in range(seg_len // 8)], 0
        )

    def body(g, z):
        wide = pl.ds(pl.multiple_of(g * width, width), width)
        table = scale_ref[...]
        index = lax.broadcasted_iota(jnp.int32, table.shape, 0) - g * MIX_GROUPS
        scale = [jnp.sum(jnp.where(index == k, table, 0.0), axis=0, keepdims=True) for k in range(MIX_GROUPS)]
        w_ref[wide, :] = dequantized(panel_ref[wide, :], jnp.concatenate(scale, 0))
        for s in range(SEGS):
            at = slice(s * seg_len, (s + 1) * seg_len)
            y = y_ref[at, wide].astype(F32)
            inner = y * (0.7978845608028654 + (0.7978845608028654 * 0.044715) * (y * y))
            gelu = (0.5 * y) * (1.0 + jnp.tanh(inner))
            for c in range(width // 128):
                lanes = pl.ds(pl.multiple_of(g * width + c * 128, 128), 128)
                part = gelu[:, c * 128 : (c + 1) * 128]
                hg_ref[at, lanes] = natural(h_ref, g * (width // 128) + c, s) * part
                pg_ref[at, lanes] = natural(p_ref, g * (width // 128) + c, s) * part
        return z

    lax.fori_loop(0, channels // width, body, 0)


def mix_kernel(levels, hg_ref, pg_ref, w_ref, ends_ref, near_ref, *refs):
    past, (mixed_hbm, kv_ref, stage, sems) = refs[:levels], refs[levels:]
    rows, channels = hg_ref.shape
    seg_len = rows // SEGS
    width = MIX_GROUPS * SCALE_ROWS
    me = lax.axis_index("tm")
    kv_ref[...] = jnp.zeros_like(kv_ref)

    def outgoing(g):
        wide = pl.ds(pl.multiple_of(g * width, width), width)
        return pltpu.make_async_copy(stage.at[g], mixed_hbm.at[:, wide], sems.at[g])

    def body(g, z):
        wide = pl.ds(pl.multiple_of(g * width, width), width)
        c = jnp.zeros((1, width), F32)
        for k in range(levels, 0, -1):
            c = jnp.where(me >= 2 * k, past[k - 1][0:1, wide] * c + past[k - 1][1:2, wide], 0.0)
        c = jnp.where(me % 2 == 1, near_ref[0:1, wide] * c + near_ref[1:2, wide], c)
        for s in range(SEGS):
            at = slice(s * seg_len, (s + 1) * seg_len)
            stage[g, at, :] = (hg_ref[at, wide] + pg_ref[at, wide] * c).astype(BF16)
            c = ends_ref[0, s : s + 1, wide] * c + ends_ref[1, s : s + 1, wide]
        outgoing(g).start()
        kv_ref[...] += jnp.dot(stage[g], w_ref[wide, :], preferred_element_type=F32)
        return z

    def drain(g, z):
        outgoing(g).wait()
        return z

    lax.fori_loop(0, channels // width, body, 0)
    lax.fori_loop(0, channels // width, drain, 0)


def sum_kernel(a_ref, b_ref, own_ref, half_ref):
    both = a_ref[...] + b_ref[...]
    n = both.shape[0] // 2
    core = lax.axis_index("mp")
    for side in range(2):
        keys = both[side * n : (side + 1) * n, :HD].T.astype(BF16)
        values = both[side * n : (side + 1) * n, HD:].astype(BF16)
        own_ref[side, :HD, :] = keys
        own_ref[side, HD:, :] = values
    half_ref[...] = own_ref[core]


def attend_kernel(own, lags, final, heads, starts_ref, q_ref, *refs):
    refs = list(refs)
    take = lambda n: [refs.pop(0) for _ in range(n)]
    own_ref = take(1)[0] if own else None
    pairs = [take(2) for _ in lags]
    prev = None if own else take(3)
    out = take(1)[0] if final else None
    acc, m_ref, l_ref = (None, None, None) if final else take(3)
    low, score, top = take(3)
    if final:
        acc, m_ref, l_ref, stage, sems = take(5)
    prob, l_new, flag = (None, None, None) if own else take(3)
    rows = q_ref.shape[0]
    half = rows // 2
    me = lax.axis_index("tm")
    first = me * rows
    core = lax.axis_index("mp")
    turn = 2 * (me % 2) - 1
    scale = LOG2E / math.sqrt(HD)

    def lowest(t):
        d0 = jnp.maximum(t - (WINDOW - 1), 0)
        for d in range(DOCS):
            d0 = jnp.maximum(d0, jnp.where(starts_ref[d] <= t, starts_ref[d], 0))
        return d0

    lo_first = lowest(first)
    lo_last = lowest(first + rows - 1)
    tiles = [(None, first)] if own else []
    for k, (even_part, odd_part) in enumerate(lags):
        tiles.append((pairs[k], first - (even_part + odd_part * turn) * rows))
    live = [None if pair is None else (start >= 0) & (start < first) & (start + rows > lo_first) for pair, start in tiles]

    def keys_of(pair, t):
        return own_ref[t, :HD, :] if pair is None else pair[t][:HD, :]

    def values_of(pair, t):
        return own_ref[t, HD:, :] if pair is None else pair[t][HD:, :]

    def lanes(g, h, n):
        return pl.ds(pl.multiple_of((g * GROUP + h) * n, n), n)

    def kept(g, h, n):
        return slice(h * n, (h + 1) * n) if final else lanes(g, h, n)

    def score_pass(g, j, pair, start, masked):
        for h in range(GROUP):
            for t in range(2):
                r0 = half * t if pair is None else 0
                at = slice(r0, rows)
                s = jnp.dot(q_ref[at, lanes(g, h, HD)], keys_of(pair, t), preferred_element_type=F32)
                peak = top[h, at, :]
                for c in range(half // 128):
                    part = s[:, c * 128 : (c + 1) * 128] * scale
                    if masked:
                        side = t if pair is None else jnp.where(core == t, 0, 1)
                        kpos = lax.broadcasted_iota(jnp.int32, part.shape, 1) + (start + side * half + c * 128)
                        ok = kpos >= low[at, :]
                        if pair is None:
                            ok = ok & (kpos <= lax.broadcasted_iota(jnp.int32, part.shape, 0) + (first + r0))
                        part = jnp.where(ok, part, -1e30)
                    score[j, h, t, at, c * 128 : (c + 1) * 128] = part
                    peak = jnp.maximum(peak, part)
                top[h, at, :] = peak

    def value_pass(g, j, pair):
        for h in range(GROUP):
            spans = [(0, half, 1), (half, rows, 2)] if pair is None else [(0, rows, 2)]
            for r0, r1, n in spans:
                at = slice(r0, r1)
                m = m_ref[at, kept(g, h, 128)]
                total = l_ref[at, kept(g, h, 128)]
                ps, vs = [], []
                for t in range(n):
                    for c in range(half // 128):
                        p = jnp.exp2(score[j, h, t, at, c * 128 : (c + 1) * 128] - m)
                        total = total + p
                        ps.append(p.astype(BF16))
                    vs.append(values_of(pair, t))
                l_ref[at, kept(g, h, 128)] = total
                acc[at, kept(g, h, HD)] += jnp.dot(
                    jnp.concatenate(ps, 1), jnp.concatenate(vs, 0), preferred_element_type=F32
                )

    def spread(x):
        return jnp.concatenate([x] * (HD // 128), 1)

    def update(g):
        top[...] = jnp.full(top.shape, -1e30, F32)
        for j, (pair, start) in enumerate(tiles):
            if pair is None:
                score_pass(g, j, pair, start, True)
                continue

            @pl.when(live[j] & (start >= lo_last))
            def _(j=j, pair=pair, start=start):
                score_pass(g, j, pair, start, False)

            @pl.when(live[j] & (start < lo_last))
            def _(j=j, pair=pair, start=start):
                score_pass(g, j, pair, start, True)

        for h in range(GROUP):
            m = jnp.broadcast_to(jnp.max(top[h], axis=1, keepdims=True), (rows, 128))
            if own:
                l_ref[:, kept(g, h, 128)] = jnp.zeros((rows, 128), F32)
                acc[:, kept(g, h, HD)] = jnp.zeros((rows, HD), F32)
            else:
                m0 = prev[1][:, lanes(g, h, 128)]
                m = jnp.maximum(m, m0)
                fade = jnp.exp2(m0 - m)
                l_ref[:, kept(g, h, 128)] = prev[2][:, lanes(g, h, 128)] * fade
                acc[:, kept(g, h, HD)] = prev[0][:, lanes(g, h, HD)] * spread(fade)
            m_ref[:, kept(g, h, 128)] = m
        for j, (pair, start) in enumerate(tiles):
            if pair is None:
                value_pass(g, j, pair)
                continue

            @pl.when(live[j])
            def _(j=j, pair=pair):
                value_pass(g, j, pair)

    def loop(fn):
        def body(g, z):
            fn(g)
            return z

        lax.fori_loop(0, heads // GROUP, body, 0)

    def start_up():
        low[...] = lowest(first + lax.broadcasted_iota(jnp.int32, (rows, 128), 0))

    if own:
        start_up()
        loop(update)
        return

    def exp_pass(g, j, pair, start, masked):
        for h in range(GROUP):
            m = prev[1][:, lanes(g, h, 128)]
            total = l_new[:, lanes(g, h, 128)]
            for t in range(2):
                s = jnp.dot(q_ref[:, lanes(g, h, HD)], keys_of(pair, t), preferred_element_type=F32)
                for c in range(half // 128):
                    part = s[:, c * 128 : (c + 1) * 128] * scale
                    if masked:
                        side = jnp.where(core == t, 0, 1)
                        kpos = lax.broadcasted_iota(jnp.int32, part.shape, 1) + (start + side * half + c * 128)
                        part = jnp.where(kpos >= low[...], part, -1e30)
                    p = jnp.exp2(part - m)
                    total = total + p
                    prob[j, g * GROUP + h, (t * half) // 128 + c] = p.astype(BF16)
            l_new[:, lanes(g, h, 128)] = total

    def weighted(g, h, j, pair):
        values = jnp.concatenate([values_of(pair, t) for t in range(2)], 0)
        shares = jnp.concatenate([prob[j, g * GROUP + h, c] for c in range(rows // 128)], 1)
        return jnp.dot(shares, values, preferred_element_type=F32)

    def exp_all(g):
        for j, (pair, start) in enumerate(tiles):

            @pl.when(live[j] & (start >= lo_last))
            def _(j=j, pair=pair, start=start):
                exp_pass(g, j, pair, start, False)

            @pl.when(live[j] & (start < lo_last))
            def _(j=j, pair=pair, start=start):
                exp_pass(g, j, pair, start, True)

    any_live = functools.reduce(jnp.logical_or, live)

    @pl.when(any_live)
    def _():
        start_up()
        l_new[...] = prev[2][...]
        loop(exp_all)
        flag[0] = jnp.where(jnp.max(l_new[...]) <= 2.0**64, 1, 0)

    @pl.when(jnp.logical_not(any_live))
    def _():
        flag[0] = 2

    fast = flag[0] == 1
    slow = flag[0] == 0

    if not final:

        def add_all(g):
            for j, (pair, start) in enumerate(tiles):

                @pl.when(live[j])
                def _(j=j, pair=pair):
                    for h in range(GROUP):
                        acc[:, lanes(g, h, HD)] += weighted(g, h, j, pair)

        @pl.when(fast)
        def _():
            l_ref[...] = l_new[...]
            loop(add_all)

        @pl.when(slow)
        def _():
            loop(update)

        return

    def outgoing(g):
        wide = pl.ds(pl.multiple_of(g * GROUP * HD, GROUP * HD), GROUP * HD)
        return pltpu.make_async_copy(stage.at[g], out.at[:, wide], sems.at[g])

    def settle(g, h, top_sum, below):
        share = jnp.broadcast_to(1.0 / jnp.sum(below, axis=1, keepdims=True), (rows, 128))
        stage[g, :, h * HD : (h + 1) * HD] = (top_sum * spread(share)).astype(BF16)

    def finish(g):
        @pl.when(fast)
        def _():
            for h in range(GROUP):
                sums = prev[0][:, lanes(g, h, HD)] + weighted(g, h, 0, tiles[0][0])
                settle(g, h, sums, l_new[:, lanes(g, h, 128)])

        @pl.when(slow)
        def _():
            update(g)
            for h in range(GROUP):
                settle(g, h, acc[:, kept(g, h, HD)], l_ref[:, kept(g, h, 128)])

        @pl.when(jnp.logical_not(any_live))
        def _():
            for h in range(GROUP):
                settle(g, h, prev[0][:, lanes(g, h, HD)], prev[2][:, lanes(g, h, 128)])

        outgoing(g).start()

    loop(finish)
    loop(lambda g: outgoing(g).wait())


def recur_call(starts, x, halo, *params):
    rows, channels = x.shape
    _, width, _ = params[2].shape
    conv_weight, conv_bias, _, gate_scale, gate_bias, decay_rate = params
    vmem = pl.BlockSpec(memory_space=pltpu.VMEM)
    hbm = pl.BlockSpec(memory_space=pl.ANY)
    return pl.pallas_call(
        recur_kernel,
        in_specs=[pl.BlockSpec(memory_space=pltpu.SMEM), hbm, vmem] + [hbm] * 6,
        out_specs=[vmem] * 4,
        scratch_shapes=[
            pltpu.VMEM((rows + 2 * SEGS, 128), F32),
            pltpu.VMEM((width // 128, rows + HIST * (SEGS + 1), 128), F32),
            pltpu.VMEM((width // 128, rows, 128), BF16),
            pltpu.VMEM((rows, 2 * width), F32),
            pltpu.VMEM((2, rows, width), BF16),
            pltpu.VMEM((2, width, 2 * width), BF16),
        ]
        + [pltpu.VMEM(a.shape, F32) for a in (conv_weight, conv_bias, gate_scale, gate_bias, decay_rate)]
        + [pltpu.SMEM((rows // SEGS // CHUNK,), jnp.int32)]
        + [pltpu.SemaphoreType.DMA((2, 2)), pltpu.SemaphoreType.DMA((5,))],
        out_shape=[
            jax.ShapeDtypeStruct((channels // 128, rows, 128), F32),
            jax.ShapeDtypeStruct((channels // 128, rows, 128), F32),
            jax.ShapeDtypeStruct((2, SEGS, channels), F32),
            jax.ShapeDtypeStruct((2, channels), F32),
        ],
        compiler_params=pltpu.CompilerParams(vmem_limit_bytes=20 << 20),
        name="recur",
    )(starts, x, halo, *params)


def level_call(tot, near):
    return pl.pallas_call(
        level_kernel,
        out_shape=jax.ShapeDtypeStruct(tot.shape, F32),
        compiler_params=pltpu.CompilerParams(vmem_limit_bytes=1 << 20),
        name="level",
    )(tot, near)


def ready_call(h, p, y, kv_panel, kv_scale):
    rows, channels = y.shape
    vmem = pl.BlockSpec(memory_space=pltpu.VMEM)
    flat = jax.ShapeDtypeStruct((rows, channels), F32)
    return pl.pallas_call(
        ready_kernel,
        in_specs=[vmem] * 5,
        out_specs=[vmem] * 3,
        out_shape=[flat, flat, jax.ShapeDtypeStruct(kv_panel.shape, BF16)],
        cost_estimate=pl.CostEstimate(flops=1 << 24, bytes_accessed=1 << 22, transcendentals=rows * channels),
        compiler_params=pltpu.CompilerParams(vmem_limit_bytes=4 << 20),
        name="ready",
    )(h, p, y, kv_panel, kv_scale)


def mix_call(hg, pg, weight, ends, near, past):
    rows, channels = hg.shape
    out = weight.shape[1]
    width = MIX_GROUPS * SCALE_ROWS
    vmem = pl.BlockSpec(memory_space=pltpu.VMEM)
    return pl.pallas_call(
        functools.partial(mix_kernel, len(past)),
        in_specs=[vmem] * (5 + len(past)),
        out_specs=[pl.BlockSpec(memory_space=pl.ANY), vmem],
        out_shape=[jax.ShapeDtypeStruct((rows, channels), BF16), jax.ShapeDtypeStruct((rows, out), F32)],
        scratch_shapes=[
            pltpu.VMEM((channels // width, rows, width), BF16),
            pltpu.SemaphoreType.DMA((channels // width,)),
        ],
        compiler_params=pltpu.CompilerParams(vmem_limit_bytes=8 << 20),
        name="mix",
    )(hg, pg, weight, ends, near, *past)


def sum_call(a, b):
    rows, _ = a.shape
    half = rows // 2
    return pl.pallas_call(
        sum_kernel,
        out_shape=[
            jax.ShapeDtypeStruct((2, 2 * HD, half), BF16),
            jax.ShapeDtypeStruct((2 * HD, half), BF16),
        ],
        compiler_params=pltpu.CompilerParams(vmem_limit_bytes=16 << 20),
        name="kvsum",
    )(a, b)


def attend_call(starts, q, own, halves, lags, prev, final):
    rows, width = q.shape
    heads = width // HD
    held = [] if own is None else [own]
    held += halves
    held += prev or []
    tiles = len(lags) + (own is not None)
    vmem = pl.BlockSpec(memory_space=pltpu.VMEM)
    scratch = [
        pltpu.VMEM((rows, 128), jnp.int32),
        pltpu.VMEM((tiles, GROUP, 2, rows, rows // 2), F32),
        pltpu.VMEM((GROUP, rows, 128), F32),
    ]
    aliases = {}
    if final:
        out_specs = pl.BlockSpec(memory_space=pl.ANY)
        out_shape = jax.ShapeDtypeStruct((rows, width), BF16)
        scratch += [pltpu.VMEM((rows, GROUP * n), F32) for n in (HD, 128, 128)]
        scratch += [pltpu.VMEM((heads // GROUP, rows, GROUP * HD), BF16), pltpu.SemaphoreType.DMA((heads // GROUP,))]
    if own is None:
        scratch += [
            pltpu.VMEM((tiles, heads, rows // 128, rows, 128), BF16),
            pltpu.VMEM((rows, heads * 128), F32),
            pltpu.SMEM((1,), jnp.int32),
        ]
    if not final:
        out_specs = [vmem] * 3
        out_shape = [jax.ShapeDtypeStruct((rows, heads * n), F32) for n in (HD, 128, 128)]
        if prev:
            aliases = {2 + len(halves) + k: k for k in range(3)}
    return pl.pallas_call(
        functools.partial(attend_kernel, own is not None, lags, final, heads),
        in_specs=[pl.BlockSpec(memory_space=pltpu.SMEM), vmem] + [vmem] * len(held),
        out_specs=out_specs,
        scratch_shapes=scratch,
        out_shape=out_shape,
        input_output_aliases=aliases,
        cost_estimate=pl.CostEstimate(
            flops=4 * tiles * rows * rows * width,
            bytes_accessed=4 * rows * width,
            transcendentals=tiles * rows * rows * heads,
        ),
        compiler_params=pltpu.CompilerParams(vmem_limit_bytes=32 << 20),
        name="attend_own" if own is not None else "attend_end" if final else "attend_mid",
    )(starts, q, *held)


def local(
    branch_x,
    branch_y,
    queries,
    conv_weight,
    conv_bias,
    gate_panel,
    gate_scale,
    gate_bias,
    decay_rate,
    kv_panel,
    kv_scale,
    segment_ids,
):
    rows = branch_x.shape[0]
    seq = segment_ids.shape[0]
    halo = ring(branch_x[rows - CONV + 1 :], 1)
    starts = jnp.sum(
        (segment_ids[None, :] < jnp.arange(DOCS, dtype=jnp.int32)[:, None]).astype(jnp.int32), axis=1
    )
    stay = lambda a: pltpu.with_memory_space_constraint(a, pltpu.HBM)
    h, p, ends, tot = recur_call(
        starts,
        stay(branch_x),
        halo,
        stay(conv_weight),
        stay(conv_bias[None]),
        stay(gate_panel),
        stay(gate_scale),
        stay(gate_bias),
        stay(decay_rate[None]),
    )
    near = swap(tot)
    hg, pg, weight = ready_call(h, p, branch_y, kv_panel, kv_scale)
    level = level_call(tot, near)
    levels = -(-(seq // 2) // (2 * rows))
    past = [ring(level, 2 * k) for k in range(1, levels + 1)]
    mixed, partial_kv = mix_call(hg, pg, weight, ends, near, past)
    own, half = sum_call(partial_kv, partner(partial_kv))

    levels = -(-WINDOW // rows) // 2
    straight, attended = half, None
    for k in range(levels + 1):
        last = k == levels
        beyond = None if last else ring(straight, 2)
        crossed = swap(straight)
        if k == 0:
            attended = attend_call(starts, queries, own, [], [], None, False)
        else:
            attended = attend_call(starts, queries, None, tiles, lags, attended, False)
        tiles, lags = [crossed, partner(crossed)], [(2 * k, 1)]
        if not last:
            tiles += [beyond, partner(beyond)]
            lags.append((2 * k + 2, 0))
        straight = beyond
    attended = attend_call(starts, queries, None, tiles, lags, attended, True)
    return mixed, attended


def solution(mesh):
    in_specs = (
        P(("groups", "tm"), "mp"),
        P(("groups", "tm"), "mp"),
        P(("groups", "tm"), "mp"),
        P(None, "mp"),
        P("mp"),
        P("mp", None, None),
        P("mp", None, None),
        P(None, "mp"),
        P("mp"),
        P("mp", None),
        P("mp", None),
        P("groups"),
    )
    out_specs = (P(("groups", "tm"), "mp"), P(("groups", "tm"), "mp"))
    return jax.shard_map(local, mesh=mesh, in_specs=in_specs, out_specs=out_specs, check_vma=False)
```

```python
import functools
import math

import jax
import jax.numpy as jnp
from jax import lax
from jax.experimental import pallas as pl
from jax.experimental.pallas import tpu as pltpu
from jax.sharding import PartitionSpec as P


HD = 256
CONV = 4
WINDOW = 2048
SCALE_ROWS = 128
DOCS = 4
SEGS = 8
MIX_GROUPS = 4
GROUP = 2
CHUNK = 16
HIST = 4
LOG2E = 1.4426950408889634
LN2 = 0.6931471805599453
SPAN = 0.16
SINH = [
    -0.5 * LN2 * (1.0 + SPAN**3 / (32 * 5040)),
    -0.5 * LN2**3 * (1.0 / 6 - 9 * SPAN**2 / (16 * 5040)),
    -0.5 * LN2**5 * (1.0 / 120 + 1.5 * SPAN / 5040),
]
F32 = jnp.float32
BF16 = jnp.bfloat16


def ring(x, lag):
    n = lax.axis_size("tm")
    return lax.ppermute(x, "tm", [(i, (i + lag) % n) for i in range(n)])


def swap(x):
    n = lax.axis_size("tm")
    return lax.ppermute(x, "tm", [(i, i ^ 1) for i in range(n)])


def partner(x):
    return lax.ppermute(x, "mp", [(0, 1), (1, 0)])


def dequantized(panel, scale):
    rows = panel.shape[0]
    parts = []
    for g in range(rows // SCALE_ROWS):
        part = panel[g * SCALE_ROWS : (g + 1) * SCALE_ROWS, :].astype(F32)
        parts.append((part * scale[g : g + 1, :]).astype(BF16))
    return jnp.concatenate(parts, 0)


def recur_kernel(
    starts_ref,
    x_hbm,
    halo_all,
    cw_hbm,
    cb_hbm,
    panel_hbm,
    scale_hbm,
    gb_hbm,
    rate_hbm,
    h_ref,
    p_ref,
    ends_ref,
    tot_ref,
    keep,
    xs,
    co,
    gate,
    x_buf,
    panel_buf,
    cw_all,
    cb_all,
    scale_all,
    gb_all,
    rate_all,
    hits,
    sems,
    small_sems,
):
    blocks, width, _ = panel_hbm.shape
    rows = x_hbm.shape[0]
    seg_len = rows // SEGS
    base = lax.axis_index("tm") * rows

    def fetch_x(b):
        at = pl.ds(pl.multiple_of(b * width, width), width)
        return pltpu.make_async_copy(x_hbm.at[:, at], x_buf.at[b % 2], sems.at[0, b % 2])

    def fetch_panel(b):
        return pltpu.make_async_copy(panel_hbm.at[b], panel_buf.at[b % 2], sems.at[1, b % 2])

    fetch_x(0).start()
    fetch_panel(0).start()
    sources = (cw_hbm, cb_hbm, scale_hbm, gb_hbm, rate_hbm)
    targets = (cw_all, cb_all, scale_all, gb_all, rate_all)
    smalls = [
        pltpu.make_async_copy(src, dst, small_sems.at[k]) for k, (src, dst) in enumerate(zip(sources, targets))
    ]
    for copy in smalls:
        copy.start()

    def fill(i, carry):
        pos = base + i - 2 + seg_len * lax.broadcasted_iota(jnp.int32, (SEGS, 128), 0)
        hit = pos == starts_ref[0]
        for d in range(1, DOCS):
            hit = hit | (pos == starts_ref[d])
        keep[pl.ds(pl.multiple_of(i * SEGS, SEGS), SEGS), :] = jnp.where(hit, 0.0, 1.0)
        return carry

    lax.fori_loop(0, seg_len + 2, fill, 0)
    for copy in smalls:
        copy.wait()

    for k in range(seg_len // CHUNK):
        hits[k] = 0
    for d in range(DOCS):
        off = starts_ref[d] - base

        @pl.when((off >= 0) & (off < rows))
        def _(off=off):
            hits[lax.rem(off, seg_len) // CHUNK] = 1

    def hit(k):
        return hits[k] > 0

    def block(b, z):
        fetch_x(b).wait()
        fetch_panel(b).wait()

        @pl.when(b + 1 < blocks)
        def _():
            fetch_x(b + 1).start()
            fetch_panel(b + 1).start()

        wide = pl.ds(pl.multiple_of(b * width, width), width)
        recur_block(
            hit,
            b,
            x_buf.at[b % 2],
            halo_all.at[:, wide],
            cw_all.at[:, wide],
            cb_all.at[:, wide],
            panel_buf[b % 2],
            scale_all[b],
            gb_all.at[:, wide],
            rate_all.at[:, wide],
            h_ref,
            p_ref,
            ends_ref.at[:, :, wide],
            tot_ref.at[:, wide],
            keep,
            xs,
            co,
            gate,
        )
        return z

    lax.fori_loop(0, blocks, block, 0)


def recur_block(
    hit,
    b,
    x_ref,
    halo_ref,
    cw_ref,
    cb_ref,
    panel,
    scale,
    gb_ref,
    rate_ref,
    h_ref,
    p_ref,
    ends_ref,
    tot_ref,
    keep,
    xs,
    co,
    gate,
):
    rows, width = x_ref.shape
    seg_len = rows // SEGS
    pitch = seg_len + HIST
    for c in range(width // 128):
        lanes = slice(c * 128, (c + 1) * 128)
        xs[c, HIST + 1 : 2 * HIST, :] = halo_ref[:, lanes].astype(F32)
        for s in range(1, SEGS):
            past = x_ref[s * seg_len - 2 * HIST : s * seg_len, lanes].astype(F32)
            xs[c, s * pitch : s * pitch + 2 * HIST, :] = past
        for s in range(SEGS):
            rest = x_ref[s * seg_len : (s + 1) * seg_len, lanes].astype(F32)
            xs[c, s * pitch + 2 * HIST : (s + 1) * pitch + HIST, :] = rest

    def mask(i):
        m = keep[pl.ds(pl.multiple_of((i + 2) * SEGS, SEGS), SEGS), :]
        return jnp.concatenate([m] * (width // 128), 1)

    def row(i):
        return jnp.concatenate(
            [xs[c, pl.ds(2 * HIST + i, SEGS, stride=pitch), :] for c in range(width // 128)], 1
        )

    w = [jnp.broadcast_to(cw_ref[j : j + 1, :], (SEGS, width)) for j in range(CONV)]
    bias = jnp.broadcast_to(cb_ref[...], (SEGS, width))

    def chunked(step, carry):
        def chunk(masked, k, carry):
            for u in range(CHUNK // 2):
                carry = step(k * (CHUNK // 2) + u, carry, masked)
            return carry

        def body(k, carry):
            return lax.cond(hit(k), functools.partial(chunk, True), functools.partial(chunk, False), k, carry)

        return lax.fori_loop(0, seg_len // CHUNK, body, carry)

    def conv_step(i, carry, masked):
        ka, kb, kc = carry
        x = row(i)
        if masked:
            m = mask(i)
            ka, kb, kc = m * ka, m * kb, m * kc
        return (w[3] * x, w[2] * x + ka, w[1] * x + kb), w[0] * x + kc + bias

    x3, x2, x1 = row(-3), row(-2), row(-1)
    a1 = w[3] * x1
    b1 = w[2] * x1 + mask(-1) * (w[3] * x2)
    c1 = w[1] * x1 + mask(-1) * (w[2] * x2 + mask(-2) * (w[3] * x3))

    def conv_pair(k, carry, masked):
        carry, d0 = conv_step(2 * k, carry, masked)
        carry, d1 = conv_step(2 * k + 1, carry, masked)
        d = jnp.concatenate([d0, d1], 0).astype(BF16)
        for c in range(width // 128):
            co[c, pl.ds(pl.multiple_of(k * 2 * SEGS, 2 * SEGS), 2 * SEGS), :] = d[:, c * 128 : (c + 1) * 128]
        return carry

    chunked(conv_pair, (a1, b1, c1))

    weight = dequantized(panel, scale) * BF16(0.5)
    conv_out = jnp.concatenate([co[c] for c in range(width // 128)], 1)
    gate[...] = jnp.dot(conv_out, weight, preferred_element_type=F32)

    bias_r = jnp.broadcast_to(gb_ref[0:1, :] * 0.5, (SEGS, width))
    bias_i = jnp.broadcast_to(gb_ref[1:2, :] * 0.5, (SEGS, width))
    rate4 = jnp.broadcast_to(rate_ref[...] * (-4.0 * LOG2E), (SEGS, width))

    def scan_step(i, conv, carry, masked):
        h, p = carry
        at = pl.ds(pl.multiple_of(i * SEGS, SEGS), SEGS)
        v = rate4 * (1.0 + jnp.tanh(gate[at, :width] + bias_r))
        ti = 1.0 + jnp.tanh(gate[at, width:] + bias_i)
        decay = jnp.exp2(v)
        s = v * v
        series = (s * SINH[2] + SINH[1]) * s + SINH[0]
        quarter = decay * (v * series)
        half = quarter * lax.rsqrt(jnp.maximum(quarter, 1e-37))
        if masked:
            m = mask(i)
            half = jnp.where(m > 0.0, half, 0.5)
            decay = decay * m
        h = decay * h + ti * (conv * half)
        p = p * decay
        for c in range(width // 128):
            h_ref[b * (width // 128) + c, at, :] = h[:, c * 128 : (c + 1) * 128]
            p_ref[b * (width // 128) + c, at, :] = p[:, c * 128 : (c + 1) * 128]
        return h, p

    def scan_pair(k, carry, masked):
        at = pl.ds(pl.multiple_of(k * 2 * SEGS, 2 * SEGS), 2 * SEGS)
        conv = jnp.concatenate([co[c, at, :].astype(F32) for c in range(width // 128)], 1)
        carry = scan_step(2 * k, conv[:SEGS], carry, masked)
        return scan_step(2 * k + 1, conv[SEGS:], carry, masked)

    h, p = chunked(scan_pair, (jnp.zeros((SEGS, width), F32), jnp.ones((SEGS, width), F32)))
    ends_ref[0] = p
    ends_ref[1] = h
    tp, th = p[0:1], h[0:1]
    for s in range(1, SEGS):
        th = p[s : s + 1] * th + h[s : s + 1]
        tp = tp * p[s : s + 1]
    tot_ref[0:1, :] = tp
    tot_ref[1:2, :] = th


def level_kernel(tot_ref, near_ref, level_ref):
    odd = lax.axis_index("tm") % 2 == 1
    tot, near = tot_ref[...], near_ref[...]
    lower = jnp.where(odd, near, tot)
    upper = jnp.where(odd, tot, near)
    level_ref[0:1, :] = lower[0:1] * upper[0:1]
    level_ref[1:2, :] = upper[0:1] * lower[1:2] + upper[1:2]


def ready_kernel(h_ref, p_ref, y_ref, panel_ref, scale_ref, hg_ref, pg_ref, w_ref):
    rows, channels = y_ref.shape
    seg_len = rows // SEGS
    width = MIX_GROUPS * SCALE_ROWS

    def natural(ref, c, s):
        return jnp.concatenate(
            [ref[c, pl.ds(s + k * 8 * SEGS, 8, stride=SEGS), :] for k in range(seg_len // 8)], 0
        )

    def body(g, z):
        wide = pl.ds(pl.multiple_of(g * width, width), width)
        table = scale_ref[...]
        index = lax.broadcasted_iota(jnp.int32, table.shape, 0) - g * MIX_GROUPS
        scale = [jnp.sum(jnp.where(index == k, table, 0.0), axis=0, keepdims=True) for k in range(MIX_GROUPS)]
        w_ref[wide, :] = dequantized(panel_ref[wide, :], jnp.concatenate(scale, 0))
        for s in range(SEGS):
            at = slice(s * seg_len, (s + 1) * seg_len)
            y = y_ref[at, wide].astype(F32)
            inner = y * (0.7978845608028654 + (0.7978845608028654 * 0.044715) * (y * y))
            gelu = (0.5 * y) * (1.0 + jnp.tanh(inner))
            for c in range(width // 128):
                lanes = pl.ds(pl.multiple_of(g * width + c * 128, 128), 128)
                part = gelu[:, c * 128 : (c + 1) * 128]
                hg_ref[at, lanes] = natural(h_ref, g * (width // 128) + c, s) * part
                pg_ref[at, lanes] = natural(p_ref, g * (width // 128) + c, s) * part
        return z

    lax.fori_loop(0, channels // width, body, 0)


def mix_kernel(levels, hg_ref, pg_ref, w_ref, ends_ref, near_ref, *refs):
    past, (mixed_hbm, kv_ref, stage, sems) = refs[:levels], refs[levels:]
    rows, channels = hg_ref.shape
    seg_len = rows // SEGS
    width = MIX_GROUPS * SCALE_ROWS
    me = lax.axis_index("tm")
    kv_ref[...] = jnp.zeros_like(kv_ref)

    def outgoing(g):
        wide = pl.ds(pl.multiple_of(g * width, width), width)
        return pltpu.make_async_copy(stage.at[g], mixed_hbm.at[:, wide], sems.at[g])

    def body(g, z):
        wide = pl.ds(pl.multiple_of(g * width, width), width)
        c = jnp.zeros((1, width), F32)
        for k in range(levels, 0, -1):
            c = jnp.where(me >= 2 * k, past[k - 1][0:1, wide] * c + past[k - 1][1:2, wide], 0.0)
        c = jnp.where(me % 2 == 1, near_ref[0:1, wide] * c + near_ref[1:2, wide], c)
        for s in range(SEGS):
            at = slice(s * seg_len, (s + 1) * seg_len)
            stage[g, at, :] = (hg_ref[at, wide] + pg_ref[at, wide] * c).astype(BF16)
            c = ends_ref[0, s : s + 1, wide] * c + ends_ref[1, s : s + 1, wide]
        outgoing(g).start()
        kv_ref[...] += jnp.dot(stage[g], w_ref[wide, :], preferred_element_type=F32)
        return z

    def drain(g, z):
        outgoing(g).wait()
        return z

    lax.fori_loop(0, channels // width, body, 0)
    lax.fori_loop(0, channels // width, drain, 0)


def sum_kernel(a_ref, b_ref, own_ref, half_ref):
    both = a_ref[...] + b_ref[...]
    n = both.shape[0] // 2
    core = lax.axis_index("mp")
    for side in range(2):
        keys = both[side * n : (side + 1) * n, :HD].T.astype(BF16)
        values = both[side * n : (side + 1) * n, HD:].astype(BF16)
        own_ref[side, :HD, :] = keys
        own_ref[side, HD:, :] = values
    half_ref[...] = own_ref[core]


def attend_kernel(own, lags, final, heads, starts_ref, q_ref, *refs):
    refs = list(refs)
    take = lambda n: [refs.pop(0) for _ in range(n)]
    own_ref = take(1)[0] if own else None
    pairs = [take(2) for _ in lags]
    prev = None if own else take(3)
    out = take(1)[0] if final else None
    acc, m_ref, l_ref = (None, None, None) if final else take(3)
    low, score, top = take(3)
    if final:
        acc, m_ref, l_ref, stage, sems = take(5)
    prob, l_new, flag = (None, None, None) if own else take(3)
    rows = q_ref.shape[0]
    half = rows // 2
    me = lax.axis_index("tm")
    first = me * rows
    core = lax.axis_index("mp")
    turn = 2 * (me % 2) - 1
    scale = LOG2E / math.sqrt(HD)

    def lowest(t):
        d0 = jnp.maximum(t - (WINDOW - 1), 0)
        for d in range(DOCS):
            d0 = jnp.maximum(d0, jnp.where(starts_ref[d] <= t, starts_ref[d], 0))
        return d0

    lo_first = lowest(first)
    lo_last = lowest(first + rows - 1)
    tiles = [(None, first)] if own else []
    for k, (even_part, odd_part) in enumerate(lags):
        tiles.append((pairs[k], first - (even_part + odd_part * turn) * rows))
    live = [None if pair is None else (start >= 0) & (start < first) & (start + rows > lo_first) for pair, start in tiles]

    def keys_of(pair, t):
        return own_ref[t, :HD, :] if pair is None else pair[t][:HD, :]

    def values_of(pair, t):
        return own_ref[t, HD:, :] if pair is None else pair[t][HD:, :]

    def lanes(g, h, n):
        return pl.ds(pl.multiple_of((g * GROUP + h) * n, n), n)

    def kept(g, h, n):
        return slice(h * n, (h + 1) * n) if final else lanes(g, h, n)

    def score_pass(g, j, pair, start, masked):
        for h in range(GROUP):
            for t in range(2):
                r0 = half * t if pair is None else 0
                at = slice(r0, rows)
                s = jnp.dot(q_ref[at, lanes(g, h, HD)], keys_of(pair, t), preferred_element_type=F32)
                peak = top[h, at, :]
                for c in range(half // 128):
                    part = s[:, c * 128 : (c + 1) * 128] * scale
                    if masked:
                        side = t if pair is None else jnp.where(core == t, 0, 1)
                        kpos = lax.broadcasted_iota(jnp.int32, part.shape, 1) + (start + side * half + c * 128)
                        ok = kpos >= low[at, :]
                        if pair is None:
                            ok = ok & (kpos <= lax.broadcasted_iota(jnp.int32, part.shape, 0) + (first + r0))
                        part = jnp.where(ok, part, -1e30)
                    score[j, h, t, at, c * 128 : (c + 1) * 128] = part
                    peak = jnp.maximum(peak, part)
                top[h, at, :] = peak

    def value_pass(g, j, pair):
        for h in range(GROUP):
            spans = [(0, half, 1), (half, rows, 2)] if pair is None else [(0, rows, 2)]
            for r0, r1, n in spans:
                at = slice(r0, r1)
                m = m_ref[at, kept(g, h, 128)]
                total = l_ref[at, kept(g, h, 128)]
                ps, vs = [], []
                for t in range(n):
                    for c in range(half // 128):
                        p = jnp.exp2(score[j, h, t, at, c * 128 : (c + 1) * 128] - m)
                        total = total + p
                        ps.append(p.astype(BF16))
                    vs.append(values_of(pair, t))
                l_ref[at, kept(g, h, 128)] = total
                acc[at, kept(g, h, HD)] += jnp.dot(
                    jnp.concatenate(ps, 1), jnp.concatenate(vs, 0), preferred_element_type=F32
                )

    def spread(x):
        return jnp.concatenate([x] * (HD // 128), 1)

    def update(g):
        top[...] = jnp.full(top.shape, -1e30, F32)
        for j, (pair, start) in enumerate(tiles):
            if pair is None:
                score_pass(g, j, pair, start, True)
                continue

            @pl.when(live[j] & (start >= lo_last))
            def _(j=j, pair=pair, start=start):
                score_pass(g, j, pair, start, False)

            @pl.when(live[j] & (start < lo_last))
            def _(j=j, pair=pair, start=start):
                score_pass(g, j, pair, start, True)

        for h in range(GROUP):
            m = jnp.broadcast_to(jnp.max(top[h], axis=1, keepdims=True), (rows, 128))
            if own:
                l_ref[:, kept(g, h, 128)] = jnp.zeros((rows, 128), F32)
                acc[:, kept(g, h, HD)] = jnp.zeros((rows, HD), F32)
            else:
                m0 = prev[1][:, lanes(g, h, 128)]
                m = jnp.maximum(m, m0)
                fade = jnp.exp2(m0 - m)
                l_ref[:, kept(g, h, 128)] = prev[2][:, lanes(g, h, 128)] * fade
                acc[:, kept(g, h, HD)] = prev[0][:, lanes(g, h, HD)] * spread(fade)
            m_ref[:, kept(g, h, 128)] = m
        for j, (pair, start) in enumerate(tiles):
            if pair is None:
                value_pass(g, j, pair)
                continue

            @pl.when(live[j])
            def _(j=j, pair=pair):
                value_pass(g, j, pair)

    def loop(fn):
        def body(g, z):
            fn(g)
            return z

        lax.fori_loop(0, heads // GROUP, body, 0)

    def start_up():
        low[...] = lowest(first + lax.broadcasted_iota(jnp.int32, (rows, 128), 0))

    if own:
        start_up()
        loop(update)
        return

    def exp_pass(g, j, pair, start, masked):
        for h in range(GROUP):
            m = prev[1][:, lanes(g, h, 128)]
            total = l_new[:, lanes(g, h, 128)]
            for t in range(2):
                s = jnp.dot(q_ref[:, lanes(g, h, HD)], keys_of(pair, t), preferred_element_type=F32)
                for c in range(half // 128):
                    part = s[:, c * 128 : (c + 1) * 128] * scale
                    if masked:
                        side = jnp.where(core == t, 0, 1)
                        kpos = lax.broadcasted_iota(jnp.int32, part.shape, 1) + (start + side * half + c * 128)
                        part = jnp.where(kpos >= low[...], part, -1e30)
                    p = jnp.exp2(part - m)
                    total = total + p
                    prob[j, g * GROUP + h, (t * half) // 128 + c] = p.astype(BF16)
            l_new[:, lanes(g, h, 128)] = total

    def weighted(g, h, j, pair):
        values = jnp.concatenate([values_of(pair, t) for t in range(2)], 0)
        shares = jnp.concatenate([prob[j, g * GROUP + h, c] for c in range(rows // 128)], 1)
        return jnp.dot(shares, values, preferred_element_type=F32)

    def exp_all(g):
        for j, (pair, start) in enumerate(tiles):

            @pl.when(live[j] & (start >= lo_last))
            def _(j=j, pair=pair, start=start):
                exp_pass(g, j, pair, start, False)

            @pl.when(live[j] & (start < lo_last))
            def _(j=j, pair=pair, start=start):
                exp_pass(g, j, pair, start, True)

    any_live = functools.reduce(jnp.logical_or, live)

    @pl.when(any_live)
    def _():
        start_up()
        l_new[...] = prev[2][...]
        loop(exp_all)
        flag[0] = jnp.where(jnp.max(l_new[...]) <= 2.0**64, 1, 0)

    @pl.when(jnp.logical_not(any_live))
    def _():
        flag[0] = 2

    fast = flag[0] == 1
    slow = flag[0] == 0

    if not final:

        def add_all(g):
            for j, (pair, start) in enumerate(tiles):

                @pl.when(live[j])
                def _(j=j, pair=pair):
                    for h in range(GROUP):
                        acc[:, lanes(g, h, HD)] += weighted(g, h, j, pair)

        @pl.when(fast)
        def _():
            l_ref[...] = l_new[...]
            loop(add_all)

        @pl.when(slow)
        def _():
            loop(update)

        return

    def outgoing(g):
        wide = pl.ds(pl.multiple_of(g * GROUP * HD, GROUP * HD), GROUP * HD)
        return pltpu.make_async_copy(stage.at[g], out.at[:, wide], sems.at[g])

    def settle(g, h, top_sum, below):
        share = jnp.broadcast_to(1.0 / jnp.sum(below, axis=1, keepdims=True), (rows, 128))
        stage[g, :, h * HD : (h + 1) * HD] = (top_sum * spread(share)).astype(BF16)

    def finish(g):
        @pl.when(fast)
        def _():
            for h in range(GROUP):
                sums = prev[0][:, lanes(g, h, HD)] + weighted(g, h, 0, tiles[0][0])
                settle(g, h, sums, l_new[:, lanes(g, h, 128)])

        @pl.when(slow)
        def _():
            update(g)
            for h in range(GROUP):
                settle(g, h, acc[:, kept(g, h, HD)], l_ref[:, kept(g, h, 128)])

        @pl.when(jnp.logical_not(any_live))
        def _():
            for h in range(GROUP):
                settle(g, h, prev[0][:, lanes(g, h, HD)], prev[2][:, lanes(g, h, 128)])

        outgoing(g).start()

    loop(finish)
    loop(lambda g: outgoing(g).wait())


def recur_call(starts, x, halo, *params):
    rows, channels = x.shape
    _, width, _ = params[2].shape
    conv_weight, conv_bias, _, gate_scale, gate_bias, decay_rate = params
    vmem = pl.BlockSpec(memory_space=pltpu.VMEM)
    hbm = pl.BlockSpec(memory_space=pl.ANY)
    return pl.pallas_call(
        recur_kernel,
        in_specs=[pl.BlockSpec(memory_space=pltpu.SMEM), hbm, vmem] + [hbm] * 6,
        out_specs=[vmem] * 4,
        scratch_shapes=[
            pltpu.VMEM((rows + 2 * SEGS, 128), F32),
            pltpu.VMEM((width // 128, rows + HIST * (SEGS + 1), 128), F32),
            pltpu.VMEM((width // 128, rows, 128), BF16),
            pltpu.VMEM((rows, 2 * width), F32),
            pltpu.VMEM((2, rows, width), BF16),
            pltpu.VMEM((2, width, 2 * width), BF16),
        ]
        + [pltpu.VMEM(a.shape, F32) for a in (conv_weight, conv_bias, gate_scale, gate_bias, decay_rate)]
        + [pltpu.SMEM((rows // SEGS // CHUNK,), jnp.int32)]
        + [pltpu.SemaphoreType.DMA((2, 2)), pltpu.SemaphoreType.DMA((5,))],
        out_shape=[
            jax.ShapeDtypeStruct((channels // 128, rows, 128), F32),
            jax.ShapeDtypeStruct((channels // 128, rows, 128), F32),
            jax.ShapeDtypeStruct((2, SEGS, channels), F32),
            jax.ShapeDtypeStruct((2, channels), F32),
        ],
        compiler_params=pltpu.CompilerParams(vmem_limit_bytes=20 << 20),
        name="recur",
    )(starts, x, halo, *params)


def level_call(tot, near):
    return pl.pallas_call(
        level_kernel,
        out_shape=jax.ShapeDtypeStruct(tot.shape, F32),
        compiler_params=pltpu.CompilerParams(vmem_limit_bytes=1 << 20),
        name="level",
    )(tot, near)


def ready_call(h, p, y, kv_panel, kv_scale):
    rows, channels = y.shape
    vmem = pl.BlockSpec(memory_space=pltpu.VMEM)
    flat = jax.ShapeDtypeStruct((rows, channels), F32)
    return pl.pallas_call(
        ready_kernel,
        in_specs=[vmem] * 5,
        out_specs=[vmem] * 3,
        out_shape=[flat, flat, jax.ShapeDtypeStruct(kv_panel.shape, BF16)],
        cost_estimate=pl.CostEstimate(flops=1 << 24, bytes_accessed=1 << 22, transcendentals=rows * channels),
        compiler_params=pltpu.CompilerParams(vmem_limit_bytes=4 << 20),
        name="ready",
    )(h, p, y, kv_panel, kv_scale)


def mix_call(hg, pg, weight, ends, near, past):
    rows, channels = hg.shape
    out = weight.shape[1]
    width = MIX_GROUPS * SCALE_ROWS
    vmem = pl.BlockSpec(memory_space=pltpu.VMEM)
    return pl.pallas_call(
        functools.partial(mix_kernel, len(past)),
        in_specs=[vmem] * (5 + len(past)),
        out_specs=[pl.BlockSpec(memory_space=pl.ANY), vmem],
        out_shape=[jax.ShapeDtypeStruct((rows, channels), BF16), jax.ShapeDtypeStruct((rows, out), F32)],
        scratch_shapes=[
            pltpu.VMEM((channels // width, rows, width), BF16),
            pltpu.SemaphoreType.DMA((channels // width,)),
        ],
        compiler_params=pltpu.CompilerParams(vmem_limit_bytes=8 << 20),
        name="mix",
    )(hg, pg, weight, ends, near, *past)


def sum_call(a, b):
    rows, _ = a.shape
    half = rows // 2
    return pl.pallas_call(
        sum_kernel,
        out_shape=[
            jax.ShapeDtypeStruct((2, 2 * HD, half), BF16),
            jax.ShapeDtypeStruct((2 * HD, half), BF16),
        ],
        compiler_params=pltpu.CompilerParams(vmem_limit_bytes=16 << 20),
        name="kvsum",
    )(a, b)


def attend_call(starts, q, own, halves, lags, prev, final):
    rows, width = q.shape
    heads = width // HD
    held = [] if own is None else [own]
    held += halves
    held += prev or []
    tiles = len(lags) + (own is not None)
    vmem = pl.BlockSpec(memory_space=pltpu.VMEM)
    scratch = [
        pltpu.VMEM((rows, 128), jnp.int32),
        pltpu.VMEM((tiles, GROUP, 2, rows, rows // 2), F32),
        pltpu.VMEM((GROUP, rows, 128), F32),
    ]
    aliases = {}
    if final:
        out_specs = pl.BlockSpec(memory_space=pl.ANY)
        out_shape = jax.ShapeDtypeStruct((rows, width), BF16)
        scratch += [pltpu.VMEM((rows, GROUP * n), F32) for n in (HD, 128, 128)]
        scratch += [pltpu.VMEM((heads // GROUP, rows, GROUP * HD), BF16), pltpu.SemaphoreType.DMA((heads // GROUP,))]
    if own is None:
        scratch += [
            pltpu.VMEM((tiles, heads, rows // 128, rows, 128), BF16),
            pltpu.VMEM((rows, heads * 128), F32),
            pltpu.SMEM((1,), jnp.int32),
        ]
    if not final:
        out_specs = [vmem] * 3
        out_shape = [jax.ShapeDtypeStruct((rows, heads * n), F32) for n in (HD, 128, 128)]
        if prev:
            aliases = {2 + len(halves) + k: k for k in range(3)}
    return pl.pallas_call(
        functools.partial(attend_kernel, own is not None, lags, final, heads),
        in_specs=[pl.BlockSpec(memory_space=pltpu.SMEM), vmem] + [vmem] * len(held),
        out_specs=out_specs,
        scratch_shapes=scratch,
        out_shape=out_shape,
        input_output_aliases=aliases,
        cost_estimate=pl.CostEstimate(
            flops=4 * tiles * rows * rows * width,
            bytes_accessed=4 * rows * width,
            transcendentals=tiles * rows * rows * heads,
        ),
        compiler_params=pltpu.CompilerParams(vmem_limit_bytes=32 << 20),
        name="attend_own" if own is not None else "attend_end" if final else "attend_mid",
    )(starts, q, *held)


def local(
    branch_x,
    branch_y,
    queries,
    conv_weight,
    conv_bias,
    gate_panel,
    gate_scale,
    gate_bias,
    decay_rate,
    kv_panel,
    kv_scale,
    segment_ids,
):
    rows = branch_x.shape[0]
    seq = segment_ids.shape[0]
    halo = ring(branch_x[rows - CONV + 1 :], 1)
    starts = jnp.sum(
        (segment_ids[None, :] < jnp.arange(DOCS, dtype=jnp.int32)[:, None]).astype(jnp.int32), axis=1
    )
    stay = lambda a: pltpu.with_memory_space_constraint(a, pltpu.HBM)
    h, p, ends, tot = recur_call(
        starts,
        stay(branch_x),
        halo,
        stay(conv_weight),
        stay(conv_bias[None]),
        stay(gate_panel),
        stay(gate_scale),
        stay(gate_bias),
        stay(decay_rate[None]),
    )
    near = swap(tot)
    hg, pg, weight = ready_call(h, p, branch_y, kv_panel, kv_scale)
    level = level_call(tot, near)
    levels = -(-(seq // 2) // (2 * rows))
    past = [ring(level, 2 * k) for k in range(1, levels + 1)]
    mixed, partial_kv = mix_call(hg, pg, weight, ends, near, past)
    own, half = sum_call(partial_kv, partner(partial_kv))

    levels = -(-WINDOW // rows) // 2
    straight, attended, held, held_lags = half, None, [], []
    for k in range(levels + 1):
        last = k == levels
        beyond = None if last else ring(straight, 2)
        crossed = swap(straight)
        if k == 0:
            attended = attend_call(starts, queries, own, [], [], None, False)
        else:
            attended = attend_call(starts, queries, None, tiles, lags, attended, False)
        near_tiles, near_lags = [crossed, partner(crossed)], [(2 * k, 1)]
        if last:
            tiles, lags = near_tiles, near_lags
        else:
            tiles, lags = [beyond, partner(beyond)], [(2 * k + 2, 0)]
            held, held_lags = held + near_tiles, held_lags + near_lags
            if k > 0:
                tiles, lags, held, held_lags = tiles + held, lags + held_lags, [], []
        straight = beyond
    attended = attend_call(starts, queries, None, tiles, lags, attended, True)
    return mixed, attended


def solution(mesh):
    in_specs = (
        P(("groups", "tm"), "mp"),
        P(("groups", "tm"), "mp"),
        P(("groups", "tm"), "mp"),
        P(None, "mp"),
        P("mp"),
        P("mp", None, None),
        P("mp", None, None),
        P(None, "mp"),
        P("mp"),
        P("mp", None),
        P("mp", None),
        P("groups"),
    )
    out_specs = (P(("groups", "tm"), "mp"), P(("groups", "tm"), "mp"))
    return jax.shard_map(local, mesh=mesh, in_specs=in_specs, out_specs=out_specs, check_vma=False)
```
